256 devices in a mesh: ctx: 32 (over x, y, z_lo), tp: 8 (over z_hi, core).
Axes of the slice: x: 4, y: 4, z: 8 (z_hi: 4, z_lo: 2; z = z_hi * 2 + z_lo), core: 2. Of those that a mesh axis runs over, the one named last changes fastest.
Arguments:
- query_rows: bfloat16 [4096, 8192], P('ctx', 'tp'), may hold values from -24 to 24
- key_rows: bfloat16 [4096, 1024], P('ctx', 'tp'), may hold values from -24 to 24
- value_rows: bfloat16 [4096, 1024], P('ctx', 'tp'), may hold values from -6 to 6
- out_grad: bfloat16 [4096, 8192], P(('ctx', 'tp')), may hold values from -6 to 6
- segment_ids: int32 [4096], replicated, may hold values from 0 to 2, as said below
- span_order: int32 [64], replicated, may hold values from 0 to 63, as said below
Outputs:
- attn_out: bfloat16 [4096, 8192], P(('ctx', 'tp'))
- query_grad: bfloat16 [4096, 8192], P('ctx', 'tp')
- key_grad: bfloat16 [4096, 1024], P('ctx', 'tp')
- value_grad: bfloat16 [4096, 1024], P('ctx', 'tp')
The draws below stay inside these ranges and needn't reach their ends.
Inputs may be any that keep to these rules, and one draw needn't show every extreme that they name: `segment_ids`: never falling: a nonempty prompt labelled 0 from position 0, then a nonempty chosen response labelled 1, then a nonempty rejected response labelled 2. `span_order`: each block number once; entries 2 j and 2 j + 1 sum to 63.
All inputs are finite; a program needn't handle non-finite values.
Results may differ from the reference program's by a relative error of at most 0.033.
Values may be sent and summed in bfloat16 or wider, within the bound.
A program may use at most 64 MiB of HBM per device.

```python
import math
import jax
import jax.numpy as jnp
from jax import lax

HEADS = 64
KV_HEADS = 8
HEAD_DIM = 128
SPAN = 64
SEQ = 4096
NCHUNKS = 64


def draw_pair(key):
    base = jax.random.fold_in(key, 11)
    key_noise = jax.random.normal(jax.random.fold_in(base, 1), (SEQ, KV_HEADS * HEAD_DIM), jnp.float32)
    query_noise = jax.random.normal(jax.random.fold_in(base, 2), (SEQ, HEADS * HEAD_DIM), jnp.float32)
    keys_out = jnp.clip(key_noise, -6.0, 6.0)
    queries_out = jnp.clip(query_noise, -6.0, 6.0)
    return (queries_out, keys_out)


def draw_query_rows(key, part):
    return draw_pair(key)[0].astype(jnp.bfloat16)


def draw_key_rows(key, part):
    return draw_pair(key)[1].astype(jnp.bfloat16)


def draw_segment_ids(key, part):
    prompt = jax.random.randint(jax.random.fold_in(key, 21), (), SEQ // 8, 3 * SEQ // 8)
    chosen = jax.random.randint(jax.random.fold_in(key, 22), (), SEQ // 4, SEQ // 2)
    spots = jnp.arange(SEQ, dtype=jnp.int32)
    return (spots >= prompt).astype(jnp.int32) + (spots >= prompt + chosen).astype(jnp.int32)


def draw_span_order(key, part):
    half = NCHUNKS // 2
    picked = jax.random.permutation(jax.random.fold_in(key, 31), half).astype(jnp.int32)
    return jnp.stack([picked, NCHUNKS - 1 - picked], axis=1).reshape(NCHUNKS)


def shard_levels(key, extent, split, least, largest):
    gain, own = 1.0, jax.random.fold_in(key, 6)
    for axis_at, shards_of in split:
        heights = jnp.exp(jax.random.uniform(jax.random.fold_in(own, axis_at), (shards_of,), jnp.float32, least / len(split), largest / len(split)))
        gain = gain * jnp.repeat(heights, extent[axis_at] // shards_of).reshape([-1 if axis == axis_at else 1 for axis in range(len(extent))])
    return gain


def bell_draw(stream_key, shape, scale, bound, pieces=(), kind=jnp.bfloat16):
    result = scale * jax.random.normal(stream_key, shape, jnp.float32)
    if pieces:
        result = result * shard_levels(stream_key, shape, pieces, -0.22, 0.18)
    return jnp.clip(result, -bound, bound).astype(kind)


def setup_inputs(seed: int = 0) -> dict:
    splits = jax.random.split(jax.random.key(seed), 7)
    query_rows = draw_query_rows(jax.random.fold_in(splits[6], 71), 0)
    key_rows = draw_key_rows(jax.random.fold_in(splits[6], 71), 0)
    value_rows = bell_draw(splits[2], (SEQ, KV_HEADS * HEAD_DIM), 1.0, 6.0, ((0, 32), (1, 8)))
    out_grad = bell_draw(splits[3], (SEQ, HEADS * HEAD_DIM), 1.0, 6.0, ((0, 256),))
    segment_ids = draw_segment_ids(jax.random.fold_in(splits[6], 71), 0)
    span_order = draw_span_order(jax.random.fold_in(splits[6], 71), 0)
    return dict(query_rows=query_rows, key_rows=key_rows, value_rows=value_rows, out_grad=out_grad, segment_ids=segment_ids, span_order=span_order)


def reference(query_rows, key_rows, value_rows, out_grad, segment_ids, span_order):
    seq = query_rows.shape[0]
    ratio = HEADS // KV_HEADS
    scale = 1.0 / math.sqrt(HEAD_DIM)
    all_rows = jnp.arange(seq, dtype=jnp.int32)
    positions = (SPAN * span_order[all_rows // SPAN] + all_rows % SPAN).astype(jnp.int32)
    labels = segment_ids[positions]
    block = math.gcd(seq, 512)
    blocks = seq // block
    queries4 = query_rows.reshape(seq, KV_HEADS, ratio, HEAD_DIM).astype(jnp.float32)
    keys3 = key_rows.reshape(seq, KV_HEADS, HEAD_DIM).astype(jnp.float32)
    values3 = value_rows.reshape(seq, KV_HEADS, HEAD_DIM).astype(jnp.float32)
    grads4 = out_grad.reshape(seq, KV_HEADS, ratio, HEAD_DIM).astype(jnp.float32)

    def one_group(group):
        query_group = jnp.take(queries4, group, axis=1)
        key_group = jnp.take(keys3, group, axis=1)
        value_group = jnp.take(values3, group, axis=1)
        grad_group = jnp.take(grads4, group, axis=1)

        def step(carry, index):
            key_acc, value_acc = carry
            start = (index * block).astype(jnp.int32)
            query_block = lax.dynamic_slice_in_dim(query_group, start, block, 0)
            grad_block = lax.dynamic_slice_in_dim(grad_group, start, block, 0)
            pos_block = lax.dynamic_slice_in_dim(positions, start, block, 0)
            label_block = lax.dynamic_slice_in_dim(labels, start, block, 0)
            visible = (positions[None, :] <= pos_block[:, None]) & ((labels[None, :] == 0) | (labels[None, :] == label_block[:, None]))
            scores = jnp.einsum('rjd,cd->jrc', query_block, key_group) * scale
            scores = jnp.where(visible[None], scores, -jnp.inf)
            row_max = lax.optimization_barrier(jnp.max(scores, axis=-1, keepdims=True))
            weights = jnp.where(visible[None], jnp.exp(scores - row_max), 0.0)
            total = lax.optimization_barrier(jnp.sum(weights, axis=-1, keepdims=True))
            weights_b = weights.astype(jnp.bfloat16).astype(jnp.float32)
            summed = jnp.einsum('jrc,cd->rjd', weights_b, value_group)
            attn_block = (summed / jnp.transpose(total, (1, 0, 2))).astype(jnp.bfloat16)
            delta = lax.optimization_barrier(jnp.sum(grad_block * attn_block.astype(jnp.float32), axis=-1))
            delta = jnp.transpose(delta)[:, :, None]
            probs = weights / total
            probs_b = probs.astype(jnp.bfloat16).astype(jnp.float32)
            dprob = jnp.einsum('rjd,cd->jrc', grad_block, value_group)
            dscore = probs * (dprob - delta)
            dscore_b = dscore.astype(jnp.bfloat16).astype(jnp.float32)
            query_block_grad = (jnp.einsum('jrc,cd->rjd', dscore_b, key_group) * scale).astype(jnp.bfloat16)
            key_acc = key_acc + jnp.einsum('jrc,rjd->cd', dscore_b, query_block)
            value_acc = value_acc + jnp.einsum('jrc,rjd->cd', probs_b, grad_block)
            return ((key_acc, value_acc), (attn_block, query_block_grad))
        zeros = jnp.zeros((seq, HEAD_DIM), jnp.float32)
        (key_acc, value_acc), (attn_blocks, query_blocks) = lax.scan(step, (zeros, zeros), jnp.arange(blocks, dtype=jnp.int32))
        attn_group = attn_blocks.reshape(seq, ratio, HEAD_DIM)
        query_group_grad = query_blocks.reshape(seq, ratio, HEAD_DIM)
        return (attn_group, query_group_grad, (key_acc * scale).astype(jnp.bfloat16), value_acc.astype(jnp.bfloat16))
    attn_all, query_all, key_all, value_all = lax.map(one_group, jnp.arange(KV_HEADS, dtype=jnp.int32))
    attn_out = jnp.transpose(attn_all, (1, 0, 2, 3)).reshape(seq, HEADS * HEAD_DIM)
    query_grad = jnp.transpose(query_all, (1, 0, 2, 3)).reshape(seq, HEADS * HEAD_DIM)
    key_grad = jnp.transpose(key_all, (1, 0, 2)).reshape(seq, KV_HEADS * HEAD_DIM)
    value_grad = jnp.transpose(value_all, (1, 0, 2)).reshape(seq, KV_HEADS * HEAD_DIM)
    return (attn_out, query_grad, key_grad, value_grad)
```

```python
import functools
import math

import jax
import jax.numpy as jnp
from jax import lax
from jax.experimental import pallas as pl
from jax.experimental.pallas import tpu as pltpu
from jax.sharding import PartitionSpec as P

HEAD_DIM = 128
SPAN = 64
MESH = pl.DeviceIdType.MESH


def greet_all(n, me):
    barrier = pltpu.get_barrier_semaphore()

    def greet(i, c):
        peer = lax.rem(me + i, n)
        pl.semaphore_signal(barrier, inc=1, device_id={"ctx": peer}, device_id_type=MESH)
        return c

    lax.fori_loop(1, n, greet, 0)
    pl.semaphore_wait(barrier, n - 1)


def gather_kernel(n, src_ref, out_ref, send_sem, recv_sem):
    me = lax.axis_index("ctx")
    greet_all(n, me)

    def copy_to(peer):
        return pltpu.make_async_remote_copy(
            src_ref, out_ref.at[me], send_sem.at[peer], recv_sem.at[me],
            device_id={"ctx": peer}, device_id_type=MESH)

    def copy_from(src):
        return pltpu.make_async_remote_copy(
            src_ref, out_ref.at[src], send_sem.at[src], recv_sem.at[src],
            device_id={"ctx": src}, device_id_type=MESH)

    def send(i, c):
        copy_to(lax.rem(me + i, n)).start()
        return c

    lax.fori_loop(1, n, send, 0)
    out_ref[me] = src_ref[...]

    def wait(i, c):
        copy_to(lax.rem(me + i, n)).wait_send()
        copy_from(lax.rem(me + n - i, n)).wait_recv()
        return c

    lax.fori_loop(1, n, wait, 0)


def ctx_gather(block, n):
    rows, width = block.shape
    return pl.pallas_call(
        functools.partial(gather_kernel, n),
        out_shape=jax.ShapeDtypeStruct((n, rows, width), block.dtype),
        in_specs=[pl.BlockSpec(memory_space=pltpu.VMEM)],
        out_specs=pl.BlockSpec(memory_space=pltpu.VMEM),
        scratch_shapes=[pltpu.SemaphoreType.DMA((n,)), pltpu.SemaphoreType.DMA((n,))],
        compiler_params=pltpu.CompilerParams(collective_id=0, has_side_effects=True),
    )(block)


def scatter_kernel(n, terms_ref, out_ref, held, send_sem, recv_sem):
    me = lax.axis_index("ctx")
    greet_all(n, me)

    def copy_to(peer):
        return pltpu.make_async_remote_copy(
            terms_ref.at[peer], held.at[me], send_sem.at[peer], recv_sem.at[me],
            device_id={"ctx": peer}, device_id_type=MESH)

    def copy_from(src):
        return pltpu.make_async_remote_copy(
            terms_ref.at[src], held.at[src], send_sem.at[src], recv_sem.at[src],
            device_id={"ctx": src}, device_id_type=MESH)

    def send(i, c):
        copy_to(lax.rem(me + i, n)).start()
        return c

    lax.fori_loop(1, n, send, 0)
    out_ref[...] = terms_ref[me].astype(jnp.float32)

    def wait(i, c):
        copy_to(lax.rem(me + i, n)).wait_send()
        src = lax.rem(me + n - i, n)
        copy_from(src).wait_recv()
        out_ref[...] += held[src].astype(jnp.float32)
        return c

    lax.fori_loop(1, n, wait, 0)


def ctx_reduce_scatter(terms, n):
    _, rows, width = terms.shape
    return pl.pallas_call(
        functools.partial(scatter_kernel, n),
        out_shape=jax.ShapeDtypeStruct((rows, width), jnp.float32),
        in_specs=[pl.BlockSpec(memory_space=pltpu.VMEM)],
        out_specs=pl.BlockSpec(memory_space=pltpu.VMEM),
        scratch_shapes=[
            pltpu.VMEM(terms.shape, terms.dtype),
            pltpu.SemaphoreType.DMA((n,)),
            pltpu.SemaphoreType.DMA((n,)),
        ],
        compiler_params=pltpu.CompilerParams(collective_id=1, has_side_effects=True),
    )(terms)


def fetch_grad(out_grad):
    return lax.all_to_all(out_grad, "tp", split_axis=1, concat_axis=0, tiled=True)


def spread_output(attn_flat):
    return lax.all_to_all(attn_flat, "tp", split_axis=0, concat_axis=1, tiled=True)


def on_device(query_rows, key_rows, value_rows, out_grad, segment_ids, span_order):
    ctx_size = lax.axis_size("ctx")
    ctx_index = lax.axis_index("ctx")
    local_rows = query_rows.shape[0]
    heads_here = query_rows.shape[1] // HEAD_DIM
    groups_here = key_rows.shape[1] // HEAD_DIM
    ratio = heads_here // groups_here
    total_rows = local_rows * ctx_size
    width = groups_here * HEAD_DIM
    scale = 1.0 / math.sqrt(HEAD_DIM)
    offsets = jnp.arange(SPAN, dtype=jnp.int32)
    positions = (SPAN * span_order[:, None] + offsets[None, :]).reshape(total_rows)
    prompt_end = jnp.sum((segment_ids == 0).astype(jnp.int32))
    chosen_end = jnp.sum((segment_ids <= 1).astype(jnp.int32))
    labels = (positions >= prompt_end).astype(jnp.int32) + (positions >= chosen_end).astype(jnp.int32)
    own_start = ctx_index * local_rows
    own_pos = lax.dynamic_slice_in_dim(positions, own_start, local_rows, 0)
    own_label = lax.dynamic_slice_in_dim(labels, own_start, local_rows, 0)
    block = math.gcd(total_rows, 512)
    blocks = total_rows // block
    queries4 = query_rows.reshape(local_rows, groups_here, ratio, HEAD_DIM)
    grad_rows = None
    kv_all = ctx_gather(jnp.concatenate([key_rows, value_rows], axis=1), ctx_size)
    keys_all = kv_all[:, :, :width].reshape(total_rows, width)
    values_all = kv_all[:, :, width:].reshape(total_rows, width)
    keys_all = keys_all.reshape(total_rows, groups_here, HEAD_DIM)
    values_all = values_all.reshape(total_rows, groups_here, HEAD_DIM)

    def block_inputs(start, size):
        key_block = lax.dynamic_slice_in_dim(keys_all, start, size, 0)
        value_block = lax.dynamic_slice_in_dim(values_all, start, size, 0)
        pos_block = lax.dynamic_slice_in_dim(positions, start, size, 0)
        label_block = lax.dynamic_slice_in_dim(labels, start, size, 0)
        visible = (pos_block[None, :] <= own_pos[:, None]) & (
            (label_block[None, :] == 0) | (label_block[None, :] == own_label[:, None])
        )
        scores = (
            jnp.einsum("rgjd,cgd->gjrc", queries4, key_block, preferred_element_type=jnp.float32)
            * scale
        )
        scores = jnp.where(visible[None, None], scores, -jnp.inf)
        return (scores, visible, key_block, value_block)

    def sum_step(index, carry):
        running, total, summed = carry
        scores, visible, key_block, value_block = block_inputs(
            (index * block).astype(jnp.int32), block
        )
        new_max = jnp.maximum(running, jnp.max(scores, axis=-1, keepdims=True))
        shift = jnp.where(new_max == -jnp.inf, 0.0, new_max)
        factor = jnp.exp(running - shift)
        weights = jnp.where(visible[None, None], jnp.exp(scores - shift), 0.0)
        total = total * factor + jnp.sum(weights, axis=-1, keepdims=True)
        summed = summed * jnp.transpose(factor, (2, 0, 1, 3)) + jnp.einsum(
            "gjrc,cgd->rgjd",
            weights.astype(jnp.bfloat16),
            value_block,
            preferred_element_type=jnp.float32,
        )
        return (new_max, total, summed)

    start_max = jnp.full((groups_here, ratio, local_rows, 1), -jnp.inf, jnp.float32)
    start_total = jnp.zeros((groups_here, ratio, local_rows, 1), jnp.float32)
    start_summed = jnp.zeros((local_rows, groups_here, ratio, HEAD_DIM), jnp.float32)
    row_max, total, summed = lax.fori_loop(
        0, blocks, sum_step, (start_max, start_total, start_summed)
    )
    attn_local = (summed / jnp.transpose(total, (2, 0, 1, 3))).astype(jnp.bfloat16)
    attn_flat = attn_local.reshape(local_rows, heads_here * HEAD_DIM)
    attn_spread = None
    grad_rows = fetch_grad(out_grad)
    grads4 = grad_rows.reshape(local_rows, groups_here, ratio, HEAD_DIM)
    delta = jnp.sum(grads4.astype(jnp.float32) * attn_local.astype(jnp.float32), axis=-1)
    delta = jnp.transpose(delta, (1, 2, 0))[..., None]

    def score_grads(start, size):
        scores, visible, key_block, value_block = block_inputs(start, size)
        weights = jnp.where(visible[None, None], jnp.exp(scores - row_max), 0.0)
        probs = weights / total
        probs_b = probs.astype(jnp.bfloat16)
        dprob = jnp.einsum(
            "rgjd,cgd->gjrc", grads4, value_block, preferred_element_type=jnp.float32
        )
        dscore_b = (probs * (dprob - delta)).astype(jnp.bfloat16)
        return (probs_b, dscore_b, key_block)

    def kv_terms(probs_b, dscore_b, size):
        key_term = (
            jnp.einsum("gjrc,rgjd->cgd", dscore_b, queries4, preferred_element_type=jnp.float32)
            * scale
        )
        value_term = jnp.einsum(
            "gjrc,rgjd->cgd", probs_b, grads4, preferred_element_type=jnp.float32
        )
        return jnp.concatenate(
            [key_term.reshape(size, width), value_term.reshape(size, width)], axis=1
        )

    start_query = jnp.zeros((local_rows, groups_here, ratio, HEAD_DIM), jnp.float32)

    def grad_step(query_acc, index):
        probs_b, dscore_b, key_block = score_grads(index * block, block)
        query_acc = query_acc + jnp.einsum(
            "gjrc,cgd->rgjd", dscore_b, key_block, preferred_element_type=jnp.float32
        )
        return (query_acc, kv_terms(probs_b, dscore_b, block))

    query_acc, term_blocks = lax.scan(grad_step, start_query, jnp.arange(blocks, dtype=jnp.int32))
    terms = term_blocks.reshape(ctx_size, local_rows, 2 * width)
    reduced = ctx_reduce_scatter(terms, ctx_size)
    key_grad = reduced[:, :width].astype(jnp.bfloat16)
    value_grad = reduced[:, width:].astype(jnp.bfloat16)
    query_grad = (query_acc * scale).astype(jnp.bfloat16).reshape(local_rows, heads_here * HEAD_DIM)
    attn_spread = spread_output(attn_flat)
    return (attn_spread, query_grad, key_grad, value_grad)


def solution(mesh):
    placed = (P("ctx", "tp"), P("ctx", "tp"), P("ctx", "tp"), P(("ctx", "tp"), None), P(), P())
    return jax.shard_map(
        on_device,
        mesh=mesh,
        in_specs=placed,
        out_specs=(P(("ctx", "tp"), None), P("ctx", "tp"), P("ctx", "tp"), P("ctx", "tp")),
        check_vma=False,
    )
```

```python
import functools
import math

import jax
import jax.numpy as jnp
from jax import lax
from jax.experimental import pallas as pl
from jax.experimental.pallas import tpu as pltpu
from jax.sharding import PartitionSpec as P

HEAD_DIM = 128
SPAN = 64
MESH = pl.DeviceIdType.MESH


def greet_all(n, me):
    barrier = pltpu.get_barrier_semaphore()

    def greet(i, c):
        peer = lax.rem(me + i, n)
        pl.semaphore_signal(barrier, inc=1, device_id={"ctx": peer}, device_id_type=MESH)
        return c

    lax.fori_loop(1, n, greet, 0)
    pl.semaphore_wait(barrier, n - 1)


def gather_kernel(n, src_ref, out_ref, send_sem, recv_sem):
    me = lax.axis_index("ctx")
    greet_all(n, me)

    def copy_to(peer):
        return pltpu.make_async_remote_copy(
            src_ref, out_ref.at[me], send_sem.at[peer], recv_sem.at[me],
            device_id={"ctx": peer}, device_id_type=MESH)

    def copy_from(src):
        return pltpu.make_async_remote_copy(
            src_ref, out_ref.at[src], send_sem.at[src], recv_sem.at[src],
            device_id={"ctx": src}, device_id_type=MESH)

    def send(i, c):
        copy_to(lax.rem(me + i, n)).start()
        return c

    lax.fori_loop(1, n, send, 0)
    out_ref[me] = src_ref[...]

    def wait(i, c):
        copy_to(lax.rem(me + i, n)).wait_send()
        copy_from(lax.rem(me + n - i, n)).wait_recv()
        return c

    lax.fori_loop(1, n, wait, 0)


def ctx_gather(block, n):
    rows, width = block.shape
    return pl.pallas_call(
        functools.partial(gather_kernel, n),
        out_shape=jax.ShapeDtypeStruct((n, rows, width), block.dtype),
        in_specs=[pl.BlockSpec(memory_space=pltpu.VMEM)],
        out_specs=pl.BlockSpec(memory_space=pltpu.VMEM),
        scratch_shapes=[pltpu.SemaphoreType.DMA((n,)), pltpu.SemaphoreType.DMA((n,))],
        compiler_params=pltpu.CompilerParams(collective_id=0, has_side_effects=True),
    )(block)


def scatter_kernel(n, terms_ref, out_ref, held, send_sem, recv_sem):
    me = lax.axis_index("ctx")
    greet_all(n, me)

    def copy_to(peer):
        return pltpu.make_async_remote_copy(
            terms_ref.at[peer], held.at[me], send_sem.at[peer], recv_sem.at[me],
            device_id={"ctx": peer}, device_id_type=MESH)

    def copy_from(src):
        return pltpu.make_async_remote_copy(
            terms_ref.at[src], held.at[src], send_sem.at[src], recv_sem.at[src],
            device_id={"ctx": src}, device_id_type=MESH)

    def send(i, c):
        copy_to(lax.rem(me + i, n)).start()
        return c

    lax.fori_loop(1, n, send, 0)
    out_ref[...] = terms_ref[me].astype(jnp.float32)

    def wait(i, c):
        copy_to(lax.rem(me + i, n)).wait_send()
        src = lax.rem(me + n - i, n)
        copy_from(src).wait_recv()
        out_ref[...] += held[src].astype(jnp.float32)
        return c

    lax.fori_loop(1, n, wait, 0)


def ctx_reduce_scatter(terms, n):
    _, rows, width = terms.shape
    return pl.pallas_call(
        functools.partial(scatter_kernel, n),
        out_shape=jax.ShapeDtypeStruct((rows, width), jnp.float32),
        in_specs=[pl.BlockSpec(memory_space=pltpu.VMEM)],
        out_specs=pl.BlockSpec(memory_space=pltpu.VMEM),
        scratch_shapes=[
            pltpu.VMEM(terms.shape, terms.dtype),
            pltpu.SemaphoreType.DMA((n,)),
            pltpu.SemaphoreType.DMA((n,)),
        ],
        compiler_params=pltpu.CompilerParams(collective_id=1, has_side_effects=True),
    )(terms)


def fetch_grad(out_grad):
    return lax.all_to_all(out_grad, "tp", split_axis=1, concat_axis=0, tiled=True)


def spread_output(attn_flat):
    return lax.all_to_all(attn_flat, "tp", split_axis=0, concat_axis=1, tiled=True)


def on_device(query_rows, key_rows, value_rows, out_grad, segment_ids, span_order):
    ctx_size = lax.axis_size("ctx")
    ctx_index = lax.axis_index("ctx")
    local_rows = query_rows.shape[0]
    heads_here = query_rows.shape[1] // HEAD_DIM
    groups_here = key_rows.shape[1] // HEAD_DIM
    ratio = heads_here // groups_here
    total_rows = local_rows * ctx_size
    width = groups_here * HEAD_DIM
    scale = 1.0 / math.sqrt(HEAD_DIM)
    offsets = jnp.arange(SPAN, dtype=jnp.int32)
    positions = (SPAN * span_order[:, None] + offsets[None, :]).reshape(total_rows)
    prompt_end = jnp.sum((segment_ids == 0).astype(jnp.int32))
    chosen_end = jnp.sum((segment_ids <= 1).astype(jnp.int32))
    labels = (positions >= prompt_end).astype(jnp.int32) + (positions >= chosen_end).astype(jnp.int32)
    own_start = ctx_index * local_rows
    own_pos = lax.dynamic_slice_in_dim(positions, own_start, local_rows, 0)
    own_label = lax.dynamic_slice_in_dim(labels, own_start, local_rows, 0)
    block = math.gcd(total_rows, 512)
    blocks = total_rows // block
    queries4 = query_rows.reshape(local_rows, groups_here, ratio, HEAD_DIM)
    grad_rows = None
    kv_all = ctx_gather(jnp.concatenate([key_rows, value_rows], axis=1), ctx_size)
    keys_all = kv_all[:, :, :width].reshape(total_rows, width)
    values_all = kv_all[:, :, width:].reshape(total_rows, width)
    keys_all = keys_all.reshape(total_rows, groups_here, HEAD_DIM)
    values_all = values_all.reshape(total_rows, groups_here, HEAD_DIM)

    def block_inputs(start, size):
        key_block = lax.dynamic_slice_in_dim(keys_all, start, size, 0)
        value_block = lax.dynamic_slice_in_dim(values_all, start, size, 0)
        pos_block = lax.dynamic_slice_in_dim(positions, start, size, 0)
        label_block = lax.dynamic_slice_in_dim(labels, start, size, 0)
        visible = (pos_block[None, :] <= own_pos[:, None]) & (
            (label_block[None, :] == 0) | (label_block[None, :] == own_label[:, None])
        )
        scores = (
            jnp.einsum("rgjd,cgd->gjrc", queries4, key_block, preferred_element_type=jnp.float32)
            * scale
        )
        scores = jnp.where(visible[None, None], scores, -jnp.inf)
        return (scores, visible, key_block, value_block)

    def sum_step(index, carry):
        running, total, summed = carry
        scores, visible, key_block, value_block = block_inputs(
            (index * block).astype(jnp.int32), block
        )
        new_max = jnp.maximum(running, jnp.max(scores, axis=-1, keepdims=True))
        shift = jnp.where(new_max == -jnp.inf, 0.0, new_max)
        factor = jnp.exp(running - shift)
        weights = jnp.where(visible[None, None], jnp.exp(scores - shift), 0.0)
        total = total * factor + jnp.sum(weights, axis=-1, keepdims=True)
        summed = summed * jnp.transpose(factor, (2, 0, 1, 3)) + jnp.einsum(
            "gjrc,cgd->rgjd",
            weights.astype(jnp.bfloat16),
            value_block,
            preferred_element_type=jnp.float32,
        )
        return (new_max, total, summed)

    start_max = jnp.full((groups_here, ratio, local_rows, 1), -jnp.inf, jnp.float32)
    start_total = jnp.zeros((groups_here, ratio, local_rows, 1), jnp.float32)
    start_summed = jnp.zeros((local_rows, groups_here, ratio, HEAD_DIM), jnp.float32)
    row_max, total, summed = lax.fori_loop(
        0, blocks, sum_step, (start_max, start_total, start_summed)
    )
    attn_local = (summed / jnp.transpose(total, (2, 0, 1, 3))).astype(jnp.bfloat16)
    attn_flat = attn_local.reshape(local_rows, heads_here * HEAD_DIM)
    attn_spread = None
    grad_rows = fetch_grad(out_grad)
    grads4 = grad_rows.reshape(local_rows, groups_here, ratio, HEAD_DIM)
    delta = jnp.sum(grads4.astype(jnp.float32) * attn_local.astype(jnp.float32), axis=-1)
    delta = jnp.transpose(delta, (1, 2, 0))[..., None]

    def score_grads(start, size):
        scores, visible, key_block, value_block = block_inputs(start, size)
        weights = jnp.where(visible[None, None], jnp.exp(scores - row_max), 0.0)
        probs = weights / total
        probs_b = probs.astype(jnp.bfloat16)
        dprob = jnp.einsum(
            "rgjd,cgd->gjrc", grads4, value_block, preferred_element_type=jnp.float32
        )
        dscore_b = (probs * (dprob - delta)).astype(jnp.bfloat16)
        return (probs_b, dscore_b, key_block)

    def kv_terms(probs_b, dscore_b, size):
        key_term = (
            jnp.einsum("gjrc,rgjd->cgd", dscore_b, queries4, preferred_element_type=jnp.float32)
            * scale
        )
        value_term = jnp.einsum(
            "gjrc,rgjd->cgd", probs_b, grads4, preferred_element_type=jnp.float32
        )
        return jnp.concatenate(
            [key_term.reshape(size, width), value_term.reshape(size, width)], axis=1
        )

    start_query = jnp.zeros((local_rows, groups_here, ratio, HEAD_DIM), jnp.float32)

    def grad_step(query_acc, index):
        probs_b, dscore_b, key_block = score_grads(index * block, block)
        query_acc = query_acc + jnp.einsum(
            "gjrc,cgd->rgjd", dscore_b, key_block, preferred_element_type=jnp.float32
        )
        return (query_acc, kv_terms(probs_b, dscore_b, block))

    query_acc, term_blocks = lax.scan(grad_step, start_query, jnp.arange(blocks, dtype=jnp.int32))
    terms = term_blocks.reshape(ctx_size, local_rows, 2 * width)
    reduced = ctx_reduce_scatter(terms.astype(jnp.bfloat16), ctx_size)
    key_grad = reduced[:, :width].astype(jnp.bfloat16)
    value_grad = reduced[:, width:].astype(jnp.bfloat16)
    query_grad = (query_acc * scale).astype(jnp.bfloat16).reshape(local_rows, heads_here * HEAD_DIM)
    attn_spread = spread_output(attn_flat)
    return (attn_spread, query_grad, key_grad, value_grad)


def solution(mesh):
    placed = (P("ctx", "tp"), P("ctx", "tp"), P("ctx", "tp"), P(("ctx", "tp"), None), P(), P())
    return jax.shard_map(
        on_device,
        mesh=mesh,
        in_specs=placed,
        out_specs=(P(("ctx", "tp"), None), P("ctx", "tp"), P("ctx", "tp"), P("ctx", "tp")),
        check_vma=False,
    )
```

```python
import functools
import math

import jax
import jax.numpy as jnp
from jax import lax
from jax.experimental import pallas as pl
from jax.experimental.pallas import tpu as pltpu
from jax.sharding import PartitionSpec as P

HEAD_DIM = 128
SPAN = 64
MESH = pl.DeviceIdType.MESH


def greet_all(n, me):
    barrier = pltpu.get_barrier_semaphore()

    def greet(i, c):
        peer = lax.rem(me + i, n)
        pl.semaphore_signal(barrier, inc=1, device_id={"ctx": peer}, device_id_type=MESH)
        return c

    lax.fori_loop(1, n, greet, 0)
    pl.semaphore_wait(barrier, n - 1)


def gather_kernel(n, src_ref, out_ref, send_sem, recv_sem):
    me = lax.axis_index("ctx")
    greet_all(n, me)

    def copy_to(peer):
        return pltpu.make_async_remote_copy(
            src_ref, out_ref.at[me], send_sem.at[peer], recv_sem.at[me],
            device_id={"ctx": peer}, device_id_type=MESH)

    def copy_from(src):
        return pltpu.make_async_remote_copy(
            src_ref, out_ref.at[src], send_sem.at[src], recv_sem.at[src],
            device_id={"ctx": src}, device_id_type=MESH)

    def send(i, c):
        copy_to(lax.rem(me + i, n)).start()
        return c

    lax.fori_loop(1, n, send, 0)
    out_ref[me] = src_ref[...]

    def wait(i, c):
        copy_to(lax.rem(me + i, n)).wait_send()
        copy_from(lax.rem(me + n - i, n)).wait_recv()
        return c

    lax.fori_loop(1, n, wait, 0)


def ctx_gather(block, n):
    rows, width = block.shape
    return pl.pallas_call(
        functools.partial(gather_kernel, n),
        out_shape=jax.ShapeDtypeStruct((n, rows, width), block.dtype),
        in_specs=[pl.BlockSpec(memory_space=pltpu.VMEM)],
        out_specs=pl.BlockSpec(memory_space=pltpu.VMEM),
        scratch_shapes=[pltpu.SemaphoreType.DMA((n,)), pltpu.SemaphoreType.DMA((n,))],
        compiler_params=pltpu.CompilerParams(collective_id=0, has_side_effects=True),
    )(block)


def scatter_kernel(n, terms_ref, out_ref, held, send_sem, recv_sem):
    me = lax.axis_index("ctx")
    greet_all(n, me)

    def copy_to(peer):
        return pltpu.make_async_remote_copy(
            terms_ref.at[peer], held.at[me], send_sem.at[peer], recv_sem.at[me],
            device_id={"ctx": peer}, device_id_type=MESH)

    def copy_from(src):
        return pltpu.make_async_remote_copy(
            terms_ref.at[src], held.at[src], send_sem.at[src], recv_sem.at[src],
            device_id={"ctx": src}, device_id_type=MESH)

    def send(i, c):
        copy_to(lax.rem(me + i, n)).start()
        return c

    lax.fori_loop(1, n, send, 0)
    out_ref[...] = terms_ref[me].astype(jnp.float32)

    def wait(i, c):
        copy_to(lax.rem(me + i, n)).wait_send()
        src = lax.rem(me + n - i, n)
        copy_from(src).wait_recv()
        out_ref[...] += held[src].astype(jnp.float32)
        return c

    lax.fori_loop(1, n, wait, 0)


def ctx_reduce_scatter(terms, n):
    _, rows, width = terms.shape
    return pl.pallas_call(
        functools.partial(scatter_kernel, n),
        out_shape=jax.ShapeDtypeStruct((rows, width), jnp.float32),
        in_specs=[pl.BlockSpec(memory_space=pltpu.VMEM)],
        out_specs=pl.BlockSpec(memory_space=pltpu.VMEM),
        scratch_shapes=[
            pltpu.VMEM(terms.shape, terms.dtype),
            pltpu.SemaphoreType.DMA((n,)),
            pltpu.SemaphoreType.DMA((n,)),
        ],
        compiler_params=pltpu.CompilerParams(collective_id=1, has_side_effects=True),
    )(terms)


def fetch_grad(out_grad):
    return lax.all_to_all(out_grad, "tp", split_axis=1, concat_axis=0, tiled=True)


def spread_output(attn_flat):
    return lax.all_to_all(attn_flat, "tp", split_axis=0, concat_axis=1, tiled=True)


KEY_BLOCK = 512
NT_DIMS = (((1,), (1,)), ((), ()))
TN_DIMS = (((0,), (0,)), ((), ()))


def stack_heads(ref):
    heads = ref.shape[1] // HEAD_DIM
    return jnp.concatenate([ref[:, h * HEAD_DIM:(h + 1) * HEAD_DIM] for h in range(heads)], axis=0)


def unstack_heads(ref, value):
    rows = ref.shape[0]
    for h in range(ref.shape[1] // HEAD_DIM):
        ref[:, h * HEAD_DIM:(h + 1) * HEAD_DIM] = value[h * rows:(h + 1) * rows]


def key_block(kv_ref, cpos_ref, clab_ref, rpos, rlab, kb):
    start = pl.multiple_of(kb * KEY_BLOCK, KEY_BLOCK)
    keys = kv_ref[pl.ds(start, KEY_BLOCK), :HEAD_DIM]
    values = kv_ref[pl.ds(start, KEY_BLOCK), HEAD_DIM:]
    cpos = cpos_ref[:, pl.ds(start, KEY_BLOCK)]
    clab = clab_ref[:, pl.ds(start, KEY_BLOCK)]
    visible = (cpos <= rpos) & ((clab == 0) | (clab == rlab))
    return start, keys, values, visible


def fwd_kernel(q_ref, kv_ref, rpos_ref, rlab_ref, cpos_ref, clab_ref, o_ref, m_ref, l_ref, acc_sc):
    scale = 1.0 / math.sqrt(HEAD_DIM)
    queries = stack_heads(q_ref)
    rpos = rpos_ref[...]
    rlab = rlab_ref[...]
    m_ref[...] = jnp.full(m_ref.shape, -jnp.inf, jnp.float32)
    l_ref[...] = jnp.zeros(l_ref.shape, jnp.float32)
    acc_sc[...] = jnp.zeros(acc_sc.shape, jnp.float32)

    def body(kb, c):
        _, keys, values, visible = key_block(kv_ref, cpos_ref, clab_ref, rpos, rlab, kb)
        scores = lax.dot_general(queries, keys, NT_DIMS, preferred_element_type=jnp.float32) * scale
        scores = jnp.where(visible, scores, -jnp.inf)
        running = m_ref[...]
        new_max = jnp.maximum(running, jnp.max(scores, axis=-1, keepdims=True))
        shift = jnp.where(new_max == -jnp.inf, 0.0, new_max)
        factor = jnp.exp(running - shift)
        weights = jnp.where(visible, jnp.exp(scores - shift), 0.0)
        l_ref[...] = l_ref[...] * factor + jnp.sum(weights, axis=-1, keepdims=True)
        acc_sc[...] = acc_sc[...] * factor + jnp.dot(
            weights.astype(jnp.bfloat16), values, preferred_element_type=jnp.float32)
        m_ref[...] = new_max
        return c

    lax.fori_loop(0, kv_ref.shape[0] // KEY_BLOCK, body, 0)
    unstack_heads(o_ref, (acc_sc[...] / l_ref[...]).astype(o_ref.dtype))


def bwd_kernel(q_ref, g_ref, o_ref, kv_ref, rpos_ref, rlab_ref, cpos_ref, clab_ref, m_ref, l_ref,
               dq_ref, terms_ref, dq_sc):
    scale = 1.0 / math.sqrt(HEAD_DIM)
    queries = stack_heads(q_ref)
    grads = stack_heads(g_ref)
    outs = stack_heads(o_ref)
    delta = jnp.sum(grads.astype(jnp.float32) * outs.astype(jnp.float32), axis=-1, keepdims=True)
    rpos = rpos_ref[...]
    rlab = rlab_ref[...]
    row_max = m_ref[...]
    inv_total = 1.0 / l_ref[...]
    dq_sc[...] = jnp.zeros(dq_sc.shape, jnp.float32)

    def body(kb, c):
        start, keys, values, visible = key_block(kv_ref, cpos_ref, clab_ref, rpos, rlab, kb)
        scores = lax.dot_general(queries, keys, NT_DIMS, preferred_element_type=jnp.float32) * scale
        probs = jnp.where(visible, jnp.exp(scores - row_max), 0.0) * inv_total
        dprob = lax.dot_general(grads, values, NT_DIMS, preferred_element_type=jnp.float32)
        dscore_b = (probs * (dprob - delta)).astype(jnp.bfloat16)
        probs_b = probs.astype(jnp.bfloat16)
        dq_sc[...] += jnp.dot(dscore_b, keys, preferred_element_type=jnp.float32)
        key_term = lax.dot_general(dscore_b, queries, TN_DIMS, preferred_element_type=jnp.float32) * scale
        value_term = lax.dot_general(probs_b, grads, TN_DIMS, preferred_element_type=jnp.float32)
        terms_ref[pl.ds(start, KEY_BLOCK), :HEAD_DIM] = key_term.astype(terms_ref.dtype)
        terms_ref[pl.ds(start, KEY_BLOCK), HEAD_DIM:] = value_term.astype(terms_ref.dtype)
        return c

    lax.fori_loop(0, kv_ref.shape[0] // KEY_BLOCK, body, 0)
    unstack_heads(dq_ref, (dq_sc[...] * scale).astype(dq_ref.dtype))


def vmem_specs(n):
    return [pl.BlockSpec(memory_space=pltpu.VMEM)] * n


def attention_fwd(q, kv, rpos, rlab, cpos, clab):
    stacked = rpos.shape[0]
    return pl.pallas_call(
        fwd_kernel,
        out_shape=(
            jax.ShapeDtypeStruct(q.shape, jnp.bfloat16),
            jax.ShapeDtypeStruct((stacked, 1), jnp.float32),
            jax.ShapeDtypeStruct((stacked, 1), jnp.float32),
        ),
        in_specs=vmem_specs(6),
        out_specs=tuple(vmem_specs(3)),
        scratch_shapes=[pltpu.VMEM((stacked, HEAD_DIM), jnp.float32)],
    )(q, kv, rpos, rlab, cpos, clab)


def attention_bwd(q, g, o, kv, rpos, rlab, cpos, clab, m, l):
    stacked = rpos.shape[0]
    return pl.pallas_call(
        bwd_kernel,
        out_shape=(
            jax.ShapeDtypeStruct(q.shape, jnp.bfloat16),
            jax.ShapeDtypeStruct(kv.shape, jnp.bfloat16),
        ),
        in_specs=vmem_specs(10),
        out_specs=tuple(vmem_specs(2)),
        scratch_shapes=[pltpu.VMEM((stacked, HEAD_DIM), jnp.float32)],
    )(q, g, o, kv, rpos, rlab, cpos, clab, m, l)


def on_device(query_rows, key_rows, value_rows, out_grad, segment_ids, span_order):
    ctx_size = lax.axis_size("ctx")
    ctx_index = lax.axis_index("ctx")
    local_rows = query_rows.shape[0]
    heads_here = query_rows.shape[1] // HEAD_DIM
    total_rows = local_rows * ctx_size
    offsets = jnp.arange(SPAN, dtype=jnp.int32)
    positions = (SPAN * span_order[:, None] + offsets[None, :]).reshape(total_rows)
    prompt_end = jnp.sum((segment_ids == 0).astype(jnp.int32))
    chosen_end = jnp.sum((segment_ids <= 1).astype(jnp.int32))
    labels = (positions >= prompt_end).astype(jnp.int32) + (positions >= chosen_end).astype(jnp.int32)
    own_pos = lax.dynamic_slice_in_dim(positions, ctx_index * local_rows, local_rows, 0)
    own_label = lax.dynamic_slice_in_dim(labels, ctx_index * local_rows, local_rows, 0)
    rpos = jnp.tile(own_pos, heads_here)[:, None]
    rlab = jnp.tile(own_label, heads_here)[:, None]
    cpos = positions[None, :]
    clab = labels[None, :]
    kv_all = ctx_gather(jnp.concatenate([key_rows, value_rows], axis=1), ctx_size)
    kv_all = kv_all.reshape(total_rows, kv_all.shape[2])
    attn_local, row_max, total = attention_fwd(query_rows, kv_all, rpos, rlab, cpos, clab)
    grad_rows = fetch_grad(out_grad)
    query_grad, terms = attention_bwd(
        query_rows, grad_rows, attn_local, kv_all, rpos, rlab, cpos, clab, row_max, total)
    reduced = ctx_reduce_scatter(terms.reshape(ctx_size, local_rows, terms.shape[1]), ctx_size)
    key_grad = reduced[:, :HEAD_DIM].astype(jnp.bfloat16)
    value_grad = reduced[:, HEAD_DIM:].astype(jnp.bfloat16)
    attn_spread = spread_output(attn_local)
    return (attn_spread, query_grad, key_grad, value_grad)


def solution(mesh):
    placed = (P("ctx", "tp"), P("ctx", "tp"), P("ctx", "tp"), P(("ctx", "tp"), None), P(), P())
    return jax.shard_map(
        on_device,
        mesh=mesh,
        in_specs=placed,
        out_specs=(P(("ctx", "tp"), None), P("ctx", "tp"), P("ctx", "tp"), P("ctx", "tp")),
        check_vma=False,
    )
```

```python
import functools
import math

import jax
import jax.numpy as jnp
from jax import lax
from jax.experimental import pallas as pl
from jax.experimental.pallas import tpu as pltpu
from jax.sharding import PartitionSpec as P

HEAD_DIM = 128
SPAN = 64
MESH = pl.DeviceIdType.MESH


def greet_all(n, me):
    barrier = pltpu.get_barrier_semaphore()

    def greet(i, c):
        peer = lax.rem(me + i, n)
        pl.semaphore_signal(barrier, inc=1, device_id={"ctx": peer}, device_id_type=MESH)
        return c

    lax.fori_loop(1, n, greet, 0)
    pl.semaphore_wait(barrier, n - 1)


def gather_kernel(n, src_ref, out_ref, send_sem, recv_sem):
    me = lax.axis_index("ctx")
    greet_all(n, me)

    def copy_to(peer):
        return pltpu.make_async_remote_copy(
            src_ref, out_ref.at[me], send_sem.at[peer], recv_sem.at[me],
            device_id={"ctx": peer}, device_id_type=MESH)

    def copy_from(src):
        return pltpu.make_async_remote_copy(
            src_ref, out_ref.at[src], send_sem.at[src], recv_sem.at[src],
            device_id={"ctx": src}, device_id_type=MESH)

    def send(i, c):
        copy_to(lax.rem(me + i, n)).start()
        return c

    lax.fori_loop(1, n, send, 0)
    out_ref[me] = src_ref[...]

    def wait(i, c):
        copy_to(lax.rem(me + i, n)).wait_send()
        copy_from(lax.rem(me + n - i, n)).wait_recv()
        return c

    lax.fori_loop(1, n, wait, 0)


def ctx_gather(block, n):
    rows, width = block.shape
    return pl.pallas_call(
        functools.partial(gather_kernel, n),
        out_shape=jax.ShapeDtypeStruct((n, rows, width), block.dtype),
        in_specs=[pl.BlockSpec(memory_space=pltpu.VMEM)],
        out_specs=pl.BlockSpec(memory_space=pltpu.VMEM),
        scratch_shapes=[pltpu.SemaphoreType.DMA((n,)), pltpu.SemaphoreType.DMA((n,))],
        compiler_params=pltpu.CompilerParams(collective_id=0, has_side_effects=True),
    )(block)


def scatter_kernel(n, terms_ref, out_ref, held, send_sem, recv_sem):
    me = lax.axis_index("ctx")
    greet_all(n, me)

    def copy_to(peer):
        return pltpu.make_async_remote_copy(
            terms_ref.at[peer], held.at[me], send_sem.at[peer], recv_sem.at[me],
            device_id={"ctx": peer}, device_id_type=MESH)

    def copy_from(src):
        return pltpu.make_async_remote_copy(
            terms_ref.at[src], held.at[src], send_sem.at[src], recv_sem.at[src],
            device_id={"ctx": src}, device_id_type=MESH)

    def send(i, c):
        copy_to(lax.rem(me + i, n)).start()
        return c

    lax.fori_loop(1, n, send, 0)
    out_ref[...] = terms_ref[me].astype(jnp.float32)

    def wait(i, c):
        copy_to(lax.rem(me + i, n)).wait_send()
        src = lax.rem(me + n - i, n)
        copy_from(src).wait_recv()
        out_ref[...] += held[src].astype(jnp.float32)
        return c

    lax.fori_loop(1, n, wait, 0)


def ctx_reduce_scatter(terms, n):
    _, rows, width = terms.shape
    return pl.pallas_call(
        functools.partial(scatter_kernel, n),
        out_shape=jax.ShapeDtypeStruct((rows, width), jnp.float32),
        in_specs=[pl.BlockSpec(memory_space=pltpu.VMEM)],
        out_specs=pl.BlockSpec(memory_space=pltpu.VMEM),
        scratch_shapes=[
            pltpu.VMEM(terms.shape, terms.dtype),
            pltpu.SemaphoreType.DMA((n,)),
            pltpu.SemaphoreType.DMA((n,)),
        ],
        compiler_params=pltpu.CompilerParams(collective_id=1, has_side_effects=True),
    )(terms)


def fetch_grad(out_grad):
    return lax.all_to_all(out_grad, "tp", split_axis=1, concat_axis=0, tiled=True)


def spread_output(attn_flat):
    return lax.all_to_all(attn_flat, "tp", split_axis=0, concat_axis=1, tiled=True)


KEY_BLOCK = 512
NT_DIMS = (((1,), (1,)), ((), ()))
TN_DIMS = (((0,), (0,)), ((), ()))


def stack_heads(ref):
    heads = ref.shape[1] // HEAD_DIM
    return jnp.concatenate([ref[:, h * HEAD_DIM:(h + 1) * HEAD_DIM] for h in range(heads)], axis=0)


def unstack_heads(ref, value):
    rows = ref.shape[0]
    for h in range(ref.shape[1] // HEAD_DIM):
        ref[:, h * HEAD_DIM:(h + 1) * HEAD_DIM] = value[h * rows:(h + 1) * rows]


def key_block(kv_ref, cpos_ref, clab_ref, rpos, rlab, kb):
    start = pl.multiple_of(kb * KEY_BLOCK, KEY_BLOCK)
    keys = kv_ref[pl.ds(start, KEY_BLOCK), :HEAD_DIM]
    values = kv_ref[pl.ds(start, KEY_BLOCK), HEAD_DIM:]
    cpos = cpos_ref[:, pl.ds(start, KEY_BLOCK)]
    clab = clab_ref[:, pl.ds(start, KEY_BLOCK)]
    visible = (cpos <= rpos) & ((clab == 0) | (clab == rlab))
    return start, keys, values, visible


def fwd_kernel(q_ref, kv_ref, rpos_ref, rlab_ref, cpos_ref, clab_ref, o_ref, m_ref, l_ref, acc_sc):
    scale = 1.0 / math.sqrt(HEAD_DIM)
    queries = stack_heads(q_ref)
    rpos = rpos_ref[...]
    rlab = rlab_ref[...]
    m_ref[...] = jnp.full(m_ref.shape, -jnp.inf, jnp.float32)
    l_ref[...] = jnp.zeros(l_ref.shape, jnp.float32)
    acc_sc[...] = jnp.zeros(acc_sc.shape, jnp.float32)

    def body(kb, c):
        _, keys, values, visible = key_block(kv_ref, cpos_ref, clab_ref, rpos, rlab, kb)
        scores = lax.dot_general(queries, keys, NT_DIMS, preferred_element_type=jnp.float32) * scale
        scores = jnp.where(visible, scores, -jnp.inf)
        running = m_ref[...]
        new_max = jnp.maximum(running, jnp.max(scores, axis=-1, keepdims=True))
        shift = jnp.where(new_max == -jnp.inf, 0.0, new_max)
        factor = jnp.exp(running - shift)
        weights = jnp.where(visible, jnp.exp(scores - shift), 0.0)
        l_ref[...] = l_ref[...] * factor + jnp.sum(weights, axis=-1, keepdims=True)
        acc_sc[...] = acc_sc[...] * factor + jnp.dot(
            weights.astype(jnp.bfloat16), values, preferred_element_type=jnp.float32)
        m_ref[...] = new_max
        return c

    lax.fori_loop(0, kv_ref.shape[0] // KEY_BLOCK, body, 0)
    unstack_heads(o_ref, (acc_sc[...] / l_ref[...]).astype(o_ref.dtype))


def bwd_kernel(q_ref, g_ref, o_ref, kv_ref, rpos_ref, rlab_ref, cpos_ref, clab_ref, m_ref, l_ref,
               dq_ref, terms_ref, dq_sc):
    scale = 1.0 / math.sqrt(HEAD_DIM)
    queries = stack_heads(q_ref)
    grads = stack_heads(g_ref)
    outs = stack_heads(o_ref)
    delta = jnp.sum(grads.astype(jnp.float32) * outs.astype(jnp.float32), axis=-1, keepdims=True)
    rpos = rpos_ref[...]
    rlab = rlab_ref[...]
    row_max = m_ref[...]
    inv_total = 1.0 / l_ref[...]
    dq_sc[...] = jnp.zeros(dq_sc.shape, jnp.float32)

    def body(kb, c):
        start, keys, values, visible = key_block(kv_ref, cpos_ref, clab_ref, rpos, rlab, kb)
        scores = lax.dot_general(queries, keys, NT_DIMS, preferred_element_type=jnp.float32) * scale
        probs = jnp.where(visible, jnp.exp(scores - row_max), 0.0) * inv_total
        dprob = lax.dot_general(grads, values, NT_DIMS, preferred_element_type=jnp.float32)
        dscore_b = (probs * (dprob - delta)).astype(jnp.bfloat16)
        probs_b = probs.astype(jnp.bfloat16)
        dq_sc[...] += jnp.dot(dscore_b, keys, preferred_element_type=jnp.float32)
        key_term = lax.dot_general(dscore_b, queries, TN_DIMS, preferred_element_type=jnp.float32) * scale
        value_term = lax.dot_general(probs_b, grads, TN_DIMS, preferred_element_type=jnp.float32)
        terms_ref[pl.ds(start, KEY_BLOCK), :HEAD_DIM] = key_term.astype(terms_ref.dtype)
        terms_ref[pl.ds(start, KEY_BLOCK), HEAD_DIM:] = value_term.astype(terms_ref.dtype)
        return c

    lax.fori_loop(0, kv_ref.shape[0] // KEY_BLOCK, body, 0)
    unstack_heads(dq_ref, (dq_sc[...] * scale).astype(dq_ref.dtype))


def vmem_specs(n):
    return [pl.BlockSpec(memory_space=pltpu.VMEM)] * n


def attention_fwd(q, kv, rpos, rlab, cpos, clab):
    stacked = rpos.shape[0]
    return pl.pallas_call(
        fwd_kernel,
        out_shape=(
            jax.ShapeDtypeStruct(q.shape, jnp.bfloat16),
            jax.ShapeDtypeStruct((stacked, 1), jnp.float32),
            jax.ShapeDtypeStruct((stacked, 1), jnp.float32),
        ),
        in_specs=vmem_specs(6),
        out_specs=tuple(vmem_specs(3)),
        scratch_shapes=[pltpu.VMEM((stacked, HEAD_DIM), jnp.float32)],
    )(q, kv, rpos, rlab, cpos, clab)


def attention_bwd(q, g, o, kv, rpos, rlab, cpos, clab, m, l):
    stacked = rpos.shape[0]
    return pl.pallas_call(
        bwd_kernel,
        out_shape=(
            jax.ShapeDtypeStruct(q.shape, jnp.bfloat16),
            jax.ShapeDtypeStruct(kv.shape, jnp.bfloat16),
        ),
        in_specs=vmem_specs(10),
        out_specs=tuple(vmem_specs(2)),
        scratch_shapes=[pltpu.VMEM((stacked, HEAD_DIM), jnp.float32)],
    )(q, g, o, kv, rpos, rlab, cpos, clab, m, l)


def fwd_step(queries, keys, values, visible, m_sc, l_sc, acc_sc):
    scale = 1.0 / math.sqrt(HEAD_DIM)
    scores = lax.dot_general(queries, keys, NT_DIMS, preferred_element_type=jnp.float32) * scale
    scores = jnp.where(visible, scores, -jnp.inf)
    running = m_sc[...]
    new_max = jnp.maximum(running, jnp.max(scores, axis=-1, keepdims=True))
    shift = jnp.where(new_max == -jnp.inf, 0.0, new_max)
    factor = jnp.exp(running - shift)
    weights = jnp.where(visible, jnp.exp(scores - shift), 0.0)
    l_sc[...] = l_sc[...] * factor + jnp.sum(weights, axis=-1, keepdims=True)
    acc_sc[...] = acc_sc[...] * factor + jnp.dot(
        weights.astype(jnp.bfloat16), values, preferred_element_type=jnp.float32)
    m_sc[...] = new_max


def column_visible(cpos_ref, clab_ref, block, rpos, rlab):
    cpos = cpos_ref[pl.ds(block, 1), :]
    clab = clab_ref[pl.ds(block, 1), :]
    return (cpos <= rpos) & ((clab == 0) | (clab == rlab))


def gather_fwd_kernel(n, kv_src, q_ref, rpos_ref, rlab_ref, cpos_ref, clab_ref,
                      kv_out, o_ref, m_ref, l_ref, acc_sc, send_sem, recv_sem):
    me = lax.axis_index("ctx")
    greet_all(n, me)

    def copy_to(peer):
        return pltpu.make_async_remote_copy(
            kv_src, kv_out.at[me], send_sem.at[peer], recv_sem.at[me],
            device_id={"ctx": peer}, device_id_type=MESH)

    def copy_from(src):
        return pltpu.make_async_remote_copy(
            kv_src, kv_out.at[src], send_sem.at[src], recv_sem.at[src],
            device_id={"ctx": src}, device_id_type=MESH)

    def send(i, c):
        copy_to(lax.rem(me + i, n)).start()
        return c

    lax.fori_loop(1, n, send, 0)
    own = kv_src[...]
    kv_out[me] = own
    queries = stack_heads(q_ref)
    rpos = rpos_ref[...]
    rlab = rlab_ref[...]
    m_ref[...] = jnp.full(m_ref.shape, -jnp.inf, jnp.float32)
    l_ref[...] = jnp.zeros(l_ref.shape, jnp.float32)
    acc_sc[...] = jnp.zeros(acc_sc.shape, jnp.float32)
    fwd_step(queries, own[:, :HEAD_DIM], own[:, HEAD_DIM:],
             column_visible(cpos_ref, clab_ref, me, rpos, rlab), m_ref, l_ref, acc_sc)

    def arrive(i, c):
        src = lax.rem(me + n - i, n)
        copy_from(src).wait_recv()
        block = kv_out[src]
        fwd_step(queries, block[:, :HEAD_DIM], block[:, HEAD_DIM:],
                 column_visible(cpos_ref, clab_ref, src, rpos, rlab), m_ref, l_ref, acc_sc)
        return c

    lax.fori_loop(1, n, arrive, 0)
    unstack_heads(o_ref, (acc_sc[...] / l_ref[...]).astype(o_ref.dtype))

    def drain(i, c):
        copy_to(lax.rem(me + i, n)).wait_send()
        return c

    lax.fori_loop(1, n, drain, 0)


def gather_fwd(kv_local, q, rpos, rlab, cpos, clab, n):
    rows, width = kv_local.shape
    stacked = rpos.shape[0]
    return pl.pallas_call(
        functools.partial(gather_fwd_kernel, n),
        out_shape=(
            jax.ShapeDtypeStruct((n, rows, width), kv_local.dtype),
            jax.ShapeDtypeStruct(q.shape, jnp.bfloat16),
            jax.ShapeDtypeStruct((stacked, 1), jnp.float32),
            jax.ShapeDtypeStruct((stacked, 1), jnp.float32),
        ),
        in_specs=vmem_specs(6),
        out_specs=tuple(vmem_specs(4)),
        scratch_shapes=[
            pltpu.VMEM((stacked, HEAD_DIM), jnp.float32),
            pltpu.SemaphoreType.DMA((n,)),
            pltpu.SemaphoreType.DMA((n,)),
        ],
        compiler_params=pltpu.CompilerParams(collective_id=0, has_side_effects=True),
    )(kv_local, q, rpos, rlab, cpos, clab)


def bwd_scatter_kernel(n, q_ref, g_ref, o_ref, kv_ref, rpos_ref, rlab_ref, cpos_ref, clab_ref,
                       m_ref, l_ref, dq_ref, red_ref, terms_sc, held, dq_sc, send_sem, recv_sem):
    me = lax.axis_index("ctx")
    greet_all(n, me)
    scale = 1.0 / math.sqrt(HEAD_DIM)
    queries = stack_heads(q_ref)
    grads = stack_heads(g_ref)
    outs = stack_heads(o_ref)
    delta = jnp.sum(grads.astype(jnp.float32) * outs.astype(jnp.float32), axis=-1, keepdims=True)
    rpos = rpos_ref[...]
    rlab = rlab_ref[...]
    row_max = m_ref[...]
    inv_total = 1.0 / l_ref[...]
    dq_sc[...] = jnp.zeros(dq_sc.shape, jnp.float32)

    def copy_to(peer):
        return pltpu.make_async_remote_copy(
            terms_sc.at[peer], held.at[me], send_sem.at[peer], recv_sem.at[me],
            device_id={"ctx": peer}, device_id_type=MESH)

    def copy_from(src):
        return pltpu.make_async_remote_copy(
            terms_sc.at[src], held.at[src], send_sem.at[src], recv_sem.at[src],
            device_id={"ctx": src}, device_id_type=MESH)

    def block_terms(p):
        block = kv_ref[p]
        keys = block[:, :HEAD_DIM]
        values = block[:, HEAD_DIM:]
        visible = column_visible(cpos_ref, clab_ref, p, rpos, rlab)
        scores = lax.dot_general(queries, keys, NT_DIMS, preferred_element_type=jnp.float32) * scale
        probs = jnp.where(visible, jnp.exp(scores - row_max), 0.0) * inv_total
        dprob = lax.dot_general(grads, values, NT_DIMS, preferred_element_type=jnp.float32)
        dscore_b = (probs * (dprob - delta)).astype(jnp.bfloat16)
        probs_b = probs.astype(jnp.bfloat16)
        dq_sc[...] += jnp.dot(dscore_b, keys, preferred_element_type=jnp.float32)
        key_term = lax.dot_general(dscore_b, queries, TN_DIMS, preferred_element_type=jnp.float32) * scale
        value_term = lax.dot_general(probs_b, grads, TN_DIMS, preferred_element_type=jnp.float32)
        return jnp.concatenate([key_term, value_term], axis=1)

    red_ref[...] = block_terms(me)

    def step(i, c):
        peer = lax.rem(me + i, n)
        terms_sc[peer] = block_terms(peer).astype(terms_sc.dtype)

        @pl.when(i >= 2)
        def _():
            copy_to(lax.rem(me + i - 1, n)).start()

        return c

    lax.fori_loop(1, n, step, 0)
    copy_to(lax.rem(me + n - 1, n)).start()
    unstack_heads(dq_ref, (dq_sc[...] * scale).astype(dq_ref.dtype))

    def arrive(i, c):
        src = lax.rem(me + n - i, n)
        copy_from(src).wait_recv()
        red_ref[...] += held[src].astype(jnp.float32)
        return c

    lax.fori_loop(1, n, arrive, 0)

    def drain(i, c):
        copy_to(lax.rem(me + i, n)).wait_send()
        return c

    lax.fori_loop(1, n, drain, 0)


def bwd_scatter(q, g, o, kv, rpos, rlab, cpos, clab, m, l, n):
    _, rows, width = kv.shape
    stacked = rpos.shape[0]
    return pl.pallas_call(
        functools.partial(bwd_scatter_kernel, n),
        out_shape=(
            jax.ShapeDtypeStruct(q.shape, jnp.bfloat16),
            jax.ShapeDtypeStruct((rows, width), jnp.float32),
        ),
        in_specs=vmem_specs(10),
        out_specs=tuple(vmem_specs(2)),
        scratch_shapes=[
            pltpu.VMEM(kv.shape, jnp.bfloat16),
            pltpu.VMEM(kv.shape, jnp.bfloat16),
            pltpu.VMEM((stacked, HEAD_DIM), jnp.float32),
            pltpu.SemaphoreType.DMA((n,)),
            pltpu.SemaphoreType.DMA((n,)),
        ],
        compiler_params=pltpu.CompilerParams(collective_id=1, has_side_effects=True),
    )(q, g, o, kv, rpos, rlab, cpos, clab, m, l)


def on_device(query_rows, key_rows, value_rows, out_grad, segment_ids, span_order):
    ctx_size = lax.axis_size("ctx")
    ctx_index = lax.axis_index("ctx")
    local_rows = query_rows.shape[0]
    heads_here = query_rows.shape[1] // HEAD_DIM
    total_rows = local_rows * ctx_size
    offsets = jnp.arange(SPAN, dtype=jnp.int32)
    positions = (SPAN * span_order[:, None] + offsets[None, :]).reshape(total_rows)
    prompt_end = jnp.sum((segment_ids == 0).astype(jnp.int32))
    chosen_end = jnp.sum((segment_ids <= 1).astype(jnp.int32))
    labels = (positions >= prompt_end).astype(jnp.int32) + (positions >= chosen_end).astype(jnp.int32)
    own_pos = lax.dynamic_slice_in_dim(positions, ctx_index * local_rows, local_rows, 0)
    own_label = lax.dynamic_slice_in_dim(labels, ctx_index * local_rows, local_rows, 0)
    rpos = jnp.tile(own_pos, heads_here)[:, None]
    rlab = jnp.tile(own_label, heads_here)[:, None]
    cpos = positions.reshape(ctx_size, local_rows)
    clab = labels.reshape(ctx_size, local_rows)
    kv_local = jnp.concatenate([key_rows, value_rows], axis=1)
    kv_all, attn_local, row_max, total = gather_fwd(
        kv_local, query_rows, rpos, rlab, cpos, clab, ctx_size)
    grad_rows = fetch_grad(out_grad)
    query_grad, reduced = bwd_scatter(
        query_rows, grad_rows, attn_local, kv_all, rpos, rlab, cpos, clab, row_max, total, ctx_size)
    key_grad = reduced[:, :HEAD_DIM].astype(jnp.bfloat16)
    value_grad = reduced[:, HEAD_DIM:].astype(jnp.bfloat16)
    attn_spread = spread_output(attn_local)
    return (attn_spread, query_grad, key_grad, value_grad)


def solution(mesh):
    placed = (P("ctx", "tp"), P("ctx", "tp"), P("ctx", "tp"), P(("ctx", "tp"), None), P(), P())
    return jax.shard_map(
        on_device,
        mesh=mesh,
        in_specs=placed,
        out_specs=(P(("ctx", "tp"), None), P("ctx", "tp"), P("ctx", "tp"), P("ctx", "tp")),
        check_vma=False,
    )
```

```python
import functools
import math

import jax
import jax.numpy as jnp
from jax import lax
from jax.experimental import pallas as pl
from jax.experimental.pallas import tpu as pltpu
from jax.sharding import PartitionSpec as P

HEAD_DIM = 128
SPAN = 64
MESH = pl.DeviceIdType.MESH


def greet_all(n, me):
    barrier = pltpu.get_barrier_semaphore()

    def greet(i, c):
        peer = lax.rem(me + i, n)
        pl.semaphore_signal(barrier, inc=1, device_id={"ctx": peer}, device_id_type=MESH)
        return c

    lax.fori_loop(1, n, greet, 0)
    pl.semaphore_wait(barrier, n - 1)


def gather_kernel(n, src_ref, out_ref, send_sem, recv_sem):
    me = lax.axis_index("ctx")
    greet_all(n, me)

    def copy_to(peer):
        return pltpu.make_async_remote_copy(
            src_ref, out_ref.at[me], send_sem.at[peer], recv_sem.at[me],
            device_id={"ctx": peer}, device_id_type=MESH)

    def copy_from(src):
        return pltpu.make_async_remote_copy(
            src_ref, out_ref.at[src], send_sem.at[src], recv_sem.at[src],
            device_id={"ctx": src}, device_id_type=MESH)

    def send(i, c):
        copy_to(lax.rem(me + i, n)).start()
        return c

    lax.fori_loop(1, n, send, 0)
    out_ref[me] = src_ref[...]

    def wait(i, c):
        copy_to(lax.rem(me + i, n)).wait_send()
        copy_from(lax.rem(me + n - i, n)).wait_recv()
        return c

    lax.fori_loop(1, n, wait, 0)


def ctx_gather(block, n):
    rows, width = block.shape
    return pl.pallas_call(
        functools.partial(gather_kernel, n),
        out_shape=jax.ShapeDtypeStruct((n, rows, width), block.dtype),
        in_specs=[pl.BlockSpec(memory_space=pltpu.VMEM)],
        out_specs=pl.BlockSpec(memory_space=pltpu.VMEM),
        scratch_shapes=[pltpu.SemaphoreType.DMA((n,)), pltpu.SemaphoreType.DMA((n,))],
        compiler_params=pltpu.CompilerParams(collective_id=0, has_side_effects=True),
    )(block)


def scatter_kernel(n, terms_ref, out_ref, held, send_sem, recv_sem):
    me = lax.axis_index("ctx")
    greet_all(n, me)

    def copy_to(peer):
        return pltpu.make_async_remote_copy(
            terms_ref.at[peer], held.at[me], send_sem.at[peer], recv_sem.at[me],
            device_id={"ctx": peer}, device_id_type=MESH)

    def copy_from(src):
        return pltpu.make_async_remote_copy(
            terms_ref.at[src], held.at[src], send_sem.at[src], recv_sem.at[src],
            device_id={"ctx": src}, device_id_type=MESH)

    def send(i, c):
        copy_to(lax.rem(me + i, n)).start()
        return c

    lax.fori_loop(1, n, send, 0)
    out_ref[...] = terms_ref[me].astype(jnp.float32)

    def wait(i, c):
        copy_to(lax.rem(me + i, n)).wait_send()
        src = lax.rem(me + n - i, n)
        copy_from(src).wait_recv()
        out_ref[...] += held[src].astype(jnp.float32)
        return c

    lax.fori_loop(1, n, wait, 0)


def ctx_reduce_scatter(terms, n):
    _, rows, width = terms.shape
    return pl.pallas_call(
        functools.partial(scatter_kernel, n),
        out_shape=jax.ShapeDtypeStruct((rows, width), jnp.float32),
        in_specs=[pl.BlockSpec(memory_space=pltpu.VMEM)],
        out_specs=pl.BlockSpec(memory_space=pltpu.VMEM),
        scratch_shapes=[
            pltpu.VMEM(terms.shape, terms.dtype),
            pltpu.SemaphoreType.DMA((n,)),
            pltpu.SemaphoreType.DMA((n,)),
        ],
        compiler_params=pltpu.CompilerParams(collective_id=1, has_side_effects=True),
    )(terms)


def fetch_grad(out_grad):
    return lax.all_to_all(out_grad, "tp", split_axis=1, concat_axis=0, tiled=True)


def spread_output(attn_flat):
    return lax.all_to_all(attn_flat, "tp", split_axis=0, concat_axis=1, tiled=True)


KEY_BLOCK = 512
SEND_WINDOW = 6
NT_DIMS = (((1,), (1,)), ((), ()))
TN_DIMS = (((0,), (0,)), ((), ()))


def stack_heads(ref):
    heads = ref.shape[1] // HEAD_DIM
    return jnp.concatenate([ref[:, h * HEAD_DIM:(h + 1) * HEAD_DIM] for h in range(heads)], axis=0)


def unstack_heads(ref, value):
    rows = ref.shape[0]
    for h in range(ref.shape[1] // HEAD_DIM):
        ref[:, h * HEAD_DIM:(h + 1) * HEAD_DIM] = value[h * rows:(h + 1) * rows]


def key_block(kv_ref, cpos_ref, clab_ref, rpos, rlab, kb):
    start = pl.multiple_of(kb * KEY_BLOCK, KEY_BLOCK)
    keys = kv_ref[pl.ds(start, KEY_BLOCK), :HEAD_DIM]
    values = kv_ref[pl.ds(start, KEY_BLOCK), HEAD_DIM:]
    cpos = cpos_ref[:, pl.ds(start, KEY_BLOCK)]
    clab = clab_ref[:, pl.ds(start, KEY_BLOCK)]
    visible = (cpos <= rpos) & ((clab == 0) | (clab == rlab))
    return start, keys, values, visible


def fwd_kernel(q_ref, kv_ref, rpos_ref, rlab_ref, cpos_ref, clab_ref, o_ref, m_ref, l_ref, acc_sc):
    scale = 1.0 / math.sqrt(HEAD_DIM)
    queries = stack_heads(q_ref)
    rpos = rpos_ref[...]
    rlab = rlab_ref[...]
    m_ref[...] = jnp.full(m_ref.shape, -jnp.inf, jnp.float32)
    l_ref[...] = jnp.zeros(l_ref.shape, jnp.float32)
    acc_sc[...] = jnp.zeros(acc_sc.shape, jnp.float32)

    def body(kb, c):
        _, keys, values, visible = key_block(kv_ref, cpos_ref, clab_ref, rpos, rlab, kb)
        scores = lax.dot_general(queries, keys, NT_DIMS, preferred_element_type=jnp.float32) * scale
        scores = jnp.where(visible, scores, -jnp.inf)
        running = m_ref[...]
        new_max = jnp.maximum(running, jnp.max(scores, axis=-1, keepdims=True))
        shift = jnp.where(new_max == -jnp.inf, 0.0, new_max)
        factor = jnp.exp(running - shift)
        weights = jnp.where(visible, jnp.exp(scores - shift), 0.0)
        l_ref[...] = l_ref[...] * factor + jnp.sum(weights, axis=-1, keepdims=True)
        acc_sc[...] = acc_sc[...] * factor + jnp.dot(
            weights.astype(jnp.bfloat16), values, preferred_element_type=jnp.float32)
        m_ref[...] = new_max
        return c

    lax.fori_loop(0, kv_ref.shape[0] // KEY_BLOCK, body, 0)
    unstack_heads(o_ref, (acc_sc[...] / l_ref[...]).astype(o_ref.dtype))


def bwd_kernel(q_ref, g_ref, o_ref, kv_ref, rpos_ref, rlab_ref, cpos_ref, clab_ref, m_ref, l_ref,
               dq_ref, terms_ref, dq_sc):
    scale = 1.0 / math.sqrt(HEAD_DIM)
    queries = stack_heads(q_ref)
    grads = stack_heads(g_ref)
    outs = stack_heads(o_ref)
    delta = jnp.sum(grads.astype(jnp.float32) * outs.astype(jnp.float32), axis=-1, keepdims=True)
    rpos = rpos_ref[...]
    rlab = rlab_ref[...]
    row_max = m_ref[...]
    inv_total = 1.0 / l_ref[...]
    dq_sc[...] = jnp.zeros(dq_sc.shape, jnp.float32)

    def body(kb, c):
        start, keys, values, visible = key_block(kv_ref, cpos_ref, clab_ref, rpos, rlab, kb)
        scores = lax.dot_general(queries, keys, NT_DIMS, preferred_element_type=jnp.float32) * scale
        probs = jnp.where(visible, jnp.exp(scores - row_max), 0.0) * inv_total
        dprob = lax.dot_general(grads, values, NT_DIMS, preferred_element_type=jnp.float32)
        dscore_b = (probs * (dprob - delta)).astype(jnp.bfloat16)
        probs_b = probs.astype(jnp.bfloat16)
        dq_sc[...] += jnp.dot(dscore_b, keys, preferred_element_type=jnp.float32)
        key_term = lax.dot_general(dscore_b, queries, TN_DIMS, preferred_element_type=jnp.float32) * scale
        value_term = lax.dot_general(probs_b, grads, TN_DIMS, preferred_element_type=jnp.float32)
        terms_ref[pl.ds(start, KEY_BLOCK), :HEAD_DIM] = key_term.astype(terms_ref.dtype)
        terms_ref[pl.ds(start, KEY_BLOCK), HEAD_DIM:] = value_term.astype(terms_ref.dtype)
        return c

    lax.fori_loop(0, kv_ref.shape[0] // KEY_BLOCK, body, 0)
    unstack_heads(dq_ref, (dq_sc[...] * scale).astype(dq_ref.dtype))


def vmem_specs(n):
    return [pl.BlockSpec(memory_space=pltpu.VMEM)] * n


def attention_fwd(q, kv, rpos, rlab, cpos, clab):
    stacked = rpos.shape[0]
    return pl.pallas_call(
        fwd_kernel,
        out_shape=(
            jax.ShapeDtypeStruct(q.shape, jnp.bfloat16),
            jax.ShapeDtypeStruct((stacked, 1), jnp.float32),
            jax.ShapeDtypeStruct((stacked, 1), jnp.float32),
        ),
        in_specs=vmem_specs(6),
        out_specs=tuple(vmem_specs(3)),
        scratch_shapes=[pltpu.VMEM((stacked, HEAD_DIM), jnp.float32)],
    )(q, kv, rpos, rlab, cpos, clab)


def attention_bwd(q, g, o, kv, rpos, rlab, cpos, clab, m, l):
    stacked = rpos.shape[0]
    return pl.pallas_call(
        bwd_kernel,
        out_shape=(
            jax.ShapeDtypeStruct(q.shape, jnp.bfloat16),
            jax.ShapeDtypeStruct(kv.shape, jnp.bfloat16),
        ),
        in_specs=vmem_specs(10),
        out_specs=tuple(vmem_specs(2)),
        scratch_shapes=[pltpu.VMEM((stacked, HEAD_DIM), jnp.float32)],
    )(q, g, o, kv, rpos, rlab, cpos, clab, m, l)


def fwd_step(queries, keys, values, visible, m_sc, l_sc, acc_sc):
    scale = 1.0 / math.sqrt(HEAD_DIM)
    scores = lax.dot_general(queries, keys, NT_DIMS, preferred_element_type=jnp.float32) * scale
    scores = jnp.where(visible, scores, -jnp.inf)
    running = m_sc[...]
    new_max = jnp.maximum(running, jnp.max(scores, axis=-1, keepdims=True))
    shift = jnp.where(new_max == -jnp.inf, 0.0, new_max)
    factor = jnp.exp(running - shift)
    weights = jnp.where(visible, jnp.exp(scores - shift), 0.0)
    l_sc[...] = l_sc[...] * factor + jnp.sum(weights, axis=-1, keepdims=True)
    acc_sc[...] = acc_sc[...] * factor + jnp.dot(
        weights.astype(jnp.bfloat16), values, preferred_element_type=jnp.float32)
    m_sc[...] = new_max


def column_visible(cpos_ref, clab_ref, block, rpos, rlab):
    cpos = cpos_ref[pl.ds(block, 1), :]
    clab = clab_ref[pl.ds(block, 1), :]
    return (cpos <= rpos) & ((clab == 0) | (clab == rlab))


def gather_fwd_kernel(n, kv_src, q_ref, rpos_ref, rlab_ref, cpos_ref, clab_ref,
                      kv_out, o_ref, m_ref, l_ref, acc_sc, send_sem, recv_sem):
    me = lax.axis_index("ctx")
    greet_all(n, me)

    def copy_to(peer):
        return pltpu.make_async_remote_copy(
            kv_src, kv_out.at[me], send_sem.at[peer], recv_sem.at[me],
            device_id={"ctx": peer}, device_id_type=MESH)

    def copy_from(src):
        return pltpu.make_async_remote_copy(
            kv_src, kv_out.at[src], send_sem.at[src], recv_sem.at[src],
            device_id={"ctx": src}, device_id_type=MESH)

    window = min(SEND_WINDOW, n - 1)

    def send(i, c):
        copy_to(lax.rem(me + i, n)).start()
        return c

    lax.fori_loop(1, window + 1, send, 0)
    own = kv_src[...]
    kv_out[me] = own
    queries = stack_heads(q_ref)
    rpos = rpos_ref[...]
    rlab = rlab_ref[...]
    m_ref[...] = jnp.full(m_ref.shape, -jnp.inf, jnp.float32)
    l_ref[...] = jnp.zeros(l_ref.shape, jnp.float32)
    acc_sc[...] = jnp.zeros(acc_sc.shape, jnp.float32)
    fwd_step(queries, own[:, :HEAD_DIM], own[:, HEAD_DIM:],
             column_visible(cpos_ref, clab_ref, me, rpos, rlab), m_ref, l_ref, acc_sc)

    def arrive(i, c):
        src = lax.rem(me + n - i, n)
        copy_from(src).wait_recv()
        block = kv_out[src]
        fwd_step(queries, block[:, :HEAD_DIM], block[:, HEAD_DIM:],
                 column_visible(cpos_ref, clab_ref, src, rpos, rlab), m_ref, l_ref, acc_sc)

        @pl.when(i + window <= n - 1)
        def _():
            copy_to(lax.rem(me + i, n)).wait_send()
            copy_to(lax.rem(me + i + window, n)).start()

        return c

    lax.fori_loop(1, n, arrive, 0)
    unstack_heads(o_ref, (acc_sc[...] / l_ref[...]).astype(o_ref.dtype))

    def drain(i, c):
        copy_to(lax.rem(me + i, n)).wait_send()
        return c

    lax.fori_loop(n - window, n, drain, 0)


def gather_fwd(kv_local, q, rpos, rlab, cpos, clab, n):
    rows, width = kv_local.shape
    stacked = rpos.shape[0]
    return pl.pallas_call(
        functools.partial(gather_fwd_kernel, n),
        out_shape=(
            jax.ShapeDtypeStruct((n, rows, width), kv_local.dtype),
            jax.ShapeDtypeStruct(q.shape, jnp.bfloat16),
            jax.ShapeDtypeStruct((stacked, 1), jnp.float32),
            jax.ShapeDtypeStruct((stacked, 1), jnp.float32),
        ),
        in_specs=vmem_specs(6),
        out_specs=tuple(vmem_specs(4)),
        scratch_shapes=[
            pltpu.VMEM((stacked, HEAD_DIM), jnp.float32),
            pltpu.SemaphoreType.DMA((n,)),
            pltpu.SemaphoreType.DMA((n,)),
        ],
        compiler_params=pltpu.CompilerParams(collective_id=0, has_side_effects=True),
    )(kv_local, q, rpos, rlab, cpos, clab)


def bwd_scatter_kernel(n, q_ref, g_ref, o_ref, kv_ref, rpos_ref, rlab_ref, cpos_ref, clab_ref,
                       m_ref, l_ref, dq_ref, red_ref, terms_sc, held, dq_sc, send_sem, recv_sem):
    me = lax.axis_index("ctx")
    greet_all(n, me)
    scale = 1.0 / math.sqrt(HEAD_DIM)
    queries = stack_heads(q_ref)
    grads = stack_heads(g_ref)
    outs = stack_heads(o_ref)
    delta = jnp.sum(grads.astype(jnp.float32) * outs.astype(jnp.float32), axis=-1, keepdims=True)
    rpos = rpos_ref[...]
    rlab = rlab_ref[...]
    row_max = m_ref[...]
    inv_total = 1.0 / l_ref[...]
    dq_sc[...] = jnp.zeros(dq_sc.shape, jnp.float32)

    def copy_to(peer):
        return pltpu.make_async_remote_copy(
            terms_sc.at[peer], held.at[me], send_sem.at[peer], recv_sem.at[me],
            device_id={"ctx": peer}, device_id_type=MESH)

    def copy_from(src):
        return pltpu.make_async_remote_copy(
            terms_sc.at[src], held.at[src], send_sem.at[src], recv_sem.at[src],
            device_id={"ctx": src}, device_id_type=MESH)

    def block_terms(p):
        block = kv_ref[p]
        keys = block[:, :HEAD_DIM]
        values = block[:, HEAD_DIM:]
        visible = column_visible(cpos_ref, clab_ref, p, rpos, rlab)
        scores = lax.dot_general(queries, keys, NT_DIMS, preferred_element_type=jnp.float32) * scale
        probs = jnp.where(visible, jnp.exp(scores - row_max), 0.0) * inv_total
        dprob = lax.dot_general(grads, values, NT_DIMS, preferred_element_type=jnp.float32)
        dscore_b = (probs * (dprob - delta)).astype(jnp.bfloat16)
        probs_b = probs.astype(jnp.bfloat16)
        dq_sc[...] += jnp.dot(dscore_b, keys, preferred_element_type=jnp.float32)
        key_term = lax.dot_general(dscore_b, queries, TN_DIMS, preferred_element_type=jnp.float32) * scale
        value_term = lax.dot_general(probs_b, grads, TN_DIMS, preferred_element_type=jnp.float32)
        return jnp.concatenate([key_term, value_term], axis=1)

    red_ref[...] = block_terms(me)

    def step(i, c):
        peer = lax.rem(me + i, n)
        terms_sc[peer] = block_terms(peer).astype(terms_sc.dtype)

        @pl.when(i >= 2)
        def _():
            copy_to(lax.rem(me + i - 1, n)).start()

        return c

    lax.fori_loop(1, n, step, 0)
    copy_to(lax.rem(me + n - 1, n)).start()
    unstack_heads(dq_ref, (dq_sc[...] * scale).astype(dq_ref.dtype))

    def arrive(i, c):
        src = lax.rem(me + n - i, n)
        copy_from(src).wait_recv()
        red_ref[...] += held[src].astype(jnp.float32)
        return c

    lax.fori_loop(1, n, arrive, 0)

    def drain(i, c):
        copy_to(lax.rem(me + i, n)).wait_send()
        return c

    lax.fori_loop(1, n, drain, 0)


def bwd_scatter(q, g, o, kv, rpos, rlab, cpos, clab, m, l, n):
    _, rows, width = kv.shape
    stacked = rpos.shape[0]
    return pl.pallas_call(
        functools.partial(bwd_scatter_kernel, n),
        out_shape=(
            jax.ShapeDtypeStruct(q.shape, jnp.bfloat16),
            jax.ShapeDtypeStruct((rows, width), jnp.float32),
        ),
        in_specs=vmem_specs(10),
        out_specs=tuple(vmem_specs(2)),
        scratch_shapes=[
            pltpu.VMEM(kv.shape, jnp.bfloat16),
            pltpu.VMEM(kv.shape, jnp.bfloat16),
            pltpu.VMEM((stacked, HEAD_DIM), jnp.float32),
            pltpu.SemaphoreType.DMA((n,)),
            pltpu.SemaphoreType.DMA((n,)),
        ],
        compiler_params=pltpu.CompilerParams(collective_id=1, has_side_effects=True),
    )(q, g, o, kv, rpos, rlab, cpos, clab, m, l)


def on_device(query_rows, key_rows, value_rows, out_grad, segment_ids, span_order):
    ctx_size = lax.axis_size("ctx")
    ctx_index = lax.axis_index("ctx")
    local_rows = query_rows.shape[0]
    heads_here = query_rows.shape[1] // HEAD_DIM
    total_rows = local_rows * ctx_size
    offsets = jnp.arange(SPAN, dtype=jnp.int32)
    positions = (SPAN * span_order[:, None] + offsets[None, :]).reshape(total_rows)
    prompt_end = jnp.sum((segment_ids == 0).astype(jnp.int32))
    chosen_end = jnp.sum((segment_ids <= 1).astype(jnp.int32))
    labels = (positions >= prompt_end).astype(jnp.int32) + (positions >= chosen_end).astype(jnp.int32)
    own_pos = lax.dynamic_slice_in_dim(positions, ctx_index * local_rows, local_rows, 0)
    own_label = lax.dynamic_slice_in_dim(labels, ctx_index * local_rows, local_rows, 0)
    rpos = jnp.tile(own_pos, heads_here)[:, None]
    rlab = jnp.tile(own_label, heads_here)[:, None]
    cpos = positions.reshape(ctx_size, local_rows)
    clab = labels.reshape(ctx_size, local_rows)
    kv_local = jnp.concatenate([key_rows, value_rows], axis=1)
    kv_all, attn_local, row_max, total = gather_fwd(
        kv_local, query_rows, rpos, rlab, cpos, clab, ctx_size)
    grad_rows = fetch_grad(out_grad)
    query_grad, reduced = bwd_scatter(
        query_rows, grad_rows, attn_local, kv_all, rpos, rlab, cpos, clab, row_max, total, ctx_size)
    key_grad = reduced[:, :HEAD_DIM].astype(jnp.bfloat16)
    value_grad = reduced[:, HEAD_DIM:].astype(jnp.bfloat16)
    attn_spread = spread_output(attn_local)
    return (attn_spread, query_grad, key_grad, value_grad)


def solution(mesh):
    placed = (P("ctx", "tp"), P("ctx", "tp"), P("ctx", "tp"), P(("ctx", "tp"), None), P(), P())
    return jax.shard_map(
        on_device,
        mesh=mesh,
        in_specs=placed,
        out_specs=(P(("ctx", "tp"), None), P("ctx", "tp"), P("ctx", "tp"), P("ctx", "tp")),
        check_vma=False,
    )
```

```python
import functools
import math

import jax
import jax.numpy as jnp
from jax import lax
from jax.experimental import pallas as pl
from jax.experimental.pallas import tpu as pltpu
from jax.sharding import PartitionSpec as P

HEAD_DIM = 128
SPAN = 64
MESH = pl.DeviceIdType.MESH


def greet_all(n, me):
    barrier = pltpu.get_barrier_semaphore()

    def greet(i, c):
        peer = lax.rem(me + i, n)
        pl.semaphore_signal(barrier, inc=1, device_id={"ctx": peer}, device_id_type=MESH)
        return c

    lax.fori_loop(1, n, greet, 0)
    pl.semaphore_wait(barrier, n - 1)


def gather_kernel(n, src_ref, out_ref, send_sem, recv_sem):
    me = lax.axis_index("ctx")
    greet_all(n, me)

    def copy_to(peer):
        return pltpu.make_async_remote_copy(
            src_ref, out_ref.at[me], send_sem.at[peer], recv_sem.at[me],
            device_id={"ctx": peer}, device_id_type=MESH)

    def copy_from(src):
        return pltpu.make_async_remote_copy(
            src_ref, out_ref.at[src], send_sem.at[src], recv_sem.at[src],
            device_id={"ctx": src}, device_id_type=MESH)

    def send(i, c):
        copy_to(lax.rem(me + i, n)).start()
        return c

    lax.fori_loop(1, n, send, 0)
    out_ref[me] = src_ref[...]

    def wait(i, c):
        copy_to(lax.rem(me + i, n)).wait_send()
        copy_from(lax.rem(me + n - i, n)).wait_recv()
        return c

    lax.fori_loop(1, n, wait, 0)


def ctx_gather(block, n):
    rows, width = block.shape
    return pl.pallas_call(
        functools.partial(gather_kernel, n),
        out_shape=jax.ShapeDtypeStruct((n, rows, width), block.dtype),
        in_specs=[pl.BlockSpec(memory_space=pltpu.VMEM)],
        out_specs=pl.BlockSpec(memory_space=pltpu.VMEM),
        scratch_shapes=[pltpu.SemaphoreType.DMA((n,)), pltpu.SemaphoreType.DMA((n,))],
        compiler_params=pltpu.CompilerParams(collective_id=0, has_side_effects=True),
    )(block)


def scatter_kernel(n, terms_ref, out_ref, held, send_sem, recv_sem):
    me = lax.axis_index("ctx")
    greet_all(n, me)

    def copy_to(peer):
        return pltpu.make_async_remote_copy(
            terms_ref.at[peer], held.at[me], send_sem.at[peer], recv_sem.at[me],
            device_id={"ctx": peer}, device_id_type=MESH)

    def copy_from(src):
        return pltpu.make_async_remote_copy(
            terms_ref.at[src], held.at[src], send_sem.at[src], recv_sem.at[src],
            device_id={"ctx": src}, device_id_type=MESH)

    def send(i, c):
        copy_to(lax.rem(me + i, n)).start()
        return c

    lax.fori_loop(1, n, send, 0)
    out_ref[...] = terms_ref[me].astype(jnp.float32)

    def wait(i, c):
        copy_to(lax.rem(me + i, n)).wait_send()
        src = lax.rem(me + n - i, n)
        copy_from(src).wait_recv()
        out_ref[...] += held[src].astype(jnp.float32)
        return c

    lax.fori_loop(1, n, wait, 0)


def ctx_reduce_scatter(terms, n):
    _, rows, width = terms.shape
    return pl.pallas_call(
        functools.partial(scatter_kernel, n),
        out_shape=jax.ShapeDtypeStruct((rows, width), jnp.float32),
        in_specs=[pl.BlockSpec(memory_space=pltpu.VMEM)],
        out_specs=pl.BlockSpec(memory_space=pltpu.VMEM),
        scratch_shapes=[
            pltpu.VMEM(terms.shape, terms.dtype),
            pltpu.SemaphoreType.DMA((n,)),
            pltpu.SemaphoreType.DMA((n,)),
        ],
        compiler_params=pltpu.CompilerParams(collective_id=1, has_side_effects=True),
    )(terms)


def fetch_grad(out_grad):
    return lax.all_to_all(out_grad, "tp", split_axis=1, concat_axis=0, tiled=True)


def spread_output(attn_flat):
    return lax.all_to_all(attn_flat, "tp", split_axis=0, concat_axis=1, tiled=True)


KEY_BLOCK = 512
SEND_WINDOW = 6
ARRIVAL_GROUP = 4
NT_DIMS = (((1,), (1,)), ((), ()))
TN_DIMS = (((0,), (0,)), ((), ()))


def stack_heads(ref):
    heads = ref.shape[1] // HEAD_DIM
    return jnp.concatenate([ref[:, h * HEAD_DIM:(h + 1) * HEAD_DIM] for h in range(heads)], axis=0)


def unstack_heads(ref, value):
    rows = ref.shape[0]
    for h in range(ref.shape[1] // HEAD_DIM):
        ref[:, h * HEAD_DIM:(h + 1) * HEAD_DIM] = value[h * rows:(h + 1) * rows]


def key_block(kv_ref, cpos_ref, clab_ref, rpos, rlab, kb):
    start = pl.multiple_of(kb * KEY_BLOCK, KEY_BLOCK)
    keys = kv_ref[pl.ds(start, KEY_BLOCK), :HEAD_DIM]
    values = kv_ref[pl.ds(start, KEY_BLOCK), HEAD_DIM:]
    cpos = cpos_ref[:, pl.ds(start, KEY_BLOCK)]
    clab = clab_ref[:, pl.ds(start, KEY_BLOCK)]
    visible = (cpos <= rpos) & ((clab == 0) | (clab == rlab))
    return start, keys, values, visible


def fwd_kernel(q_ref, kv_ref, rpos_ref, rlab_ref, cpos_ref, clab_ref, o_ref, m_ref, l_ref, acc_sc):
    scale = 1.0 / math.sqrt(HEAD_DIM)
    queries = stack_heads(q_ref)
    rpos = rpos_ref[...]
    rlab = rlab_ref[...]
    m_ref[...] = jnp.full(m_ref.shape, -jnp.inf, jnp.float32)
    l_ref[...] = jnp.zeros(l_ref.shape, jnp.float32)
    acc_sc[...] = jnp.zeros(acc_sc.shape, jnp.float32)

    def body(kb, c):
        _, keys, values, visible = key_block(kv_ref, cpos_ref, clab_ref, rpos, rlab, kb)
        scores = lax.dot_general(queries, keys, NT_DIMS, preferred_element_type=jnp.float32) * scale
        scores = jnp.where(visible, scores, -jnp.inf)
        running = m_ref[...]
        new_max = jnp.maximum(running, jnp.max(scores, axis=-1, keepdims=True))
        shift = jnp.where(new_max == -jnp.inf, 0.0, new_max)
        factor = jnp.exp(running - shift)
        weights = jnp.where(visible, jnp.exp(scores - shift), 0.0)
        l_ref[...] = l_ref[...] * factor + jnp.sum(weights, axis=-1, keepdims=True)
        acc_sc[...] = acc_sc[...] * factor + jnp.dot(
            weights.astype(jnp.bfloat16), values, preferred_element_type=jnp.float32)
        m_ref[...] = new_max
        return c

    lax.fori_loop(0, kv_ref.shape[0] // KEY_BLOCK, body, 0)
    unstack_heads(o_ref, (acc_sc[...] / l_ref[...]).astype(o_ref.dtype))


def bwd_kernel(q_ref, g_ref, o_ref, kv_ref, rpos_ref, rlab_ref, cpos_ref, clab_ref, m_ref, l_ref,
               dq_ref, terms_ref, dq_sc):
    scale = 1.0 / math.sqrt(HEAD_DIM)
    queries = stack_heads(q_ref)
    grads = stack_heads(g_ref)
    outs = stack_heads(o_ref)
    delta = jnp.sum(grads.astype(jnp.float32) * outs.astype(jnp.float32), axis=-1, keepdims=True)
    rpos = rpos_ref[...]
    rlab = rlab_ref[...]
    row_max = m_ref[...]
    inv_total = 1.0 / l_ref[...]
    dq_sc[...] = jnp.zeros(dq_sc.shape, jnp.float32)

    def body(kb, c):
        start, keys, values, visible = key_block(kv_ref, cpos_ref, clab_ref, rpos, rlab, kb)
        scores = lax.dot_general(queries, keys, NT_DIMS, preferred_element_type=jnp.float32) * scale
        probs = jnp.where(visible, jnp.exp(scores - row_max), 0.0) * inv_total
        dprob = lax.dot_general(grads, values, NT_DIMS, preferred_element_type=jnp.float32)
        dscore_b = (probs * (dprob - delta)).astype(jnp.bfloat16)
        probs_b = probs.astype(jnp.bfloat16)
        dq_sc[...] += jnp.dot(dscore_b, keys, preferred_element_type=jnp.float32)
        key_term = lax.dot_general(dscore_b, queries, TN_DIMS, preferred_element_type=jnp.float32) * scale
        value_term = lax.dot_general(probs_b, grads, TN_DIMS, preferred_element_type=jnp.float32)
        terms_ref[pl.ds(start, KEY_BLOCK), :HEAD_DIM] = key_term.astype(terms_ref.dtype)
        terms_ref[pl.ds(start, KEY_BLOCK), HEAD_DIM:] = value_term.astype(terms_ref.dtype)
        return c

    lax.fori_loop(0, kv_ref.shape[0] // KEY_BLOCK, body, 0)
    unstack_heads(dq_ref, (dq_sc[...] * scale).astype(dq_ref.dtype))


def vmem_specs(n):
    return [pl.BlockSpec(memory_space=pltpu.VMEM)] * n


def attention_fwd(q, kv, rpos, rlab, cpos, clab):
    stacked = rpos.shape[0]
    return pl.pallas_call(
        fwd_kernel,
        out_shape=(
            jax.ShapeDtypeStruct(q.shape, jnp.bfloat16),
            jax.ShapeDtypeStruct((stacked, 1), jnp.float32),
            jax.ShapeDtypeStruct((stacked, 1), jnp.float32),
        ),
        in_specs=vmem_specs(6),
        out_specs=tuple(vmem_specs(3)),
        scratch_shapes=[pltpu.VMEM((stacked, HEAD_DIM), jnp.float32)],
    )(q, kv, rpos, rlab, cpos, clab)


def attention_bwd(q, g, o, kv, rpos, rlab, cpos, clab, m, l):
    stacked = rpos.shape[0]
    return pl.pallas_call(
        bwd_kernel,
        out_shape=(
            jax.ShapeDtypeStruct(q.shape, jnp.bfloat16),
            jax.ShapeDtypeStruct(kv.shape, jnp.bfloat16),
        ),
        in_specs=vmem_specs(10),
        out_specs=tuple(vmem_specs(2)),
        scratch_shapes=[pltpu.VMEM((stacked, HEAD_DIM), jnp.float32)],
    )(q, g, o, kv, rpos, rlab, cpos, clab, m, l)


def fwd_step(queries, keys, values, visible, m_sc, l_sc, acc_sc):
    scale = 1.0 / math.sqrt(HEAD_DIM)
    scores = lax.dot_general(queries, keys, NT_DIMS, preferred_element_type=jnp.float32) * scale
    scores = jnp.where(visible, scores, -jnp.inf)
    running = m_sc[...]
    new_max = jnp.maximum(running, jnp.max(scores, axis=-1, keepdims=True))
    shift = jnp.where(new_max == -jnp.inf, 0.0, new_max)
    factor = jnp.exp(running - shift)
    weights = jnp.where(visible, jnp.exp(scores - shift), 0.0)
    l_sc[...] = l_sc[...] * factor + jnp.sum(weights, axis=-1, keepdims=True)
    acc_sc[...] = acc_sc[...] * factor + jnp.dot(
        weights.astype(jnp.bfloat16), values, preferred_element_type=jnp.float32)
    m_sc[...] = new_max


def column_visible(cpos_ref, clab_ref, block, rpos, rlab):
    cpos = cpos_ref[pl.ds(block, 1), :]
    clab = clab_ref[pl.ds(block, 1), :]
    return (cpos <= rpos) & ((clab == 0) | (clab == rlab))


def gather_fwd_kernel(n, kv_src, q_ref, rpos_ref, rlab_ref, cpos_ref, clab_ref,
                      kv_out, o_ref, m_ref, l_ref, acc_sc, send_sem, recv_sem):
    me = lax.axis_index("ctx")
    greet_all(n, me)

    def copy_to(peer):
        return pltpu.make_async_remote_copy(
            kv_src, kv_out.at[me], send_sem.at[peer], recv_sem.at[me],
            device_id={"ctx": peer}, device_id_type=MESH)

    def copy_from(src):
        return pltpu.make_async_remote_copy(
            kv_src, kv_out.at[src], send_sem.at[src], recv_sem.at[src],
            device_id={"ctx": src}, device_id_type=MESH)

    group = math.gcd(n, ARRIVAL_GROUP)
    window = min(max(SEND_WINDOW, group), n - 1)

    def send(i, c):
        copy_to(lax.rem(me + i, n)).start()
        return c

    lax.fori_loop(1, window + 1, send, 0)
    kv_out[me] = kv_src[...]
    queries = stack_heads(q_ref)
    rpos = rpos_ref[...]
    rlab = rlab_ref[...]
    m_ref[...] = jnp.full(m_ref.shape, -jnp.inf, jnp.float32)
    l_ref[...] = jnp.zeros(l_ref.shape, jnp.float32)
    acc_sc[...] = jnp.zeros(acc_sc.shape, jnp.float32)

    def arrive(j, c):
        blocks, cposs, clabs = [], [], []
        for t in range(group):
            i = j * group + t
            src = lax.rem(me + n - i, n)

            @pl.when(i > 0)
            def _():
                copy_from(src).wait_recv()

            blocks.append(kv_out[src])
            cposs.append(cpos_ref[pl.ds(src, 1), :])
            clabs.append(clab_ref[pl.ds(src, 1), :])
        block = jnp.concatenate(blocks, axis=0)
        cpos = jnp.concatenate(cposs, axis=1)
        clab = jnp.concatenate(clabs, axis=1)
        visible = (cpos <= rpos) & ((clab == 0) | (clab == rlab))
        fwd_step(queries, block[:, :HEAD_DIM], block[:, HEAD_DIM:], visible, m_ref, l_ref, acc_sc)
        for t in range(group):
            i = j * group + t

            @pl.when((i > 0) & (i + window <= n - 1))
            def _():
                copy_to(lax.rem(me + i, n)).wait_send()
                copy_to(lax.rem(me + i + window, n)).start()

        return c

    lax.fori_loop(0, n // group, arrive, 0)
    unstack_heads(o_ref, (acc_sc[...] / l_ref[...]).astype(o_ref.dtype))

    def drain(i, c):
        copy_to(lax.rem(me + i, n)).wait_send()
        return c

    lax.fori_loop(n - window, n, drain, 0)


def gather_fwd(kv_local, q, rpos, rlab, cpos, clab, n):
    rows, width = kv_local.shape
    stacked = rpos.shape[0]
    return pl.pallas_call(
        functools.partial(gather_fwd_kernel, n),
        out_shape=(
            jax.ShapeDtypeStruct((n, rows, width), kv_local.dtype),
            jax.ShapeDtypeStruct(q.shape, jnp.bfloat16),
            jax.ShapeDtypeStruct((stacked, 1), jnp.float32),
            jax.ShapeDtypeStruct((stacked, 1), jnp.float32),
        ),
        in_specs=vmem_specs(6),
        out_specs=tuple(vmem_specs(4)),
        scratch_shapes=[
            pltpu.VMEM((stacked, HEAD_DIM), jnp.float32),
            pltpu.SemaphoreType.DMA((n,)),
            pltpu.SemaphoreType.DMA((n,)),
        ],
        compiler_params=pltpu.CompilerParams(collective_id=0, has_side_effects=True),
    )(kv_local, q, rpos, rlab, cpos, clab)


def bwd_scatter_kernel(n, q_ref, g_ref, o_ref, kv_ref, rpos_ref, rlab_ref, cpos_ref, clab_ref,
                       m_ref, l_ref, dq_ref, red_ref, terms_sc, held, dq_sc, send_sem, recv_sem):
    me = lax.axis_index("ctx")
    greet_all(n, me)
    scale = 1.0 / math.sqrt(HEAD_DIM)
    queries = stack_heads(q_ref)
    grads = stack_heads(g_ref)
    outs = stack_heads(o_ref)
    delta = jnp.sum(grads.astype(jnp.float32) * outs.astype(jnp.float32), axis=-1, keepdims=True)
    rpos = rpos_ref[...]
    rlab = rlab_ref[...]
    row_max = m_ref[...]
    inv_total = 1.0 / l_ref[...]
    dq_sc[...] = jnp.zeros(dq_sc.shape, jnp.float32)

    def copy_to(peer):
        return pltpu.make_async_remote_copy(
            terms_sc.at[peer], held.at[me], send_sem.at[peer], recv_sem.at[me],
            device_id={"ctx": peer}, device_id_type=MESH)

    def copy_from(src):
        return pltpu.make_async_remote_copy(
            terms_sc.at[src], held.at[src], send_sem.at[src], recv_sem.at[src],
            device_id={"ctx": src}, device_id_type=MESH)

    def block_terms(p):
        block = kv_ref[p]
        keys = block[:, :HEAD_DIM]
        values = block[:, HEAD_DIM:]
        visible = column_visible(cpos_ref, clab_ref, p, rpos, rlab)
        scores = lax.dot_general(queries, keys, NT_DIMS, preferred_element_type=jnp.float32) * scale
        probs = jnp.where(visible, jnp.exp(scores - row_max), 0.0) * inv_total
        dprob = lax.dot_general(grads, values, NT_DIMS, preferred_element_type=jnp.float32)
        dscore_b = (probs * (dprob - delta)).astype(jnp.bfloat16)
        probs_b = probs.astype(jnp.bfloat16)
        dq_sc[...] += jnp.dot(dscore_b, keys, preferred_element_type=jnp.float32)
        key_term = lax.dot_general(dscore_b, queries, TN_DIMS, preferred_element_type=jnp.float32) * scale
        value_term = lax.dot_general(probs_b, grads, TN_DIMS, preferred_element_type=jnp.float32)
        return jnp.concatenate([key_term, value_term], axis=1)

    red_ref[...] = block_terms(me)

    def step(i, c):
        peer = lax.rem(me + i, n)
        terms_sc[peer] = block_terms(peer).astype(terms_sc.dtype)

        @pl.when(i >= 2)
        def _():
            copy_to(lax.rem(me + i - 1, n)).start()

        return c

    lax.fori_loop(1, n, step, 0)
    copy_to(lax.rem(me + n - 1, n)).start()
    unstack_heads(dq_ref, (dq_sc[...] * scale).astype(dq_ref.dtype))

    def arrive(i, c):
        src = lax.rem(me + n - i, n)
        copy_from(src).wait_recv()
        red_ref[...] += held[src].astype(jnp.float32)
        return c

    lax.fori_loop(1, n, arrive, 0)

    def drain(i, c):
        copy_to(lax.rem(me + i, n)).wait_send()
        return c

    lax.fori_loop(1, n, drain, 0)


def bwd_scatter(q, g, o, kv, rpos, rlab, cpos, clab, m, l, n):
    _, rows, width = kv.shape
    stacked = rpos.shape[0]
    return pl.pallas_call(
        functools.partial(bwd_scatter_kernel, n),
        out_shape=(
            jax.ShapeDtypeStruct(q.shape, jnp.bfloat16),
            jax.ShapeDtypeStruct((rows, width), jnp.float32),
        ),
        in_specs=vmem_specs(10),
        out_specs=tuple(vmem_specs(2)),
        scratch_shapes=[
            pltpu.VMEM(kv.shape, jnp.bfloat16),
            pltpu.VMEM(kv.shape, jnp.bfloat16),
            pltpu.VMEM((stacked, HEAD_DIM), jnp.float32),
            pltpu.SemaphoreType.DMA((n,)),
            pltpu.SemaphoreType.DMA((n,)),
        ],
        compiler_params=pltpu.CompilerParams(collective_id=1, has_side_effects=True),
    )(q, g, o, kv, rpos, rlab, cpos, clab, m, l)


def on_device(query_rows, key_rows, value_rows, out_grad, segment_ids, span_order):
    ctx_size = lax.axis_size("ctx")
    ctx_index = lax.axis_index("ctx")
    local_rows = query_rows.shape[0]
    heads_here = query_rows.shape[1] // HEAD_DIM
    total_rows = local_rows * ctx_size
    offsets = jnp.arange(SPAN, dtype=jnp.int32)
    positions = (SPAN * span_order[:, None] + offsets[None, :]).reshape(total_rows)
    prompt_end = jnp.sum((segment_ids == 0).astype(jnp.int32))
    chosen_end = jnp.sum((segment_ids <= 1).astype(jnp.int32))
    labels = (positions >= prompt_end).astype(jnp.int32) + (positions >= chosen_end).astype(jnp.int32)
    own_pos = lax.dynamic_slice_in_dim(positions, ctx_index * local_rows, local_rows, 0)
    own_label = lax.dynamic_slice_in_dim(labels, ctx_index * local_rows, local_rows, 0)
    rpos = jnp.tile(own_pos, heads_here)[:, None]
    rlab = jnp.tile(own_label, heads_here)[:, None]
    cpos = positions.reshape(ctx_size, local_rows)
    clab = labels.reshape(ctx_size, local_rows)
    kv_local = jnp.concatenate([key_rows, value_rows], axis=1)
    kv_all, attn_local, row_max, total = gather_fwd(
        kv_local, query_rows, rpos, rlab, cpos, clab, ctx_size)
    grad_rows = fetch_grad(out_grad)
    query_grad, reduced = bwd_scatter(
        query_rows, grad_rows, attn_local, kv_all, rpos, rlab, cpos, clab, row_max, total, ctx_size)
    key_grad = reduced[:, :HEAD_DIM].astype(jnp.bfloat16)
    value_grad = reduced[:, HEAD_DIM:].astype(jnp.bfloat16)
    attn_spread = spread_output(attn_local)
    return (attn_spread, query_grad, key_grad, value_grad)


def solution(mesh):
    placed = (P("ctx", "tp"), P("ctx", "tp"), P("ctx", "tp"), P(("ctx", "tp"), None), P(), P())
    return jax.shard_map(
        on_device,
        mesh=mesh,
        in_specs=placed,
        out_specs=(P(("ctx", "tp"), None), P("ctx", "tp"), P("ctx", "tp"), P("ctx", "tp")),
        check_vma=False,
    )
```

```python
import functools
import math

import jax
import jax.numpy as jnp
from jax import lax
from jax.experimental import pallas as pl
from jax.experimental.pallas import tpu as pltpu
from jax.sharding import PartitionSpec as P

HEAD_DIM = 128
SPAN = 64
MESH = pl.DeviceIdType.MESH


def greet_all(n, me):
    barrier = pltpu.get_barrier_semaphore()

    def greet(i, c):
        peer = lax.rem(me + i, n)
        pl.semaphore_signal(barrier, inc=1, device_id={"ctx": peer}, device_id_type=MESH)
        return c

    lax.fori_loop(1, n, greet, 0)
    pl.semaphore_wait(barrier, n - 1)


def gather_kernel(n, src_ref, out_ref, send_sem, recv_sem):
    me = lax.axis_index("ctx")
    greet_all(n, me)

    def copy_to(peer):
        return pltpu.make_async_remote_copy(
            src_ref, out_ref.at[me], send_sem.at[peer], recv_sem.at[me],
            device_id={"ctx": peer}, device_id_type=MESH)

    def copy_from(src):
        return pltpu.make_async_remote_copy(
            src_ref, out_ref.at[src], send_sem.at[src], recv_sem.at[src],
            device_id={"ctx": src}, device_id_type=MESH)

    def send(i, c):
        copy_to(lax.rem(me + i, n)).start()
        return c

    lax.fori_loop(1, n, send, 0)
    out_ref[me] = src_ref[...]

    def wait(i, c):
        copy_to(lax.rem(me + i, n)).wait_send()
        copy_from(lax.rem(me + n - i, n)).wait_recv()
        return c

    lax.fori_loop(1, n, wait, 0)


def ctx_gather(block, n):
    rows, width = block.shape
    return pl.pallas_call(
        functools.partial(gather_kernel, n),
        out_shape=jax.ShapeDtypeStruct((n, rows, width), block.dtype),
        in_specs=[pl.BlockSpec(memory_space=pltpu.VMEM)],
        out_specs=pl.BlockSpec(memory_space=pltpu.VMEM),
        scratch_shapes=[pltpu.SemaphoreType.DMA((n,)), pltpu.SemaphoreType.DMA((n,))],
        compiler_params=pltpu.CompilerParams(collective_id=0, has_side_effects=True),
    )(block)


def fetch_grad(out_grad):
    return lax.all_to_all(out_grad, "tp", split_axis=1, concat_axis=0, tiled=True)


def spread_output(attn_flat):
    return lax.all_to_all(attn_flat, "tp", split_axis=0, concat_axis=1, tiled=True)


KEY_BLOCK = 512
NT_DIMS = (((1,), (1,)), ((), ()))
TN_DIMS = (((0,), (0,)), ((), ()))


def stack_heads(ref):
    heads = ref.shape[1] // HEAD_DIM
    return jnp.concatenate([ref[:, h * HEAD_DIM:(h + 1) * HEAD_DIM] for h in range(heads)], axis=0)


def unstack_heads(ref, value):
    rows = ref.shape[0]
    for h in range(ref.shape[1] // HEAD_DIM):
        ref[:, h * HEAD_DIM:(h + 1) * HEAD_DIM] = value[h * rows:(h + 1) * rows]


def key_block(kv_ref, cpos_ref, clab_ref, rpos, rlab, kb):
    start = pl.multiple_of(kb * KEY_BLOCK, KEY_BLOCK)
    keys = kv_ref[pl.ds(start, KEY_BLOCK), :HEAD_DIM]
    values = kv_ref[pl.ds(start, KEY_BLOCK), HEAD_DIM:]
    cpos = cpos_ref[:, pl.ds(start, KEY_BLOCK)]
    clab = clab_ref[:, pl.ds(start, KEY_BLOCK)]
    visible = (cpos <= rpos) & ((clab == 0) | (clab == rlab))
    return start, keys, values, visible


def fwd_kernel(q_ref, kv_ref, rpos_ref, rlab_ref, cpos_ref, clab_ref, o_ref, m_ref, l_ref, acc_sc):
    scale = 1.0 / math.sqrt(HEAD_DIM)
    queries = stack_heads(q_ref)
    rpos = rpos_ref[...]
    rlab = rlab_ref[...]
    m_ref[...] = jnp.full(m_ref.shape, -jnp.inf, jnp.float32)
    l_ref[...] = jnp.zeros(l_ref.shape, jnp.float32)
    acc_sc[...] = jnp.zeros(acc_sc.shape, jnp.float32)

    def body(kb, c):
        _, keys, values, visible = key_block(kv_ref, cpos_ref, clab_ref, rpos, rlab, kb)
        scores = lax.dot_general(queries, keys, NT_DIMS, preferred_element_type=jnp.float32) * scale
        scores = jnp.where(visible, scores, -jnp.inf)
        running = m_ref[...]
        new_max = jnp.maximum(running, jnp.max(scores, axis=-1, keepdims=True))
        shift = jnp.where(new_max == -jnp.inf, 0.0, new_max)
        factor = jnp.exp(running - shift)
        weights = jnp.where(visible, jnp.exp(scores - shift), 0.0)
        l_ref[...] = l_ref[...] * factor + jnp.sum(weights, axis=-1, keepdims=True)
        acc_sc[...] = acc_sc[...] * factor + jnp.dot(
            weights.astype(jnp.bfloat16), values, preferred_element_type=jnp.float32)
        m_ref[...] = new_max
        return c

    lax.fori_loop(0, kv_ref.shape[0] // KEY_BLOCK, body, 0)
    unstack_heads(o_ref, (acc_sc[...] / l_ref[...]).astype(o_ref.dtype))


def vmem_specs(n):
    return [pl.BlockSpec(memory_space=pltpu.VMEM)] * n


def attention_fwd(q, kv, rpos, rlab, cpos, clab):
    stacked = rpos.shape[0]
    return pl.pallas_call(
        fwd_kernel,
        out_shape=(
            jax.ShapeDtypeStruct(q.shape, jnp.bfloat16),
            jax.ShapeDtypeStruct((stacked, 1), jnp.float32),
            jax.ShapeDtypeStruct((stacked, 1), jnp.float32),
        ),
        in_specs=vmem_specs(6),
        out_specs=tuple(vmem_specs(3)),
        scratch_shapes=[pltpu.VMEM((stacked, HEAD_DIM), jnp.float32)],
    )(q, kv, rpos, rlab, cpos, clab)


def fwd_step(queries, keys, values, visible, m_sc, l_sc, acc_sc):
    scale = 1.0 / math.sqrt(HEAD_DIM)
    scores = lax.dot_general(queries, keys, NT_DIMS, preferred_element_type=jnp.float32) * scale
    scores = jnp.where(visible, scores, -jnp.inf)
    running = m_sc[...]
    new_max = jnp.maximum(running, jnp.max(scores, axis=-1, keepdims=True))
    shift = jnp.where(new_max == -jnp.inf, 0.0, new_max)
    factor = jnp.exp(running - shift)
    weights = jnp.where(visible, jnp.exp(scores - shift), 0.0)
    l_sc[...] = l_sc[...] * factor + jnp.sum(weights, axis=-1, keepdims=True)
    acc_sc[...] = acc_sc[...] * factor + jnp.dot(
        weights.astype(jnp.bfloat16), values, preferred_element_type=jnp.float32)
    m_sc[...] = new_max


def column_visible(cpos_ref, clab_ref, block, rpos, rlab):
    cpos = cpos_ref[pl.ds(block, 1), :]
    clab = clab_ref[pl.ds(block, 1), :]
    return (cpos <= rpos) & ((clab == 0) | (clab == rlab))


def bwd_scatter_kernel(n, q_ref, g_ref, o_ref, kv_ref, rpos_ref, rlab_ref, cpos_ref, clab_ref,
                       m_ref, l_ref, dq_ref, red_ref, terms_sc, held, dq_sc, send_sem, recv_sem):
    me = lax.axis_index("ctx")
    greet_all(n, me)
    scale = 1.0 / math.sqrt(HEAD_DIM)
    queries = stack_heads(q_ref)
    grads = stack_heads(g_ref)
    outs = stack_heads(o_ref)
    delta = jnp.sum(grads.astype(jnp.float32) * outs.astype(jnp.float32), axis=-1, keepdims=True)
    rpos = rpos_ref[...]
    rlab = rlab_ref[...]
    row_max = m_ref[...]
    inv_total = 1.0 / l_ref[...]
    dq_sc[...] = jnp.zeros(dq_sc.shape, jnp.float32)

    def copy_to(peer):
        return pltpu.make_async_remote_copy(
            terms_sc.at[peer], held.at[me], send_sem.at[peer], recv_sem.at[me],
            device_id={"ctx": peer}, device_id_type=MESH)

    def copy_from(src):
        return pltpu.make_async_remote_copy(
            terms_sc.at[src], held.at[src], send_sem.at[src], recv_sem.at[src],
            device_id={"ctx": src}, device_id_type=MESH)

    def block_terms(p):
        block = kv_ref[p]
        keys = block[:, :HEAD_DIM]
        values = block[:, HEAD_DIM:]
        visible = column_visible(cpos_ref, clab_ref, p, rpos, rlab)
        scores = lax.dot_general(queries, keys, NT_DIMS, preferred_element_type=jnp.float32) * scale
        probs = jnp.where(visible, jnp.exp(scores - row_max), 0.0) * inv_total
        dprob = lax.dot_general(grads, values, NT_DIMS, preferred_element_type=jnp.float32)
        dscore_b = (probs * (dprob - delta)).astype(jnp.bfloat16)
        probs_b = probs.astype(jnp.bfloat16)
        dq_sc[...] += jnp.dot(dscore_b, keys, preferred_element_type=jnp.float32)
        key_term = lax.dot_general(dscore_b, queries, TN_DIMS, preferred_element_type=jnp.float32) * scale
        value_term = lax.dot_general(probs_b, grads, TN_DIMS, preferred_element_type=jnp.float32)
        return jnp.concatenate([key_term, value_term], axis=1)

    red_ref[...] = block_terms(me)

    def step(i, c):
        peer = lax.rem(me + i, n)
        terms_sc[peer] = block_terms(peer).astype(terms_sc.dtype)

        @pl.when(i >= 2)
        def _():
            copy_to(lax.rem(me + i - 1, n)).start()

        return c

    lax.fori_loop(1, n, step, 0)
    copy_to(lax.rem(me + n - 1, n)).start()
    unstack_heads(dq_ref, (dq_sc[...] * scale).astype(dq_ref.dtype))

    def arrive(i, c):
        src = lax.rem(me + n - i, n)
        copy_from(src).wait_recv()
        red_ref[...] += held[src].astype(jnp.float32)
        return c

    lax.fori_loop(1, n, arrive, 0)

    def drain(i, c):
        copy_to(lax.rem(me + i, n)).wait_send()
        return c

    lax.fori_loop(1, n, drain, 0)


def bwd_scatter(q, g, o, kv, rpos, rlab, cpos, clab, m, l, n):
    _, rows, width = kv.shape
    stacked = rpos.shape[0]
    return pl.pallas_call(
        functools.partial(bwd_scatter_kernel, n),
        out_shape=(
            jax.ShapeDtypeStruct(q.shape, jnp.bfloat16),
            jax.ShapeDtypeStruct((rows, width), jnp.float32),
        ),
        in_specs=vmem_specs(10),
        out_specs=tuple(vmem_specs(2)),
        scratch_shapes=[
            pltpu.VMEM(kv.shape, jnp.bfloat16),
            pltpu.VMEM(kv.shape, jnp.bfloat16),
            pltpu.VMEM((stacked, HEAD_DIM), jnp.float32),
            pltpu.SemaphoreType.DMA((n,)),
            pltpu.SemaphoreType.DMA((n,)),
        ],
        compiler_params=pltpu.CompilerParams(collective_id=1, has_side_effects=True),
    )(q, g, o, kv, rpos, rlab, cpos, clab, m, l)


def on_device(query_rows, key_rows, value_rows, out_grad, segment_ids, span_order):
    ctx_size = lax.axis_size("ctx")
    ctx_index = lax.axis_index("ctx")
    local_rows = query_rows.shape[0]
    heads_here = query_rows.shape[1] // HEAD_DIM
    total_rows = local_rows * ctx_size
    offsets = jnp.arange(SPAN, dtype=jnp.int32)
    positions = (SPAN * span_order[:, None] + offsets[None, :]).reshape(total_rows)
    prompt_end = jnp.sum((segment_ids == 0).astype(jnp.int32))
    chosen_end = jnp.sum((segment_ids <= 1).astype(jnp.int32))
    labels = (positions >= prompt_end).astype(jnp.int32) + (positions >= chosen_end).astype(jnp.int32)
    own_pos = lax.dynamic_slice_in_dim(positions, ctx_index * local_rows, local_rows, 0)
    own_label = lax.dynamic_slice_in_dim(labels, ctx_index * local_rows, local_rows, 0)
    rpos = jnp.tile(own_pos, heads_here)[:, None]
    rlab = jnp.tile(own_label, heads_here)[:, None]
    cpos = positions.reshape(ctx_size, local_rows)
    clab = labels.reshape(ctx_size, local_rows)
    kv_local = jnp.concatenate([key_rows, value_rows], axis=1)
    kv_all = ctx_gather(kv_local, ctx_size)
    attn_local, row_max, total = attention_fwd(
        query_rows, kv_all.reshape(total_rows, kv_all.shape[2]), rpos, rlab,
        positions[None, :], labels[None, :])
    grad_rows = fetch_grad(out_grad)
    query_grad, reduced = bwd_scatter(
        query_rows, grad_rows, attn_local, kv_all, rpos, rlab, cpos, clab, row_max, total, ctx_size)
    key_grad = reduced[:, :HEAD_DIM].astype(jnp.bfloat16)
    value_grad = reduced[:, HEAD_DIM:].astype(jnp.bfloat16)
    attn_spread = spread_output(attn_local)
    return (attn_spread, query_grad, key_grad, value_grad)


def solution(mesh):
    placed = (P("ctx", "tp"), P("ctx", "tp"), P("ctx", "tp"), P(("ctx", "tp"), None), P(), P())
    return jax.shard_map(
        on_device,
        mesh=mesh,
        in_specs=placed,
        out_specs=(P(("ctx", "tp"), None), P("ctx", "tp"), P("ctx", "tp"), P("ctx", "tp")),
        check_vma=False,
    )
```

```python
import functools
import math

import jax
import jax.numpy as jnp
from jax import lax
from jax.experimental import pallas as pl
from jax.experimental.pallas import tpu as pltpu
from jax.sharding import PartitionSpec as P

HEAD_DIM = 128
SPAN = 64
MESH = pl.DeviceIdType.MESH


def greet_all(n, me, t=1, mt=None):
    barrier = pltpu.get_barrier_semaphore()

    def greet(i, c):
        peer = lax.rem(me + i, n)
        pl.semaphore_signal(barrier, inc=1, device_id={"ctx": peer}, device_id_type=MESH)
        return c

    def greet_tp(i, c):
        peer = lax.rem(mt + i, t)
        pl.semaphore_signal(barrier, inc=1, device_id={"tp": peer}, device_id_type=MESH)
        return c

    lax.fori_loop(1, n, greet, 0)
    if t > 1:
        lax.fori_loop(1, t, greet_tp, 0)
    pl.semaphore_wait(barrier, n - 1 + t - 1)


def tp_exchange(t, mt, src_of, dst_of, send_sem, recv_sem):
    def copy_to(peer):
        return pltpu.make_async_remote_copy(
            src_of(peer), dst_of(mt), send_sem.at[peer], recv_sem.at[mt],
            device_id={"tp": peer}, device_id_type=MESH)

    def copy_from(src):
        return pltpu.make_async_remote_copy(
            src_of(mt), dst_of(src), send_sem.at[src], recv_sem.at[src],
            device_id={"tp": src}, device_id_type=MESH)

    def start():
        def send(i, c):
            copy_to(lax.rem(mt + i, t)).start()
            return c

        lax.fori_loop(1, t, send, 0)

    def finish():
        def wait(i, c):
            copy_to(lax.rem(mt + i, t)).wait_send()
            copy_from(lax.rem(mt + t - i, t)).wait_recv()
            return c

        lax.fori_loop(1, t, wait, 0)

    return start, finish


def gather_kernel(n, t, src_ref, og_ref, out_ref, grad_ref, send_sem, recv_sem, gsend_sem, grecv_sem):
    me = lax.axis_index("ctx")
    mt = lax.axis_index("tp")
    greet_all(n, me, t, mt)
    rows = og_ref.shape[0]
    cols = grad_ref.shape[1]

    def grad_src(p):
        return og_ref.at[:, pl.ds(pl.multiple_of(p * cols, cols), cols)]

    def grad_dst(p):
        return grad_ref.at[pl.ds(pl.multiple_of(p * rows, rows), rows), :]

    grad_start, grad_finish = tp_exchange(t, mt, grad_src, grad_dst, gsend_sem, grecv_sem)
    grad_start()

    def copy_to(peer):
        return pltpu.make_async_remote_copy(
            src_ref, out_ref.at[me], send_sem.at[peer], recv_sem.at[me],
            device_id={"ctx": peer}, device_id_type=MESH)

    def copy_from(src):
        return pltpu.make_async_remote_copy(
            src_ref, out_ref.at[src], send_sem.at[src], recv_sem.at[src],
            device_id={"ctx": src}, device_id_type=MESH)

    def send(i, c):
        copy_to(lax.rem(me + i, n)).start()
        return c

    lax.fori_loop(1, n, send, 0)
    out_ref[me] = src_ref[...]
    grad_ref[pl.ds(pl.multiple_of(mt * rows, rows), rows), :] = og_ref[
        :, pl.ds(pl.multiple_of(mt * cols, cols), cols)]

    def wait(i, c):
        copy_to(lax.rem(me + i, n)).wait_send()
        copy_from(lax.rem(me + n - i, n)).wait_recv()
        return c

    lax.fori_loop(1, n, wait, 0)
    grad_finish()


def ctx_gather(block, out_grad, n, t):
    rows, width = block.shape
    grad_shape = (out_grad.shape[0] * t, out_grad.shape[1] // t)
    return pl.pallas_call(
        functools.partial(gather_kernel, n, t),
        out_shape=(
            jax.ShapeDtypeStruct((n, rows, width), block.dtype),
            jax.ShapeDtypeStruct(grad_shape, out_grad.dtype),
        ),
        in_specs=[pl.BlockSpec(memory_space=pltpu.VMEM)] * 2,
        out_specs=(pl.BlockSpec(memory_space=pltpu.VMEM),) * 2,
        scratch_shapes=[pltpu.SemaphoreType.DMA((n,)), pltpu.SemaphoreType.DMA((n,)),
                        pltpu.SemaphoreType.DMA((t,)), pltpu.SemaphoreType.DMA((t,))],
        compiler_params=pltpu.CompilerParams(collective_id=0, has_side_effects=True),
    )(block, out_grad)


KEY_BLOCK = 512
NT_DIMS = (((1,), (1,)), ((), ()))
TN_DIMS = (((0,), (0,)), ((), ()))


def stack_heads(ref):
    heads = ref.shape[1] // HEAD_DIM
    return jnp.concatenate([ref[:, h * HEAD_DIM:(h + 1) * HEAD_DIM] for h in range(heads)], axis=0)


def unstack_heads(ref, value):
    rows = ref.shape[0]
    for h in range(ref.shape[1] // HEAD_DIM):
        ref[:, h * HEAD_DIM:(h + 1) * HEAD_DIM] = value[h * rows:(h + 1) * rows]


def key_block(kv_ref, cpos_ref, clab_ref, rpos, rlab, kb):
    start = pl.multiple_of(kb * KEY_BLOCK, KEY_BLOCK)
    keys = kv_ref[pl.ds(start, KEY_BLOCK), :HEAD_DIM]
    values = kv_ref[pl.ds(start, KEY_BLOCK), HEAD_DIM:]
    cpos = cpos_ref[:, pl.ds(start, KEY_BLOCK)]
    clab = clab_ref[:, pl.ds(start, KEY_BLOCK)]
    visible = (cpos <= rpos) & ((clab == 0) | (clab == rlab))
    return start, keys, values, visible


def fwd_kernel(q_ref, kv_ref, rpos_ref, rlab_ref, cpos_ref, clab_ref, o_ref, m_ref, l_ref, acc_sc):
    scale = 1.0 / math.sqrt(HEAD_DIM)
    queries = stack_heads(q_ref)
    rpos = rpos_ref[...]
    rlab = rlab_ref[...]
    m_ref[...] = jnp.full(m_ref.shape, -jnp.inf, jnp.float32)
    l_ref[...] = jnp.zeros(l_ref.shape, jnp.float32)
    acc_sc[...] = jnp.zeros(acc_sc.shape, jnp.float32)

    def body(kb, c):
        _, keys, values, visible = key_block(kv_ref, cpos_ref, clab_ref, rpos, rlab, kb)
        scores = lax.dot_general(queries, keys, NT_DIMS, preferred_element_type=jnp.float32) * scale
        scores = jnp.where(visible, scores, -jnp.inf)
        running = m_ref[...]
        new_max = jnp.maximum(running, jnp.max(scores, axis=-1, keepdims=True))
        shift = jnp.where(new_max == -jnp.inf, 0.0, new_max)
        factor = jnp.exp(running - shift)
        weights = jnp.where(visible, jnp.exp(scores - shift), 0.0)
        l_ref[...] = l_ref[...] * factor + jnp.sum(weights, axis=-1, keepdims=True)
        acc_sc[...] = acc_sc[...] * factor + jnp.dot(
            weights.astype(jnp.bfloat16), values, preferred_element_type=jnp.float32)
        m_ref[...] = new_max
        return c

    lax.fori_loop(0, kv_ref.shape[0] // KEY_BLOCK, body, 0)
    unstack_heads(o_ref, (acc_sc[...] / l_ref[...]).astype(o_ref.dtype))


def vmem_specs(n):
    return [pl.BlockSpec(memory_space=pltpu.VMEM)] * n


def attention_fwd(q, kv, rpos, rlab, cpos, clab):
    stacked = rpos.shape[0]
    return pl.pallas_call(
        fwd_kernel,
        out_shape=(
            jax.ShapeDtypeStruct(q.shape, jnp.bfloat16),
            jax.ShapeDtypeStruct((stacked, 1), jnp.float32),
            jax.ShapeDtypeStruct((stacked, 1), jnp.float32),
        ),
        in_specs=vmem_specs(6),
        out_specs=tuple(vmem_specs(3)),
        scratch_shapes=[pltpu.VMEM((stacked, HEAD_DIM), jnp.float32)],
    )(q, kv, rpos, rlab, cpos, clab)


def column_visible(cpos_ref, clab_ref, block, rpos, rlab):
    cpos = cpos_ref[pl.ds(block, 1), :]
    clab = clab_ref[pl.ds(block, 1), :]
    return (cpos <= rpos) & ((clab == 0) | (clab == rlab))


def bwd_scatter_kernel(n, t, q_ref, g_ref, o_ref, kv_ref, rpos_ref, rlab_ref, cpos_ref, clab_ref,
                       m_ref, l_ref, dq_ref, red_ref, spread_ref, terms_sc, held, dq_sc, send_sem, recv_sem,
                       osend_sem, orecv_sem):
    me = lax.axis_index("ctx")
    mt = lax.axis_index("tp")
    greet_all(n, me, t, mt)
    rows = spread_ref.shape[0]
    cols = o_ref.shape[1]

    def out_src(p):
        return o_ref.at[pl.ds(pl.multiple_of(p * rows, rows), rows), :]

    def out_dst(p):
        return spread_ref.at[:, pl.ds(pl.multiple_of(p * cols, cols), cols)]

    out_start, out_finish = tp_exchange(t, mt, out_src, out_dst, osend_sem, orecv_sem)
    out_start()
    spread_ref[:, pl.ds(pl.multiple_of(mt * cols, cols), cols)] = o_ref[
        pl.ds(pl.multiple_of(mt * rows, rows), rows), :]
    scale = 1.0 / math.sqrt(HEAD_DIM)
    queries = stack_heads(q_ref)
    grads = stack_heads(g_ref)
    outs = stack_heads(o_ref)
    delta = jnp.sum(grads.astype(jnp.float32) * outs.astype(jnp.float32), axis=-1, keepdims=True)
    rpos = rpos_ref[...]
    rlab = rlab_ref[...]
    row_max = m_ref[...]
    inv_total = 1.0 / l_ref[...]
    dq_sc[...] = jnp.zeros(dq_sc.shape, jnp.float32)

    def copy_to(peer):
        return pltpu.make_async_remote_copy(
            terms_sc.at[peer], held.at[me], send_sem.at[peer], recv_sem.at[me],
            device_id={"ctx": peer}, device_id_type=MESH)

    def copy_from(src):
        return pltpu.make_async_remote_copy(
            terms_sc.at[src], held.at[src], send_sem.at[src], recv_sem.at[src],
            device_id={"ctx": src}, device_id_type=MESH)

    def block_terms(p):
        block = kv_ref[p]
        keys = block[:, :HEAD_DIM]
        values = block[:, HEAD_DIM:]
        visible = column_visible(cpos_ref, clab_ref, p, rpos, rlab)
        scores = lax.dot_general(queries, keys, NT_DIMS, preferred_element_type=jnp.float32) * scale
        probs = jnp.where(visible, jnp.exp(scores - row_max), 0.0) * inv_total
        dprob = lax.dot_general(grads, values, NT_DIMS, preferred_element_type=jnp.float32)
        dscore_b = (probs * (dprob - delta)).astype(jnp.bfloat16)
        probs_b = probs.astype(jnp.bfloat16)
        dq_sc[...] += jnp.dot(dscore_b, keys, preferred_element_type=jnp.float32)
        key_term = lax.dot_general(dscore_b, queries, TN_DIMS, preferred_element_type=jnp.float32) * scale
        value_term = lax.dot_general(probs_b, grads, TN_DIMS, preferred_element_type=jnp.float32)
        return jnp.concatenate([key_term, value_term], axis=1)

    red_ref[...] = block_terms(me)

    def step(i, c):
        peer = lax.rem(me + i, n)
        terms_sc[peer] = block_terms(peer).astype(terms_sc.dtype)

        @pl.when(i >= 2)
        def _():
            copy_to(lax.rem(me + i - 1, n)).start()

        return c

    lax.fori_loop(1, n, step, 0)
    copy_to(lax.rem(me + n - 1, n)).start()
    unstack_heads(dq_ref, (dq_sc[...] * scale).astype(dq_ref.dtype))

    def arrive(i, c):
        src = lax.rem(me + n - i, n)
        copy_from(src).wait_recv()
        red_ref[...] += held[src].astype(jnp.float32)
        return c

    lax.fori_loop(1, n, arrive, 0)

    def drain(i, c):
        copy_to(lax.rem(me + i, n)).wait_send()
        return c

    lax.fori_loop(1, n, drain, 0)
    out_finish()


def bwd_scatter(q, g, o, kv, rpos, rlab, cpos, clab, m, l, n, t):
    _, rows, width = kv.shape
    stacked = rpos.shape[0]
    return pl.pallas_call(
        functools.partial(bwd_scatter_kernel, n, t),
        out_shape=(
            jax.ShapeDtypeStruct(q.shape, jnp.bfloat16),
            jax.ShapeDtypeStruct((rows, width), jnp.float32),
            jax.ShapeDtypeStruct((o.shape[0] // t, o.shape[1] * t), o.dtype),
        ),
        in_specs=vmem_specs(10),
        out_specs=tuple(vmem_specs(3)),
        scratch_shapes=[
            pltpu.VMEM(kv.shape, jnp.bfloat16),
            pltpu.VMEM(kv.shape, jnp.bfloat16),
            pltpu.VMEM((stacked, HEAD_DIM), jnp.float32),
            pltpu.SemaphoreType.DMA((n,)),
            pltpu.SemaphoreType.DMA((n,)),
            pltpu.SemaphoreType.DMA((t,)),
            pltpu.SemaphoreType.DMA((t,)),
        ],
        compiler_params=pltpu.CompilerParams(collective_id=1, has_side_effects=True),
    )(q, g, o, kv, rpos, rlab, cpos, clab, m, l)


def on_device(query_rows, key_rows, value_rows, out_grad, segment_ids, span_order):
    ctx_size = lax.axis_size("ctx")
    ctx_index = lax.axis_index("ctx")
    local_rows = query_rows.shape[0]
    heads_here = query_rows.shape[1] // HEAD_DIM
    total_rows = local_rows * ctx_size
    offsets = jnp.arange(SPAN, dtype=jnp.int32)
    positions = (SPAN * span_order[:, None] + offsets[None, :]).reshape(total_rows)
    prompt_end = jnp.sum((segment_ids == 0).astype(jnp.int32))
    chosen_end = jnp.sum((segment_ids <= 1).astype(jnp.int32))
    labels = (positions >= prompt_end).astype(jnp.int32) + (positions >= chosen_end).astype(jnp.int32)
    own_pos = lax.dynamic_slice_in_dim(positions, ctx_index * local_rows, local_rows, 0)
    own_label = lax.dynamic_slice_in_dim(labels, ctx_index * local_rows, local_rows, 0)
    rpos = jnp.tile(own_pos, heads_here)[:, None]
    rlab = jnp.tile(own_label, heads_here)[:, None]
    cpos = positions.reshape(ctx_size, local_rows)
    clab = labels.reshape(ctx_size, local_rows)
    kv_local = jnp.concatenate([key_rows, value_rows], axis=1)
    tp_size = lax.axis_size("tp")
    kv_all, grad_rows = ctx_gather(kv_local, out_grad, ctx_size, tp_size)
    attn_local, row_max, total = attention_fwd(
        query_rows, kv_all.reshape(total_rows, kv_all.shape[2]), rpos, rlab,
        positions[None, :], labels[None, :])
    query_grad, reduced, attn_spread = bwd_scatter(
        query_rows, grad_rows, attn_local, kv_all, rpos, rlab, cpos, clab, row_max, total,
        ctx_size, tp_size)
    key_grad = reduced[:, :HEAD_DIM].astype(jnp.bfloat16)
    value_grad = reduced[:, HEAD_DIM:].astype(jnp.bfloat16)
    return (attn_spread, query_grad, key_grad, value_grad)


def solution(mesh):
    placed = (P("ctx", "tp"), P("ctx", "tp"), P("ctx", "tp"), P(("ctx", "tp"), None), P(), P())
    return jax.shard_map(
        on_device,
        mesh=mesh,
        in_specs=placed,
        out_specs=(P(("ctx", "tp"), None), P("ctx", "tp"), P("ctx", "tp"), P("ctx", "tp")),
        check_vma=False,
    )
```

```python
import functools
import math

import jax
import jax.numpy as jnp
from jax import lax
from jax.experimental import pallas as pl
from jax.experimental.pallas import tpu as pltpu
from jax.sharding import PartitionSpec as P

HEAD_DIM = 128
SPAN = 64
MESH = pl.DeviceIdType.MESH


def greet_all(n, me, t=1, mt=None):
    barrier = pltpu.get_barrier_semaphore()

    def greet(i, c):
        peer = lax.rem(me + i, n)
        pl.semaphore_signal(barrier, inc=1, device_id={"ctx": peer}, device_id_type=MESH)
        return c

    def greet_tp(i, c):
        peer = lax.rem(mt + i, t)
        pl.semaphore_signal(barrier, inc=1, device_id={"tp": peer}, device_id_type=MESH)
        return c

    lax.fori_loop(1, n, greet, 0)
    if t > 1:
        lax.fori_loop(1, t, greet_tp, 0)
    pl.semaphore_wait(barrier, n - 1 + t - 1)


def tp_exchange(t, mt, src_of, dst_of, send_sem, recv_sem):
    def copy_to(peer):
        return pltpu.make_async_remote_copy(
            src_of(peer), dst_of(mt), send_sem.at[peer], recv_sem.at[mt],
            device_id={"tp": peer}, device_id_type=MESH)

    def copy_from(src):
        return pltpu.make_async_remote_copy(
            src_of(mt), dst_of(src), send_sem.at[src], recv_sem.at[src],
            device_id={"tp": src}, device_id_type=MESH)

    def start():
        def send(i, c):
            copy_to(lax.rem(mt + i, t)).start()
            return c

        lax.fori_loop(1, t, send, 0)

    def finish():
        def wait(i, c):
            copy_to(lax.rem(mt + i, t)).wait_send()
            copy_from(lax.rem(mt + t - i, t)).wait_recv()
            return c

        lax.fori_loop(1, t, wait, 0)

    return start, finish


def mask_vectors(me, heads, so_ref, seg_ref, rpos_ref, rlab_ref, cpos_ref, clab_ref, cgrid_ref, lgrid_ref):
    seg = seg_ref[...]
    prompt_end = jnp.sum(jnp.sum((seg == 0).astype(jnp.int32), axis=1, keepdims=True), axis=0, keepdims=True)
    chosen_end = jnp.sum(jnp.sum((seg <= 1).astype(jnp.int32), axis=1, keepdims=True), axis=0, keepdims=True)

    def label_of(pos):
        return (pos >= prompt_end).astype(jnp.int32) + (pos >= chosen_end).astype(jnp.int32)

    def position_of(rows):
        block = lax.shift_right_logical(rows, 6)
        start = jnp.zeros(rows.shape, jnp.int32)
        for b in range(so_ref.shape[0]):
            start = jnp.where(block == b, so_ref[b], start)
        return start * SPAN + jnp.bitwise_and(rows, SPAN - 1)

    lanes = lax.broadcasted_iota(jnp.int32, cpos_ref.shape, 1)
    cpos = position_of(lanes)
    cpos_ref[...] = cpos
    clab_ref[...] = label_of(cpos)
    grid = (lax.broadcasted_iota(jnp.int32, cgrid_ref.shape, 0) * cgrid_ref.shape[1]
            + lax.broadcasted_iota(jnp.int32, cgrid_ref.shape, 1))
    gpos = position_of(grid)
    cgrid_ref[...] = gpos
    lgrid_ref[...] = label_of(gpos)
    local = rpos_ref.shape[0] // heads
    within = jnp.bitwise_and(lax.broadcasted_iota(jnp.int32, rpos_ref.shape, 0), local - 1)
    first = so_ref[me * (local // SPAN)]
    second = so_ref[me * (local // SPAN) + 1]
    start = jnp.where(within < SPAN, first, second)
    rpos = start * SPAN + jnp.bitwise_and(within, SPAN - 1)
    rpos_ref[...] = rpos
    rlab_ref[...] = label_of(rpos)


def gather_kernel(n, t, src_ref, og_ref, so_ref, seg_ref, out_ref, grad_ref,
                  rpos_ref, rlab_ref, cpos_ref, clab_ref, cgrid_ref, lgrid_ref,
                  send_sem, recv_sem, gsend_sem, grecv_sem):
    me = lax.axis_index("ctx")
    mt = lax.axis_index("tp")
    greet_all(n, me, t, mt)
    rows = og_ref.shape[0]
    cols = grad_ref.shape[1]

    def grad_src(p):
        return og_ref.at[:, pl.ds(pl.multiple_of(p * cols, cols), cols)]

    def grad_dst(p):
        return grad_ref.at[pl.ds(pl.multiple_of(p * rows, rows), rows), :]

    grad_start, grad_finish = tp_exchange(t, mt, grad_src, grad_dst, gsend_sem, grecv_sem)
    grad_start()

    def copy_to(peer):
        return pltpu.make_async_remote_copy(
            src_ref, out_ref.at[me], send_sem.at[peer], recv_sem.at[me],
            device_id={"ctx": peer}, device_id_type=MESH)

    def copy_from(src):
        return pltpu.make_async_remote_copy(
            src_ref, out_ref.at[src], send_sem.at[src], recv_sem.at[src],
            device_id={"ctx": src}, device_id_type=MESH)

    def send(i, c):
        copy_to(lax.rem(me + i, n)).start()
        return c

    lax.fori_loop(1, n, send, 0)
    out_ref[me] = src_ref[...]
    mask_vectors(me, grad_ref.shape[1] // HEAD_DIM, so_ref, seg_ref,
                 rpos_ref, rlab_ref, cpos_ref, clab_ref, cgrid_ref, lgrid_ref)
    grad_ref[pl.ds(pl.multiple_of(mt * rows, rows), rows), :] = og_ref[
        :, pl.ds(pl.multiple_of(mt * cols, cols), cols)]

    def wait(i, c):
        copy_to(lax.rem(me + i, n)).wait_send()
        copy_from(lax.rem(me + n - i, n)).wait_recv()
        return c

    lax.fori_loop(1, n, wait, 0)
    grad_finish()


def ctx_gather(block, out_grad, span_order, segment_ids, n, t):
    rows, width = block.shape
    grad_shape = (out_grad.shape[0] * t, out_grad.shape[1] // t)
    stacked = rows * (grad_shape[1] // HEAD_DIM)
    seg = segment_ids.reshape(n, segment_ids.shape[0] // n)
    column = jax.ShapeDtypeStruct((1, n * rows), jnp.int32)
    row = jax.ShapeDtypeStruct((stacked, 1), jnp.int32)
    grid = jax.ShapeDtypeStruct((n, rows), jnp.int32)
    return pl.pallas_call(
        functools.partial(gather_kernel, n, t),
        out_shape=(
            jax.ShapeDtypeStruct((n, rows, width), block.dtype),
            jax.ShapeDtypeStruct(grad_shape, out_grad.dtype),
            row, row, column, column, grid, grid,
        ),
        in_specs=[pl.BlockSpec(memory_space=pltpu.VMEM)] * 2
        + [pl.BlockSpec(memory_space=pltpu.SMEM), pl.BlockSpec(memory_space=pltpu.VMEM)],
        out_specs=(pl.BlockSpec(memory_space=pltpu.VMEM),) * 8,
        scratch_shapes=[pltpu.SemaphoreType.DMA((n,)), pltpu.SemaphoreType.DMA((n,)),
                        pltpu.SemaphoreType.DMA((t,)), pltpu.SemaphoreType.DMA((t,))],
        compiler_params=pltpu.CompilerParams(collective_id=0, has_side_effects=True),
    )(block, out_grad, span_order, seg)


KEY_BLOCK = 512
NT_DIMS = (((1,), (1,)), ((), ()))
TN_DIMS = (((0,), (0,)), ((), ()))


def stack_heads(ref):
    heads = ref.shape[1] // HEAD_DIM
    return jnp.concatenate([ref[:, h * HEAD_DIM:(h + 1) * HEAD_DIM] for h in range(heads)], axis=0)


def unstack_heads(ref, value):
    rows = ref.shape[0]
    for h in range(ref.shape[1] // HEAD_DIM):
        ref[:, h * HEAD_DIM:(h + 1) * HEAD_DIM] = value[h * rows:(h + 1) * rows]


def key_block(kv_ref, cpos_ref, clab_ref, rpos, rlab, kb):
    start = pl.multiple_of(kb * KEY_BLOCK, KEY_BLOCK)
    keys = kv_ref[pl.ds(start, KEY_BLOCK), :HEAD_DIM]
    values = kv_ref[pl.ds(start, KEY_BLOCK), HEAD_DIM:]
    cpos = cpos_ref[:, pl.ds(start, KEY_BLOCK)]
    clab = clab_ref[:, pl.ds(start, KEY_BLOCK)]
    visible = (cpos <= rpos) & ((clab == 0) | (clab == rlab))
    return start, keys, values, visible


def fwd_kernel(q_ref, kv_ref, rpos_ref, rlab_ref, cpos_ref, clab_ref, o_ref, m_ref, l_ref, acc_sc):
    scale = 1.0 / math.sqrt(HEAD_DIM)
    queries = stack_heads(q_ref)
    rpos = rpos_ref[...]
    rlab = rlab_ref[...]
    m_ref[...] = jnp.full(m_ref.shape, -jnp.inf, jnp.float32)
    l_ref[...] = jnp.zeros(l_ref.shape, jnp.float32)
    acc_sc[...] = jnp.zeros(acc_sc.shape, jnp.float32)

    def body(kb, c):
        _, keys, values, visible = key_block(kv_ref, cpos_ref, clab_ref, rpos, rlab, kb)
        scores = lax.dot_general(queries, keys, NT_DIMS, preferred_element_type=jnp.float32) * scale
        scores = jnp.where(visible, scores, -jnp.inf)
        running = m_ref[...]
        new_max = jnp.maximum(running, jnp.max(scores, axis=-1, keepdims=True))
        shift = jnp.where(new_max == -jnp.inf, 0.0, new_max)
        factor = jnp.exp(running - shift)
        weights = jnp.where(visible, jnp.exp(scores - shift), 0.0)
        l_ref[...] = l_ref[...] * factor + jnp.sum(weights, axis=-1, keepdims=True)
        acc_sc[...] = acc_sc[...] * factor + jnp.dot(
            weights.astype(jnp.bfloat16), values, preferred_element_type=jnp.float32)
        m_ref[...] = new_max
        return c

    lax.fori_loop(0, kv_ref.shape[0] // KEY_BLOCK, body, 0)
    unstack_heads(o_ref, (acc_sc[...] / l_ref[...]).astype(o_ref.dtype))


def vmem_specs(n):
    return [pl.BlockSpec(memory_space=pltpu.VMEM)] * n


def attention_fwd(q, kv, rpos, rlab, cpos, clab):
    stacked = rpos.shape[0]
    return pl.pallas_call(
        fwd_kernel,
        out_shape=(
            jax.ShapeDtypeStruct(q.shape, jnp.bfloat16),
            jax.ShapeDtypeStruct((stacked, 1), jnp.float32),
            jax.ShapeDtypeStruct((stacked, 1), jnp.float32),
        ),
        in_specs=vmem_specs(6),
        out_specs=tuple(vmem_specs(3)),
        scratch_shapes=[pltpu.VMEM((stacked, HEAD_DIM), jnp.float32)],
    )(q, kv, rpos, rlab, cpos, clab)


def column_visible(cpos_ref, clab_ref, block, rpos, rlab):
    cpos = cpos_ref[pl.ds(block, 1), :]
    clab = clab_ref[pl.ds(block, 1), :]
    return (cpos <= rpos) & ((clab == 0) | (clab == rlab))


def bwd_scatter_kernel(n, t, q_ref, g_ref, o_ref, kv_ref, rpos_ref, rlab_ref, cpos_ref, clab_ref,
                       m_ref, l_ref, dq_ref, red_ref, spread_ref, terms_sc, held, dq_sc, send_sem, recv_sem,
                       osend_sem, orecv_sem):
    me = lax.axis_index("ctx")
    mt = lax.axis_index("tp")
    greet_all(n, me, t, mt)
    rows = spread_ref.shape[0]
    cols = o_ref.shape[1]

    def out_src(p):
        return o_ref.at[pl.ds(pl.multiple_of(p * rows, rows), rows), :]

    def out_dst(p):
        return spread_ref.at[:, pl.ds(pl.multiple_of(p * cols, cols), cols)]

    out_start, out_finish = tp_exchange(t, mt, out_src, out_dst, osend_sem, orecv_sem)
    out_start()
    spread_ref[:, pl.ds(pl.multiple_of(mt * cols, cols), cols)] = o_ref[
        pl.ds(pl.multiple_of(mt * rows, rows), rows), :]
    scale = 1.0 / math.sqrt(HEAD_DIM)
    queries = stack_heads(q_ref)
    grads = stack_heads(g_ref)
    outs = stack_heads(o_ref)
    delta = jnp.sum(grads.astype(jnp.float32) * outs.astype(jnp.float32), axis=-1, keepdims=True)
    rpos = rpos_ref[...]
    rlab = rlab_ref[...]
    row_max = m_ref[...]
    inv_total = 1.0 / l_ref[...]
    dq_sc[...] = jnp.zeros(dq_sc.shape, jnp.float32)

    def copy_to(peer):
        return pltpu.make_async_remote_copy(
            terms_sc.at[peer], held.at[me], send_sem.at[peer], recv_sem.at[me],
            device_id={"ctx": peer}, device_id_type=MESH)

    def copy_from(src):
        return pltpu.make_async_remote_copy(
            terms_sc.at[src], held.at[src], send_sem.at[src], recv_sem.at[src],
            device_id={"ctx": src}, device_id_type=MESH)

    def block_terms(p):
        block = kv_ref[p]
        keys = block[:, :HEAD_DIM]
        values = block[:, HEAD_DIM:]
        visible = column_visible(cpos_ref, clab_ref, p, rpos, rlab)
        scores = lax.dot_general(queries, keys, NT_DIMS, preferred_element_type=jnp.float32) * scale
        probs = jnp.where(visible, jnp.exp(scores - row_max), 0.0) * inv_total
        dprob = lax.dot_general(grads, values, NT_DIMS, preferred_element_type=jnp.float32)
        dscore_b = (probs * (dprob - delta)).astype(jnp.bfloat16)
        probs_b = probs.astype(jnp.bfloat16)
        dq_sc[...] += jnp.dot(dscore_b, keys, preferred_element_type=jnp.float32)
        key_term = lax.dot_general(dscore_b, queries, TN_DIMS, preferred_element_type=jnp.float32) * scale
        value_term = lax.dot_general(probs_b, grads, TN_DIMS, preferred_element_type=jnp.float32)
        return jnp.concatenate([key_term, value_term], axis=1)

    red_ref[...] = block_terms(me)

    def step(i, c):
        peer = lax.rem(me + i, n)
        terms_sc[peer] = block_terms(peer).astype(terms_sc.dtype)

        @pl.when(i >= 2)
        def _():
            copy_to(lax.rem(me + i - 1, n)).start()

        return c

    lax.fori_loop(1, n, step, 0)
    copy_to(lax.rem(me + n - 1, n)).start()
    unstack_heads(dq_ref, (dq_sc[...] * scale).astype(dq_ref.dtype))

    def arrive(i, c):
        src = lax.rem(me + n - i, n)
        copy_from(src).wait_recv()
        red_ref[...] += held[src].astype(jnp.float32)
        return c

    lax.fori_loop(1, n, arrive, 0)

    def drain(i, c):
        copy_to(lax.rem(me + i, n)).wait_send()
        return c

    lax.fori_loop(1, n, drain, 0)
    out_finish()


def bwd_scatter(q, g, o, kv, rpos, rlab, cpos, clab, m, l, n, t):
    _, rows, width = kv.shape
    stacked = rpos.shape[0]
    return pl.pallas_call(
        functools.partial(bwd_scatter_kernel, n, t),
        out_shape=(
            jax.ShapeDtypeStruct(q.shape, jnp.bfloat16),
            jax.ShapeDtypeStruct((rows, width), jnp.float32),
            jax.ShapeDtypeStruct((o.shape[0] // t, o.shape[1] * t), o.dtype),
        ),
        in_specs=vmem_specs(10),
        out_specs=tuple(vmem_specs(3)),
        scratch_shapes=[
            pltpu.VMEM(kv.shape, jnp.bfloat16),
            pltpu.VMEM(kv.shape, jnp.bfloat16),
            pltpu.VMEM((stacked, HEAD_DIM), jnp.float32),
            pltpu.SemaphoreType.DMA((n,)),
            pltpu.SemaphoreType.DMA((n,)),
            pltpu.SemaphoreType.DMA((t,)),
            pltpu.SemaphoreType.DMA((t,)),
        ],
        compiler_params=pltpu.CompilerParams(collective_id=1, has_side_effects=True),
    )(q, g, o, kv, rpos, rlab, cpos, clab, m, l)


def on_device(query_rows, key_rows, value_rows, out_grad, segment_ids, span_order):
    ctx_size = lax.axis_size("ctx")
    ctx_index = lax.axis_index("ctx")
    local_rows = query_rows.shape[0]
    heads_here = query_rows.shape[1] // HEAD_DIM
    total_rows = local_rows * ctx_size
    kv_local = jnp.concatenate([key_rows, value_rows], axis=1)
    tp_size = lax.axis_size("tp")
    kv_all, grad_rows, rpos, rlab, cpos_row, clab_row, cpos, clab = ctx_gather(
        kv_local, out_grad, span_order, segment_ids, ctx_size, tp_size)
    attn_local, row_max, total = attention_fwd(
        query_rows, kv_all.reshape(total_rows, kv_all.shape[2]), rpos, rlab, cpos_row, clab_row)
    query_grad, reduced, attn_spread = bwd_scatter(
        query_rows, grad_rows, attn_local, kv_all, rpos, rlab, cpos, clab, row_max, total,
        ctx_size, tp_size)
    key_grad = reduced[:, :HEAD_DIM].astype(jnp.bfloat16)
    value_grad = reduced[:, HEAD_DIM:].astype(jnp.bfloat16)
    return (attn_spread, query_grad, key_grad, value_grad)


def solution(mesh):
    placed = (P("ctx", "tp"), P("ctx", "tp"), P("ctx", "tp"), P(("ctx", "tp"), None), P(), P())
    return jax.shard_map(
        on_device,
        mesh=mesh,
        in_specs=placed,
        out_specs=(P(("ctx", "tp"), None), P("ctx", "tp"), P("ctx", "tp"), P("ctx", "tp")),
        check_vma=False,
    )
```

```python
import functools
import math

import jax
import jax.numpy as jnp
from jax import lax
from jax.experimental import pallas as pl
from jax.experimental.pallas import tpu as pltpu
from jax.sharding import PartitionSpec as P

HEAD_DIM = 128
SPAN = 64
MESH = pl.DeviceIdType.MESH


CTX_SHAPE = (4, 4, 2)


def ctx_peer(me, i, n, sign):
    if n != math.prod(CTX_SHAPE):
        return lax.rem(me + sign * i + n, n)
    sx, sy, sz = CTX_SHAPE
    dz = lax.rem(i, sz)
    dx = lax.rem(i // sz, sx)
    dy = i // (sz * sx)
    x = me // (sy * sz)
    y = lax.rem(me // sz, sy)
    z = lax.rem(me, sz)
    x = lax.rem(x + sign * dx + sx, sx)
    y = lax.rem(y + sign * dy + sy, sy)
    z = lax.rem(z + sign * dz + sz, sz)
    return (x * sy + y) * sz + z


def greet_all(n, me, t=1, mt=None):
    barrier = pltpu.get_barrier_semaphore()

    def greet(i, c):
        peer = lax.rem(me + i, n)
        pl.semaphore_signal(barrier, inc=1, device_id={"ctx": peer}, device_id_type=MESH)
        return c

    def greet_tp(i, c):
        peer = lax.rem(mt + i, t)
        pl.semaphore_signal(barrier, inc=1, device_id={"tp": peer}, device_id_type=MESH)
        return c

    lax.fori_loop(1, n, greet, 0)
    if t > 1:
        lax.fori_loop(1, t, greet_tp, 0)
    pl.semaphore_wait(barrier, n - 1 + t - 1)


def tp_exchange(t, mt, src_of, dst_of, send_sem, recv_sem):
    def copy_to(peer):
        return pltpu.make_async_remote_copy(
            src_of(peer), dst_of(mt), send_sem.at[peer], recv_sem.at[mt],
            device_id={"tp": peer}, device_id_type=MESH)

    def copy_from(src):
        return pltpu.make_async_remote_copy(
            src_of(mt), dst_of(src), send_sem.at[src], recv_sem.at[src],
            device_id={"tp": src}, device_id_type=MESH)

    def start():
        def send(i, c):
            copy_to(lax.rem(mt + i, t)).start()
            return c

        lax.fori_loop(1, t, send, 0)

    def finish():
        def wait(i, c):
            copy_to(lax.rem(mt + i, t)).wait_send()
            copy_from(lax.rem(mt + t - i, t)).wait_recv()
            return c

        lax.fori_loop(1, t, wait, 0)

    return start, finish


def mask_vectors(me, heads, so_ref, seg_ref, rpos_ref, rlab_ref, cpos_ref, clab_ref, cgrid_ref, lgrid_ref):
    seg = seg_ref[...]
    prompt_end = jnp.sum(jnp.sum((seg == 0).astype(jnp.int32), axis=1, keepdims=True), axis=0, keepdims=True)
    chosen_end = jnp.sum(jnp.sum((seg <= 1).astype(jnp.int32), axis=1, keepdims=True), axis=0, keepdims=True)

    def label_of(pos):
        return (pos >= prompt_end).astype(jnp.int32) + (pos >= chosen_end).astype(jnp.int32)

    def position_of(rows):
        block = lax.shift_right_logical(rows, 6)
        start = jnp.zeros(rows.shape, jnp.int32)
        for b in range(so_ref.shape[0]):
            start = jnp.where(block == b, so_ref[b], start)
        return start * SPAN + jnp.bitwise_and(rows, SPAN - 1)

    lanes = lax.broadcasted_iota(jnp.int32, cpos_ref.shape, 1)
    cpos = position_of(lanes)
    cpos_ref[...] = cpos
    clab_ref[...] = label_of(cpos)
    grid = (lax.broadcasted_iota(jnp.int32, cgrid_ref.shape, 0) * cgrid_ref.shape[1]
            + lax.broadcasted_iota(jnp.int32, cgrid_ref.shape, 1))
    gpos = position_of(grid)
    cgrid_ref[...] = gpos
    lgrid_ref[...] = label_of(gpos)
    local = rpos_ref.shape[0] // heads
    within = jnp.bitwise_and(lax.broadcasted_iota(jnp.int32, rpos_ref.shape, 0), local - 1)
    first = so_ref[me * (local // SPAN)]
    second = so_ref[me * (local // SPAN) + 1]
    start = jnp.where(within < SPAN, first, second)
    rpos = start * SPAN + jnp.bitwise_and(within, SPAN - 1)
    rpos_ref[...] = rpos
    rlab_ref[...] = label_of(rpos)


def gather_kernel(n, t, src_ref, og_ref, so_ref, seg_ref, out_ref, grad_ref,
                  rpos_ref, rlab_ref, cpos_ref, clab_ref, cgrid_ref, lgrid_ref,
                  send_sem, recv_sem, gsend_sem, grecv_sem):
    me = lax.axis_index("ctx")
    mt = lax.axis_index("tp")
    greet_all(n, me, t, mt)
    rows = og_ref.shape[0]
    cols = grad_ref.shape[1]

    def grad_src(p):
        return og_ref.at[:, pl.ds(pl.multiple_of(p * cols, cols), cols)]

    def grad_dst(p):
        return grad_ref.at[pl.ds(pl.multiple_of(p * rows, rows), rows), :]

    grad_start, grad_finish = tp_exchange(t, mt, grad_src, grad_dst, gsend_sem, grecv_sem)
    grad_start()

    def copy_to(peer):
        return pltpu.make_async_remote_copy(
            src_ref, out_ref.at[me], send_sem.at[peer], recv_sem.at[me],
            device_id={"ctx": peer}, device_id_type=MESH)

    def copy_from(src):
        return pltpu.make_async_remote_copy(
            src_ref, out_ref.at[src], send_sem.at[src], recv_sem.at[src],
            device_id={"ctx": src}, device_id_type=MESH)

    def send(i, c):
        copy_to(ctx_peer(me, i, n, 1)).start()
        return c

    lax.fori_loop(1, n, send, 0)
    out_ref[me] = src_ref[...]
    mask_vectors(me, grad_ref.shape[1] // HEAD_DIM, so_ref, seg_ref,
                 rpos_ref, rlab_ref, cpos_ref, clab_ref, cgrid_ref, lgrid_ref)
    grad_ref[pl.ds(pl.multiple_of(mt * rows, rows), rows), :] = og_ref[
        :, pl.ds(pl.multiple_of(mt * cols, cols), cols)]

    def wait(i, c):
        copy_to(ctx_peer(me, i, n, 1)).wait_send()
        copy_from(ctx_peer(me, i, n, -1)).wait_recv()
        return c

    lax.fori_loop(1, n, wait, 0)
    grad_finish()


def ctx_gather(block, out_grad, span_order, segment_ids, n, t):
    rows, width = block.shape
    grad_shape = (out_grad.shape[0] * t, out_grad.shape[1] // t)
    stacked = rows * (grad_shape[1] // HEAD_DIM)
    seg = segment_ids.reshape(n, segment_ids.shape[0] // n)
    column = jax.ShapeDtypeStruct((1, n * rows), jnp.int32)
    row = jax.ShapeDtypeStruct((stacked, 1), jnp.int32)
    grid = jax.ShapeDtypeStruct((n, rows), jnp.int32)
    return pl.pallas_call(
        functools.partial(gather_kernel, n, t),
        out_shape=(
            jax.ShapeDtypeStruct((n, rows, width), block.dtype),
            jax.ShapeDtypeStruct(grad_shape, out_grad.dtype),
            row, row, column, column, grid, grid,
        ),
        in_specs=[pl.BlockSpec(memory_space=pltpu.VMEM)] * 2
        + [pl.BlockSpec(memory_space=pltpu.SMEM), pl.BlockSpec(memory_space=pltpu.VMEM)],
        out_specs=(pl.BlockSpec(memory_space=pltpu.VMEM),) * 8,
        scratch_shapes=[pltpu.SemaphoreType.DMA((n,)), pltpu.SemaphoreType.DMA((n,)),
                        pltpu.SemaphoreType.DMA((t,)), pltpu.SemaphoreType.DMA((t,))],
        compiler_params=pltpu.CompilerParams(collective_id=0, has_side_effects=True),
    )(block, out_grad, span_order, seg)


KEY_BLOCK = 512
NT_DIMS = (((1,), (1,)), ((), ()))
TN_DIMS = (((0,), (0,)), ((), ()))


def stack_heads(ref):
    heads = ref.shape[1] // HEAD_DIM
    return jnp.concatenate([ref[:, h * HEAD_DIM:(h + 1) * HEAD_DIM] for h in range(heads)], axis=0)


def unstack_heads(ref, value):
    rows = ref.shape[0]
    for h in range(ref.shape[1] // HEAD_DIM):
        ref[:, h * HEAD_DIM:(h + 1) * HEAD_DIM] = value[h * rows:(h + 1) * rows]


def key_block(kv_ref, cpos_ref, clab_ref, rpos, rlab, kb):
    start = pl.multiple_of(kb * KEY_BLOCK, KEY_BLOCK)
    keys = kv_ref[pl.ds(start, KEY_BLOCK), :HEAD_DIM]
    values = kv_ref[pl.ds(start, KEY_BLOCK), HEAD_DIM:]
    cpos = cpos_ref[:, pl.ds(start, KEY_BLOCK)]
    clab = clab_ref[:, pl.ds(start, KEY_BLOCK)]
    visible = (cpos <= rpos) & ((clab == 0) | (clab == rlab))
    return start, keys, values, visible


def fwd_kernel(q_ref, kv_ref, rpos_ref, rlab_ref, cpos_ref, clab_ref, o_ref, m_ref, l_ref, acc_sc):
    scale = 1.0 / math.sqrt(HEAD_DIM)
    queries = stack_heads(q_ref)
    rpos = rpos_ref[...]
    rlab = rlab_ref[...]
    m_ref[...] = jnp.full(m_ref.shape, -jnp.inf, jnp.float32)
    l_ref[...] = jnp.zeros(l_ref.shape, jnp.float32)
    acc_sc[...] = jnp.zeros(acc_sc.shape, jnp.float32)

    def body(kb, c):
        _, keys, values, visible = key_block(kv_ref, cpos_ref, clab_ref, rpos, rlab, kb)
        scores = lax.dot_general(queries, keys, NT_DIMS, preferred_element_type=jnp.float32) * scale
        scores = jnp.where(visible, scores, -jnp.inf)
        running = m_ref[...]
        new_max = jnp.maximum(running, jnp.max(scores, axis=-1, keepdims=True))
        shift = jnp.where(new_max == -jnp.inf, 0.0, new_max)
        factor = jnp.exp(running - shift)
        weights = jnp.where(visible, jnp.exp(scores - shift), 0.0)
        l_ref[...] = l_ref[...] * factor + jnp.sum(weights, axis=-1, keepdims=True)
        acc_sc[...] = acc_sc[...] * factor + jnp.dot(
            weights.astype(jnp.bfloat16), values, preferred_element_type=jnp.float32)
        m_ref[...] = new_max
        return c

    lax.fori_loop(0, kv_ref.shape[0] // KEY_BLOCK, body, 0)
    unstack_heads(o_ref, (acc_sc[...] / l_ref[...]).astype(o_ref.dtype))


def vmem_specs(n):
    return [pl.BlockSpec(memory_space=pltpu.VMEM)] * n


def attention_fwd(q, kv, rpos, rlab, cpos, clab):
    stacked = rpos.shape[0]
    return pl.pallas_call(
        fwd_kernel,
        out_shape=(
            jax.ShapeDtypeStruct(q.shape, jnp.bfloat16),
            jax.ShapeDtypeStruct((stacked, 1), jnp.float32),
            jax.ShapeDtypeStruct((stacked, 1), jnp.float32),
        ),
        in_specs=vmem_specs(6),
        out_specs=tuple(vmem_specs(3)),
        scratch_shapes=[pltpu.VMEM((stacked, HEAD_DIM), jnp.float32)],
    )(q, kv, rpos, rlab, cpos, clab)


def column_visible(cpos_ref, clab_ref, block, rpos, rlab):
    cpos = cpos_ref[pl.ds(block, 1), :]
    clab = clab_ref[pl.ds(block, 1), :]
    return (cpos <= rpos) & ((clab == 0) | (clab == rlab))


def bwd_scatter_kernel(n, t, q_ref, g_ref, o_ref, kv_ref, rpos_ref, rlab_ref, cpos_ref, clab_ref,
                       m_ref, l_ref, dq_ref, red_ref, spread_ref, terms_sc, held, dq_sc, send_sem, recv_sem,
                       osend_sem, orecv_sem):
    me = lax.axis_index("ctx")
    mt = lax.axis_index("tp")
    greet_all(n, me, t, mt)
    rows = spread_ref.shape[0]
    cols = o_ref.shape[1]

    def out_src(p):
        return o_ref.at[pl.ds(pl.multiple_of(p * rows, rows), rows), :]

    def out_dst(p):
        return spread_ref.at[:, pl.ds(pl.multiple_of(p * cols, cols), cols)]

    out_start, out_finish = tp_exchange(t, mt, out_src, out_dst, osend_sem, orecv_sem)
    out_start()
    spread_ref[:, pl.ds(pl.multiple_of(mt * cols, cols), cols)] = o_ref[
        pl.ds(pl.multiple_of(mt * rows, rows), rows), :]
    scale = 1.0 / math.sqrt(HEAD_DIM)
    queries = stack_heads(q_ref)
    grads = stack_heads(g_ref)
    outs = stack_heads(o_ref)
    delta = jnp.sum(grads.astype(jnp.float32) * outs.astype(jnp.float32), axis=-1, keepdims=True)
    rpos = rpos_ref[...]
    rlab = rlab_ref[...]
    row_max = m_ref[...]
    inv_total = 1.0 / l_ref[...]
    dq_sc[...] = jnp.zeros(dq_sc.shape, jnp.float32)

    def copy_to(peer):
        return pltpu.make_async_remote_copy(
            terms_sc.at[peer], held.at[me], send_sem.at[peer], recv_sem.at[me],
            device_id={"ctx": peer}, device_id_type=MESH)

    def copy_from(src):
        return pltpu.make_async_remote_copy(
            terms_sc.at[src], held.at[src], send_sem.at[src], recv_sem.at[src],
            device_id={"ctx": src}, device_id_type=MESH)

    def block_terms(p):
        block = kv_ref[p]
        keys = block[:, :HEAD_DIM]
        values = block[:, HEAD_DIM:]
        visible = column_visible(cpos_ref, clab_ref, p, rpos, rlab)
        scores = lax.dot_general(queries, keys, NT_DIMS, preferred_element_type=jnp.float32) * scale
        probs = jnp.where(visible, jnp.exp(scores - row_max), 0.0) * inv_total
        dprob = lax.dot_general(grads, values, NT_DIMS, preferred_element_type=jnp.float32)
        dscore_b = (probs * (dprob - delta)).astype(jnp.bfloat16)
        probs_b = probs.astype(jnp.bfloat16)
        dq_sc[...] += jnp.dot(dscore_b, keys, preferred_element_type=jnp.float32)
        key_term = lax.dot_general(dscore_b, queries, TN_DIMS, preferred_element_type=jnp.float32) * scale
        value_term = lax.dot_general(probs_b, grads, TN_DIMS, preferred_element_type=jnp.float32)
        return jnp.concatenate([key_term, value_term], axis=1)

    red_ref[...] = block_terms(me)

    def step(i, c):
        peer = ctx_peer(me, i, n, 1)
        terms_sc[peer] = block_terms(peer).astype(terms_sc.dtype)

        @pl.when(i >= 2)
        def _():
            copy_to(ctx_peer(me, i - 1, n, 1)).start()

        return c

    lax.fori_loop(1, n, step, 0)
    copy_to(ctx_peer(me, n - 1, n, 1)).start()
    unstack_heads(dq_ref, (dq_sc[...] * scale).astype(dq_ref.dtype))

    def arrive(i, c):
        src = ctx_peer(me, i, n, -1)
        copy_from(src).wait_recv()
        red_ref[...] += held[src].astype(jnp.float32)
        return c

    lax.fori_loop(1, n, arrive, 0)

    def drain(i, c):
        copy_to(ctx_peer(me, i, n, 1)).wait_send()
        return c

    lax.fori_loop(1, n, drain, 0)
    out_finish()


def bwd_scatter(q, g, o, kv, rpos, rlab, cpos, clab, m, l, n, t):
    _, rows, width = kv.shape
    stacked = rpos.shape[0]
    return pl.pallas_call(
        functools.partial(bwd_scatter_kernel, n, t),
        out_shape=(
            jax.ShapeDtypeStruct(q.shape, jnp.bfloat16),
            jax.ShapeDtypeStruct((rows, width), jnp.float32),
            jax.ShapeDtypeStruct((o.shape[0] // t, o.shape[1] * t), o.dtype),
        ),
        in_specs=vmem_specs(10),
        out_specs=tuple(vmem_specs(3)),
        scratch_shapes=[
            pltpu.VMEM(kv.shape, jnp.bfloat16),
            pltpu.VMEM(kv.shape, jnp.bfloat16),
            pltpu.VMEM((stacked, HEAD_DIM), jnp.float32),
            pltpu.SemaphoreType.DMA((n,)),
            pltpu.SemaphoreType.DMA((n,)),
            pltpu.SemaphoreType.DMA((t,)),
            pltpu.SemaphoreType.DMA((t,)),
        ],
        compiler_params=pltpu.CompilerParams(collective_id=1, has_side_effects=True),
    )(q, g, o, kv, rpos, rlab, cpos, clab, m, l)


def on_device(query_rows, key_rows, value_rows, out_grad, segment_ids, span_order):
    ctx_size = lax.axis_size("ctx")
    ctx_index = lax.axis_index("ctx")
    local_rows = query_rows.shape[0]
    heads_here = query_rows.shape[1] // HEAD_DIM
    total_rows = local_rows * ctx_size
    kv_local = jnp.concatenate([key_rows, value_rows], axis=1)
    tp_size = lax.axis_size("tp")
    kv_all, grad_rows, rpos, rlab, cpos_row, clab_row, cpos, clab = ctx_gather(
        kv_local, out_grad, span_order, segment_ids, ctx_size, tp_size)
    attn_local, row_max, total = attention_fwd(
        query_rows, kv_all.reshape(total_rows, kv_all.shape[2]), rpos, rlab, cpos_row, clab_row)
    query_grad, reduced, attn_spread = bwd_scatter(
        query_rows, grad_rows, attn_local, kv_all, rpos, rlab, cpos, clab, row_max, total,
        ctx_size, tp_size)
    key_grad = reduced[:, :HEAD_DIM].astype(jnp.bfloat16)
    value_grad = reduced[:, HEAD_DIM:].astype(jnp.bfloat16)
    return (attn_spread, query_grad, key_grad, value_grad)


def solution(mesh):
    placed = (P("ctx", "tp"), P("ctx", "tp"), P("ctx", "tp"), P(("ctx", "tp"), None), P(), P())
    return jax.shard_map(
        on_device,
        mesh=mesh,
        in_specs=placed,
        out_specs=(P(("ctx", "tp"), None), P("ctx", "tp"), P("ctx", "tp"), P("ctx", "tp")),
        check_vma=False,
    )
```

```python
import functools
import math

import jax
import jax.numpy as jnp
from jax import lax
from jax.experimental import pallas as pl
from jax.experimental.pallas import tpu as pltpu
from jax.sharding import PartitionSpec as P

HEAD_DIM = 128
SPAN = 64
MESH = pl.DeviceIdType.MESH


CTX_SHAPE = (4, 4, 2)


def ctx_peer(me, i, n, sign):
    if n != math.prod(CTX_SHAPE):
        return lax.rem(me + sign * i + n, n)
    sx, sy, sz = CTX_SHAPE
    dz = lax.rem(i, sz)
    dx = lax.rem(i // sz, sx)
    dy = i // (sz * sx)
    x = me // (sy * sz)
    y = lax.rem(me // sz, sy)
    z = lax.rem(me, sz)
    x = lax.rem(x + sign * dx + sx, sx)
    y = lax.rem(y + sign * dy + sy, sy)
    z = lax.rem(z + sign * dz + sz, sz)
    return (x * sy + y) * sz + z


def greet_all(n, me, t=1, mt=None):
    barrier = pltpu.get_barrier_semaphore()

    def greet(i, c):
        peer = lax.rem(me + i, n)
        pl.semaphore_signal(barrier, inc=1, device_id={"ctx": peer}, device_id_type=MESH)
        return c

    def greet_tp(i, c):
        peer = lax.rem(mt + i, t)
        pl.semaphore_signal(barrier, inc=1, device_id={"tp": peer}, device_id_type=MESH)
        return c

    lax.fori_loop(1, n, greet, 0)
    if t > 1:
        lax.fori_loop(1, t, greet_tp, 0)
    pl.semaphore_wait(barrier, n - 1 + t - 1)


def tp_exchange(t, mt, src_of, dst_of, send_sem, recv_sem):
    def copy_to(peer):
        return pltpu.make_async_remote_copy(
            src_of(peer), dst_of(mt), send_sem.at[peer], recv_sem.at[mt],
            device_id={"tp": peer}, device_id_type=MESH)

    def copy_from(src):
        return pltpu.make_async_remote_copy(
            src_of(mt), dst_of(src), send_sem.at[src], recv_sem.at[src],
            device_id={"tp": src}, device_id_type=MESH)

    def start():
        def send(i, c):
            copy_to(lax.rem(mt + i, t)).start()
            return c

        lax.fori_loop(1, t, send, 0)

    def finish():
        def wait(i, c):
            copy_to(lax.rem(mt + i, t)).wait_send()
            copy_from(lax.rem(mt + t - i, t)).wait_recv()
            return c

        lax.fori_loop(1, t, wait, 0)

    return start, finish


def mask_vectors(me, heads, so_ref, seg_ref, rpos_ref, rlab_ref, cpos_ref, clab_ref, cgrid_ref, lgrid_ref):
    seg = seg_ref[...]
    prompt_end = jnp.sum(jnp.sum((seg == 0).astype(jnp.int32), axis=1, keepdims=True), axis=0, keepdims=True)
    chosen_end = jnp.sum(jnp.sum((seg <= 1).astype(jnp.int32), axis=1, keepdims=True), axis=0, keepdims=True)

    def label_of(pos):
        return (pos >= prompt_end).astype(jnp.int32) + (pos >= chosen_end).astype(jnp.int32)

    def position_of(rows):
        block = lax.shift_right_logical(rows, 6)
        start = jnp.zeros(rows.shape, jnp.int32)
        for b in range(so_ref.shape[0]):
            start = jnp.where(block == b, so_ref[b], start)
        return start * SPAN + jnp.bitwise_and(rows, SPAN - 1)

    lanes = lax.broadcasted_iota(jnp.int32, cpos_ref.shape, 1)
    cpos = position_of(lanes)
    cpos_ref[...] = cpos
    clab_ref[...] = label_of(cpos)
    grid = (lax.broadcasted_iota(jnp.int32, cgrid_ref.shape, 0) * cgrid_ref.shape[1]
            + lax.broadcasted_iota(jnp.int32, cgrid_ref.shape, 1))
    gpos = position_of(grid)
    cgrid_ref[...] = gpos
    lgrid_ref[...] = label_of(gpos)
    local = rpos_ref.shape[0] // heads
    within = jnp.bitwise_and(lax.broadcasted_iota(jnp.int32, rpos_ref.shape, 0), local - 1)
    first = so_ref[me * (local // SPAN)]
    second = so_ref[me * (local // SPAN) + 1]
    start = jnp.where(within < SPAN, first, second)
    rpos = start * SPAN + jnp.bitwise_and(within, SPAN - 1)
    rpos_ref[...] = rpos
    rlab_ref[...] = label_of(rpos)


def gather_kernel(n, t, src_ref, og_ref, so_ref, seg_ref, out_ref, grad_ref,
                  rpos_ref, rlab_ref, cpos_ref, clab_ref, cgrid_ref, lgrid_ref,
                  send_sem, recv_sem, gsend_sem, grecv_sem):
    me = lax.axis_index("ctx")
    mt = lax.axis_index("tp")
    greet_all(n, me, t, mt)
    rows = og_ref.shape[0]
    cols = grad_ref.shape[1]

    def grad_src(p):
        return og_ref.at[:, pl.ds(pl.multiple_of(p * cols, cols), cols)]

    def grad_dst(p):
        return grad_ref.at[pl.ds(pl.multiple_of(p * rows, rows), rows), :]

    grad_start, grad_finish = tp_exchange(t, mt, grad_src, grad_dst, gsend_sem, grecv_sem)
    grad_start()

    def copy_to(peer):
        return pltpu.make_async_remote_copy(
            src_ref, out_ref.at[me], send_sem.at[peer], recv_sem.at[me],
            device_id={"ctx": peer}, device_id_type=MESH)

    def copy_from(src):
        return pltpu.make_async_remote_copy(
            src_ref, out_ref.at[src], send_sem.at[src], recv_sem.at[src],
            device_id={"ctx": src}, device_id_type=MESH)

    def send(i, c):
        copy_to(ctx_peer(me, i, n, 1)).start()
        return c

    lax.fori_loop(1, n, send, 0)
    out_ref[me] = src_ref[...]
    mask_vectors(me, grad_ref.shape[1] // HEAD_DIM, so_ref, seg_ref,
                 rpos_ref, rlab_ref, cpos_ref, clab_ref, cgrid_ref, lgrid_ref)
    grad_ref[pl.ds(pl.multiple_of(mt * rows, rows), rows), :] = og_ref[
        :, pl.ds(pl.multiple_of(mt * cols, cols), cols)]

    def wait(i, c):
        copy_to(ctx_peer(me, i, n, 1)).wait_send()
        copy_from(ctx_peer(me, i, n, -1)).wait_recv()
        return c

    lax.fori_loop(1, n, wait, 0)
    grad_finish()


def ctx_gather(block, out_grad, span_order, segment_ids, n, t):
    rows, width = block.shape
    grad_shape = (out_grad.shape[0] * t, out_grad.shape[1] // t)
    stacked = rows * (grad_shape[1] // HEAD_DIM)
    seg = segment_ids.reshape(n, segment_ids.shape[0] // n)
    column = jax.ShapeDtypeStruct((1, n * rows), jnp.int32)
    row = jax.ShapeDtypeStruct((stacked, 1), jnp.int32)
    grid = jax.ShapeDtypeStruct((n, rows), jnp.int32)
    return pl.pallas_call(
        functools.partial(gather_kernel, n, t),
        out_shape=(
            jax.ShapeDtypeStruct((n, rows, width), block.dtype),
            jax.ShapeDtypeStruct(grad_shape, out_grad.dtype),
            row, row, column, column, grid, grid,
        ),
        in_specs=[pl.BlockSpec(memory_space=pltpu.VMEM)] * 2
        + [pl.BlockSpec(memory_space=pltpu.SMEM), pl.BlockSpec(memory_space=pltpu.VMEM)],
        out_specs=(pl.BlockSpec(memory_space=pltpu.VMEM),) * 8,
        scratch_shapes=[pltpu.SemaphoreType.DMA((n,)), pltpu.SemaphoreType.DMA((n,)),
                        pltpu.SemaphoreType.DMA((t,)), pltpu.SemaphoreType.DMA((t,))],
        compiler_params=pltpu.CompilerParams(collective_id=0, has_side_effects=True),
    )(block, out_grad, span_order, seg)


KEY_BLOCK = 1024
NT_DIMS = (((1,), (1,)), ((), ()))
TN_DIMS = (((0,), (0,)), ((), ()))


def stack_heads(ref):
    heads = ref.shape[1] // HEAD_DIM
    return jnp.concatenate([ref[:, h * HEAD_DIM:(h + 1) * HEAD_DIM] for h in range(heads)], axis=0)


def unstack_heads(ref, value):
    rows = ref.shape[0]
    for h in range(ref.shape[1] // HEAD_DIM):
        ref[:, h * HEAD_DIM:(h + 1) * HEAD_DIM] = value[h * rows:(h + 1) * rows]


def key_block(kv_ref, cpos_ref, clab_ref, rpos, rlab, kb):
    size = min(KEY_BLOCK, kv_ref.shape[0])
    start = pl.multiple_of(kb * size, size)
    keys = kv_ref[pl.ds(start, size), :HEAD_DIM]
    values = kv_ref[pl.ds(start, size), HEAD_DIM:]
    cpos = cpos_ref[:, pl.ds(start, size)]
    clab = clab_ref[:, pl.ds(start, size)]
    visible = (cpos <= rpos) & ((clab == 0) | (clab == rlab))
    return start, keys, values, visible


def fwd_kernel(q_ref, kv_ref, rpos_ref, rlab_ref, cpos_ref, clab_ref, o_ref, m_ref, l_ref, acc_sc):
    scale = 1.0 / math.sqrt(HEAD_DIM)
    queries = stack_heads(q_ref)
    rpos = rpos_ref[...]
    rlab = rlab_ref[...]
    m_ref[...] = jnp.full(m_ref.shape, -jnp.inf, jnp.float32)
    l_ref[...] = jnp.zeros(l_ref.shape, jnp.float32)
    acc_sc[...] = jnp.zeros(acc_sc.shape, jnp.float32)

    def body(kb, c):
        _, keys, values, visible = key_block(kv_ref, cpos_ref, clab_ref, rpos, rlab, kb)
        scores = lax.dot_general(queries, keys, NT_DIMS, preferred_element_type=jnp.float32) * scale
        scores = jnp.where(visible, scores, -jnp.inf)
        running = m_ref[...]
        new_max = jnp.maximum(running, jnp.max(scores, axis=-1, keepdims=True))
        shift = jnp.where(new_max == -jnp.inf, 0.0, new_max)
        factor = jnp.exp(running - shift)
        weights = jnp.exp(scores - shift)
        l_ref[...] = l_ref[...] * factor + jnp.sum(weights, axis=-1, keepdims=True)
        acc_sc[...] = acc_sc[...] * factor + jnp.dot(
            weights.astype(jnp.bfloat16), values, preferred_element_type=jnp.float32)
        m_ref[...] = new_max
        return c

    lax.fori_loop(0, kv_ref.shape[0] // min(KEY_BLOCK, kv_ref.shape[0]), body, 0)
    unstack_heads(o_ref, (acc_sc[...] / l_ref[...]).astype(o_ref.dtype))


def vmem_specs(n):
    return [pl.BlockSpec(memory_space=pltpu.VMEM)] * n


def attention_fwd(q, kv, rpos, rlab, cpos, clab):
    stacked = rpos.shape[0]
    return pl.pallas_call(
        fwd_kernel,
        out_shape=(
            jax.ShapeDtypeStruct(q.shape, jnp.bfloat16),
            jax.ShapeDtypeStruct((stacked, 1), jnp.float32),
            jax.ShapeDtypeStruct((stacked, 1), jnp.float32),
        ),
        in_specs=vmem_specs(6),
        out_specs=tuple(vmem_specs(3)),
        scratch_shapes=[pltpu.VMEM((stacked, HEAD_DIM), jnp.float32)],
    )(q, kv, rpos, rlab, cpos, clab)


def column_visible(cpos_ref, clab_ref, block, rpos, rlab):
    cpos = cpos_ref[pl.ds(block, 1), :]
    clab = clab_ref[pl.ds(block, 1), :]
    return (cpos <= rpos) & ((clab == 0) | (clab == rlab))


def bwd_scatter_kernel(n, t, q_ref, g_ref, o_ref, kv_ref, rpos_ref, rlab_ref, cpos_ref, clab_ref,
                       m_ref, l_ref, dq_ref, red_ref, spread_ref, terms_sc, held, dq_sc, send_sem, recv_sem,
                       osend_sem, orecv_sem):
    me = lax.axis_index("ctx")
    mt = lax.axis_index("tp")
    greet_all(n, me, t, mt)
    rows = spread_ref.shape[0]
    cols = o_ref.shape[1]

    def out_src(p):
        return o_ref.at[pl.ds(pl.multiple_of(p * rows, rows), rows), :]

    def out_dst(p):
        return spread_ref.at[:, pl.ds(pl.multiple_of(p * cols, cols), cols)]

    out_start, out_finish = tp_exchange(t, mt, out_src, out_dst, osend_sem, orecv_sem)
    out_start()
    spread_ref[:, pl.ds(pl.multiple_of(mt * cols, cols), cols)] = o_ref[
        pl.ds(pl.multiple_of(mt * rows, rows), rows), :]
    scale = 1.0 / math.sqrt(HEAD_DIM)
    queries = stack_heads(q_ref)
    grads = stack_heads(g_ref)
    outs = stack_heads(o_ref)
    delta = jnp.sum(grads.astype(jnp.float32) * outs.astype(jnp.float32), axis=-1, keepdims=True)
    rpos = rpos_ref[...]
    rlab = rlab_ref[...]
    row_max = m_ref[...]
    inv_total = 1.0 / l_ref[...]
    dq_sc[...] = jnp.zeros(dq_sc.shape, jnp.float32)

    def copy_to(peer):
        return pltpu.make_async_remote_copy(
            terms_sc.at[peer], held.at[me], send_sem.at[peer], recv_sem.at[me],
            device_id={"ctx": peer}, device_id_type=MESH)

    def copy_from(src):
        return pltpu.make_async_remote_copy(
            terms_sc.at[src], held.at[src], send_sem.at[src], recv_sem.at[src],
            device_id={"ctx": src}, device_id_type=MESH)

    def block_terms(p):
        block = kv_ref[p]
        keys = block[:, :HEAD_DIM]
        values = block[:, HEAD_DIM:]
        visible = column_visible(cpos_ref, clab_ref, p, rpos, rlab)
        scores = lax.dot_general(queries, keys, NT_DIMS, preferred_element_type=jnp.float32) * scale
        probs = jnp.where(visible, jnp.exp(scores - row_max), 0.0) * inv_total
        dprob = lax.dot_general(grads, values, NT_DIMS, preferred_element_type=jnp.float32)
        dscore_b = (probs * (dprob - delta)).astype(jnp.bfloat16)
        probs_b = probs.astype(jnp.bfloat16)
        dq_sc[...] += jnp.dot(dscore_b, keys, preferred_element_type=jnp.float32)
        key_term = lax.dot_general(dscore_b, queries, TN_DIMS, preferred_element_type=jnp.float32) * scale
        value_term = lax.dot_general(probs_b, grads, TN_DIMS, preferred_element_type=jnp.float32)
        return jnp.concatenate([key_term, value_term], axis=1)

    red_ref[...] = block_terms(me)

    def step(i, c):
        peer = ctx_peer(me, i, n, 1)
        terms_sc[peer] = block_terms(peer).astype(terms_sc.dtype)

        @pl.when(i >= 2)
        def _():
            copy_to(ctx_peer(me, i - 1, n, 1)).start()

        return c

    lax.fori_loop(1, n, step, 0)
    copy_to(ctx_peer(me, n - 1, n, 1)).start()
    unstack_heads(dq_ref, (dq_sc[...] * scale).astype(dq_ref.dtype))

    def arrive(i, c):
        src = ctx_peer(me, i, n, -1)
        copy_from(src).wait_recv()
        red_ref[...] += held[src].astype(jnp.float32)
        return c

    lax.fori_loop(1, n, arrive, 0)

    def drain(i, c):
        copy_to(ctx_peer(me, i, n, 1)).wait_send()
        return c

    lax.fori_loop(1, n, drain, 0)
    out_finish()


def bwd_scatter(q, g, o, kv, rpos, rlab, cpos, clab, m, l, n, t):
    _, rows, width = kv.shape
    stacked = rpos.shape[0]
    return pl.pallas_call(
        functools.partial(bwd_scatter_kernel, n, t),
        out_shape=(
            jax.ShapeDtypeStruct(q.shape, jnp.bfloat16),
            jax.ShapeDtypeStruct((rows, width), jnp.float32),
            jax.ShapeDtypeStruct((o.shape[0] // t, o.shape[1] * t), o.dtype),
        ),
        in_specs=vmem_specs(10),
        out_specs=tuple(vmem_specs(3)),
        scratch_shapes=[
            pltpu.VMEM(kv.shape, jnp.bfloat16),
            pltpu.VMEM(kv.shape, jnp.bfloat16),
            pltpu.VMEM((stacked, HEAD_DIM), jnp.float32),
            pltpu.SemaphoreType.DMA((n,)),
            pltpu.SemaphoreType.DMA((n,)),
            pltpu.SemaphoreType.DMA((t,)),
            pltpu.SemaphoreType.DMA((t,)),
        ],
        compiler_params=pltpu.CompilerParams(collective_id=1, has_side_effects=True),
    )(q, g, o, kv, rpos, rlab, cpos, clab, m, l)


def on_device(query_rows, key_rows, value_rows, out_grad, segment_ids, span_order):
    ctx_size = lax.axis_size("ctx")
    ctx_index = lax.axis_index("ctx")
    local_rows = query_rows.shape[0]
    heads_here = query_rows.shape[1] // HEAD_DIM
    total_rows = local_rows * ctx_size
    kv_local = jnp.concatenate([key_rows, value_rows], axis=1)
    tp_size = lax.axis_size("tp")
    kv_all, grad_rows, rpos, rlab, cpos_row, clab_row, cpos, clab = ctx_gather(
        kv_local, out_grad, span_order, segment_ids, ctx_size, tp_size)
    attn_local, row_max, total = attention_fwd(
        query_rows, kv_all.reshape(total_rows, kv_all.shape[2]), rpos, rlab, cpos_row, clab_row)
    query_grad, reduced, attn_spread = bwd_scatter(
        query_rows, grad_rows, attn_local, kv_all, rpos, rlab, cpos, clab, row_max, total,
        ctx_size, tp_size)
    key_grad = reduced[:, :HEAD_DIM].astype(jnp.bfloat16)
    value_grad = reduced[:, HEAD_DIM:].astype(jnp.bfloat16)
    return (attn_spread, query_grad, key_grad, value_grad)


def solution(mesh):
    placed = (P("ctx", "tp"), P("ctx", "tp"), P("ctx", "tp"), P(("ctx", "tp"), None), P(), P())
    return jax.shard_map(
        on_device,
        mesh=mesh,
        in_specs=placed,
        out_specs=(P(("ctx", "tp"), None), P("ctx", "tp"), P("ctx", "tp"), P("ctx", "tp")),
        check_vma=False,
    )
```

```python
import functools
import math

import jax
import jax.numpy as jnp
from jax import lax
from jax.experimental import pallas as pl
from jax.experimental.pallas import tpu as pltpu
from jax.sharding import PartitionSpec as P

HEAD_DIM = 128
SPAN = 64
MESH = pl.DeviceIdType.MESH


CTX_SHAPE = (4, 4, 2)


def ctx_peer(me, i, n, sign):
    if n != math.prod(CTX_SHAPE):
        return lax.rem(me + sign * i + n, n)
    sx, sy, sz = CTX_SHAPE
    dz = lax.rem(i, sz)
    dx = lax.rem(i // sz, sx)
    dy = i // (sz * sx)
    x = me // (sy * sz)
    y = lax.rem(me // sz, sy)
    z = lax.rem(me, sz)
    x = lax.rem(x + sign * dx + sx, sx)
    y = lax.rem(y + sign * dy + sy, sy)
    z = lax.rem(z + sign * dz + sz, sz)
    return (x * sy + y) * sz + z


def greet_all(n, me, t=1, mt=None):
    barrier = pltpu.get_barrier_semaphore()

    def greet(i, c):
        peer = lax.rem(me + i, n)
        pl.semaphore_signal(barrier, inc=1, device_id={"ctx": peer}, device_id_type=MESH)
        return c

    def greet_tp(i, c):
        peer = lax.rem(mt + i, t)
        pl.semaphore_signal(barrier, inc=1, device_id={"tp": peer}, device_id_type=MESH)
        return c

    lax.fori_loop(1, n, greet, 0)
    if t > 1:
        lax.fori_loop(1, t, greet_tp, 0)
    pl.semaphore_wait(barrier, n - 1 + t - 1)


def tp_exchange(t, mt, src_of, dst_of, send_sem, recv_sem):
    def copy_to(peer):
        return pltpu.make_async_remote_copy(
            src_of(peer), dst_of(mt), send_sem.at[peer], recv_sem.at[mt],
            device_id={"tp": peer}, device_id_type=MESH)

    def copy_from(src):
        return pltpu.make_async_remote_copy(
            src_of(mt), dst_of(src), send_sem.at[src], recv_sem.at[src],
            device_id={"tp": src}, device_id_type=MESH)

    def start():
        def send(i, c):
            copy_to(lax.rem(mt + i, t)).start()
            return c

        lax.fori_loop(1, t, send, 0)

    def finish():
        def wait(i, c):
            copy_to(lax.rem(mt + i, t)).wait_send()
            copy_from(lax.rem(mt + t - i, t)).wait_recv()
            return c

        lax.fori_loop(1, t, wait, 0)

    return start, finish


def mask_vectors(me, heads, so_ref, seg_ref, rpos_ref, rlab_ref, cpos_ref, clab_ref, cgrid_ref, lgrid_ref):
    seg = seg_ref[...]
    prompt_end = jnp.sum(jnp.sum((seg == 0).astype(jnp.int32), axis=1, keepdims=True), axis=0, keepdims=True)
    chosen_end = jnp.sum(jnp.sum((seg <= 1).astype(jnp.int32), axis=1, keepdims=True), axis=0, keepdims=True)

    def label_of(pos):
        return (pos >= prompt_end).astype(jnp.int32) + (pos >= chosen_end).astype(jnp.int32)

    def position_of(rows):
        block = lax.shift_right_logical(rows, 6)
        start = jnp.zeros(rows.shape, jnp.int32)
        for b in range(so_ref.shape[0]):
            start = jnp.where(block == b, so_ref[b], start)
        return start * SPAN + jnp.bitwise_and(rows, SPAN - 1)

    lanes = lax.broadcasted_iota(jnp.int32, cpos_ref.shape, 1)
    cpos = position_of(lanes)
    cpos_ref[...] = cpos
    clab_ref[...] = label_of(cpos)
    grid = (lax.broadcasted_iota(jnp.int32, cgrid_ref.shape, 0) * cgrid_ref.shape[1]
            + lax.broadcasted_iota(jnp.int32, cgrid_ref.shape, 1))
    gpos = position_of(grid)
    cgrid_ref[...] = gpos
    lgrid_ref[...] = label_of(gpos)
    local = rpos_ref.shape[0] // heads
    within = jnp.bitwise_and(lax.broadcasted_iota(jnp.int32, rpos_ref.shape, 0), local - 1)
    first = so_ref[me * (local // SPAN)]
    second = so_ref[me * (local // SPAN) + 1]
    start = jnp.where(within < SPAN, first, second)
    rpos = start * SPAN + jnp.bitwise_and(within, SPAN - 1)
    rpos_ref[...] = rpos
    rlab_ref[...] = label_of(rpos)


def gather_kernel(n, t, k_ref, v_ref, og_ref, so_ref, seg_ref, out_ref, grad_ref,
                  rpos_ref, rlab_ref, cpos_ref, clab_ref, cgrid_ref, lgrid_ref,
                  send_sem, recv_sem, vsend_sem, vrecv_sem, gsend_sem, grecv_sem):
    me = lax.axis_index("ctx")
    mt = lax.axis_index("tp")
    greet_all(n, me, t, mt)
    rows = og_ref.shape[0]
    cols = grad_ref.shape[1]

    def grad_src(p):
        return og_ref.at[:, pl.ds(pl.multiple_of(p * cols, cols), cols)]

    def grad_dst(p):
        return grad_ref.at[pl.ds(pl.multiple_of(p * rows, rows), rows), :]

    grad_start, grad_finish = tp_exchange(t, mt, grad_src, grad_dst, gsend_sem, grecv_sem)
    grad_start()

    width = k_ref.shape[1]

    def copies(dst, peer, slot):
        return (
            pltpu.make_async_remote_copy(
                k_ref, out_ref.at[dst, :, :width], send_sem.at[slot], recv_sem.at[dst],
                device_id={"ctx": peer}, device_id_type=MESH),
            pltpu.make_async_remote_copy(
                v_ref, out_ref.at[dst, :, width:], vsend_sem.at[slot], vrecv_sem.at[dst],
                device_id={"ctx": peer}, device_id_type=MESH),
        )

    def send(i, c):
        peer = ctx_peer(me, i, n, 1)
        for copy in copies(me, peer, peer):
            copy.start()
        return c

    lax.fori_loop(1, n, send, 0)
    out_ref[me, :, :width] = k_ref[...]
    out_ref[me, :, width:] = v_ref[...]
    mask_vectors(me, grad_ref.shape[1] // HEAD_DIM, so_ref, seg_ref,
                 rpos_ref, rlab_ref, cpos_ref, clab_ref, cgrid_ref, lgrid_ref)
    grad_ref[pl.ds(pl.multiple_of(mt * rows, rows), rows), :] = og_ref[
        :, pl.ds(pl.multiple_of(mt * cols, cols), cols)]

    def wait(i, c):
        peer = ctx_peer(me, i, n, 1)
        for copy in copies(me, peer, peer):
            copy.wait_send()
        src = ctx_peer(me, i, n, -1)
        for copy in copies(src, src, src):
            copy.wait_recv()
        return c

    lax.fori_loop(1, n, wait, 0)
    grad_finish()


def ctx_gather(key_rows, value_rows, out_grad, span_order, segment_ids, n, t):
    rows = key_rows.shape[0]
    width = key_rows.shape[1] + value_rows.shape[1]
    grad_shape = (out_grad.shape[0] * t, out_grad.shape[1] // t)
    stacked = rows * (grad_shape[1] // HEAD_DIM)
    seg = segment_ids.reshape(n, segment_ids.shape[0] // n)
    column = jax.ShapeDtypeStruct((1, n * rows), jnp.int32)
    row = jax.ShapeDtypeStruct((stacked, 1), jnp.int32)
    grid = jax.ShapeDtypeStruct((n, rows), jnp.int32)
    return pl.pallas_call(
        functools.partial(gather_kernel, n, t),
        out_shape=(
            jax.ShapeDtypeStruct((n, rows, width), key_rows.dtype),
            jax.ShapeDtypeStruct(grad_shape, out_grad.dtype),
            row, row, column, column, grid, grid,
        ),
        in_specs=[pl.BlockSpec(memory_space=pltpu.VMEM)] * 3
        + [pl.BlockSpec(memory_space=pltpu.SMEM), pl.BlockSpec(memory_space=pltpu.VMEM)],
        out_specs=(pl.BlockSpec(memory_space=pltpu.VMEM),) * 8,
        scratch_shapes=[pltpu.SemaphoreType.DMA((n,))] * 4 + [pltpu.SemaphoreType.DMA((t,))] * 2,
        compiler_params=pltpu.CompilerParams(collective_id=0, has_side_effects=True),
    )(key_rows, value_rows, out_grad, span_order, seg)


KEY_BLOCK = 1024
NT_DIMS = (((1,), (1,)), ((), ()))
TN_DIMS = (((0,), (0,)), ((), ()))


def stack_heads(ref):
    heads = ref.shape[1] // HEAD_DIM
    return jnp.concatenate([ref[:, h * HEAD_DIM:(h + 1) * HEAD_DIM] for h in range(heads)], axis=0)


def unstack_heads(ref, value):
    rows = ref.shape[0]
    for h in range(ref.shape[1] // HEAD_DIM):
        ref[:, h * HEAD_DIM:(h + 1) * HEAD_DIM] = value[h * rows:(h + 1) * rows]


def key_block(kv_ref, cpos_ref, clab_ref, rpos, rlab, kb):
    size = min(KEY_BLOCK, kv_ref.shape[0])
    start = pl.multiple_of(kb * size, size)
    keys = kv_ref[pl.ds(start, size), :HEAD_DIM]
    values = kv_ref[pl.ds(start, size), HEAD_DIM:]
    cpos = cpos_ref[:, pl.ds(start, size)]
    clab = clab_ref[:, pl.ds(start, size)]
    visible = (cpos <= rpos) & ((clab == 0) | (clab == rlab))
    return start, keys, values, visible


def fwd_kernel(q_ref, kv_ref, rpos_ref, rlab_ref, cpos_ref, clab_ref, o_ref, m_ref, l_ref, acc_sc):
    scale = 1.0 / math.sqrt(HEAD_DIM)
    queries = stack_heads(q_ref)
    rpos = rpos_ref[...]
    rlab = rlab_ref[...]
    m_ref[...] = jnp.full(m_ref.shape, -jnp.inf, jnp.float32)
    l_ref[...] = jnp.zeros(l_ref.shape, jnp.float32)
    acc_sc[...] = jnp.zeros(acc_sc.shape, jnp.float32)

    def body(kb, c):
        _, keys, values, visible = key_block(kv_ref, cpos_ref, clab_ref, rpos, rlab, kb)
        scores = lax.dot_general(queries, keys, NT_DIMS, preferred_element_type=jnp.float32) * scale
        scores = jnp.where(visible, scores, -jnp.inf)
        running = m_ref[...]
        new_max = jnp.maximum(running, jnp.max(scores, axis=-1, keepdims=True))
        shift = jnp.where(new_max == -jnp.inf, 0.0, new_max)
        factor = jnp.exp(running - shift)
        weights = jnp.exp(scores - shift)
        l_ref[...] = l_ref[...] * factor + jnp.sum(weights, axis=-1, keepdims=True)
        acc_sc[...] = acc_sc[...] * factor + jnp.dot(
            weights.astype(jnp.bfloat16), values, preferred_element_type=jnp.float32)
        m_ref[...] = new_max
        return c

    lax.fori_loop(0, kv_ref.shape[0] // min(KEY_BLOCK, kv_ref.shape[0]), body, 0)
    unstack_heads(o_ref, (acc_sc[...] / l_ref[...]).astype(o_ref.dtype))


def vmem_specs(n):
    return [pl.BlockSpec(memory_space=pltpu.VMEM)] * n


def attention_fwd(q, kv, rpos, rlab, cpos, clab):
    stacked = rpos.shape[0]
    return pl.pallas_call(
        fwd_kernel,
        out_shape=(
            jax.ShapeDtypeStruct(q.shape, jnp.bfloat16),
            jax.ShapeDtypeStruct((stacked, 1), jnp.float32),
            jax.ShapeDtypeStruct((stacked, 1), jnp.float32),
        ),
        in_specs=vmem_specs(6),
        out_specs=tuple(vmem_specs(3)),
        scratch_shapes=[pltpu.VMEM((stacked, HEAD_DIM), jnp.float32)],
    )(q, kv, rpos, rlab, cpos, clab)


def column_visible(cpos_ref, clab_ref, block, rpos, rlab):
    cpos = cpos_ref[pl.ds(block, 1), :]
    clab = clab_ref[pl.ds(block, 1), :]
    return (cpos <= rpos) & ((clab == 0) | (clab == rlab))


def bwd_scatter_kernel(n, t, q_ref, g_ref, o_ref, kv_ref, rpos_ref, rlab_ref, cpos_ref, clab_ref,
                       m_ref, l_ref, dq_ref, red_ref, spread_ref, terms_sc, held, dq_sc, send_sem, recv_sem,
                       osend_sem, orecv_sem):
    me = lax.axis_index("ctx")
    mt = lax.axis_index("tp")
    greet_all(n, me, t, mt)
    rows = spread_ref.shape[0]
    cols = o_ref.shape[1]

    def out_src(p):
        return o_ref.at[pl.ds(pl.multiple_of(p * rows, rows), rows), :]

    def out_dst(p):
        return spread_ref.at[:, pl.ds(pl.multiple_of(p * cols, cols), cols)]

    out_start, out_finish = tp_exchange(t, mt, out_src, out_dst, osend_sem, orecv_sem)
    out_start()
    spread_ref[:, pl.ds(pl.multiple_of(mt * cols, cols), cols)] = o_ref[
        pl.ds(pl.multiple_of(mt * rows, rows), rows), :]
    scale = 1.0 / math.sqrt(HEAD_DIM)
    queries = stack_heads(q_ref)
    grads = stack_heads(g_ref)
    outs = stack_heads(o_ref)
    delta = jnp.sum(grads.astype(jnp.float32) * outs.astype(jnp.float32), axis=-1, keepdims=True)
    rpos = rpos_ref[...]
    rlab = rlab_ref[...]
    row_max = m_ref[...]
    inv_total = 1.0 / l_ref[...]
    dq_sc[...] = jnp.zeros(dq_sc.shape, jnp.float32)

    def copy_to(peer):
        return pltpu.make_async_remote_copy(
            terms_sc.at[peer], held.at[me], send_sem.at[peer], recv_sem.at[me],
            device_id={"ctx": peer}, device_id_type=MESH)

    def copy_from(src):
        return pltpu.make_async_remote_copy(
            terms_sc.at[src], held.at[src], send_sem.at[src], recv_sem.at[src],
            device_id={"ctx": src}, device_id_type=MESH)

    def block_terms(p):
        block = kv_ref[p]
        keys = block[:, :HEAD_DIM]
        values = block[:, HEAD_DIM:]
        visible = column_visible(cpos_ref, clab_ref, p, rpos, rlab)
        scores = lax.dot_general(queries, keys, NT_DIMS, preferred_element_type=jnp.float32) * scale
        probs = jnp.where(visible, jnp.exp(scores - row_max), 0.0) * inv_total
        dprob = lax.dot_general(grads, values, NT_DIMS, preferred_element_type=jnp.float32)
        dscore_b = (probs * (dprob - delta)).astype(jnp.bfloat16)
        probs_b = probs.astype(jnp.bfloat16)
        dq_sc[...] += jnp.dot(dscore_b, keys, preferred_element_type=jnp.float32)
        key_term = lax.dot_general(dscore_b, queries, TN_DIMS, preferred_element_type=jnp.float32) * scale
        value_term = lax.dot_general(probs_b, grads, TN_DIMS, preferred_element_type=jnp.float32)
        return jnp.concatenate([key_term, value_term], axis=1)

    red_ref[...] = block_terms(me)

    def step(i, c):
        peer = ctx_peer(me, i, n, 1)
        terms_sc[peer] = block_terms(peer).astype(terms_sc.dtype)

        @pl.when(i >= 2)
        def _():
            copy_to(ctx_peer(me, i - 1, n, 1)).start()

        return c

    lax.fori_loop(1, n, step, 0)
    copy_to(ctx_peer(me, n - 1, n, 1)).start()
    unstack_heads(dq_ref, (dq_sc[...] * scale).astype(dq_ref.dtype))

    def arrive(i, c):
        src = ctx_peer(me, i, n, -1)
        copy_from(src).wait_recv()
        red_ref[...] += held[src].astype(jnp.float32)
        return c

    lax.fori_loop(1, n, arrive, 0)

    def drain(i, c):
        copy_to(ctx_peer(me, i, n, 1)).wait_send()
        return c

    lax.fori_loop(1, n, drain, 0)
    out_finish()


def bwd_scatter(q, g, o, kv, rpos, rlab, cpos, clab, m, l, n, t):
    _, rows, width = kv.shape
    stacked = rpos.shape[0]
    return pl.pallas_call(
        functools.partial(bwd_scatter_kernel, n, t),
        out_shape=(
            jax.ShapeDtypeStruct(q.shape, jnp.bfloat16),
            jax.ShapeDtypeStruct((rows, width), jnp.float32),
            jax.ShapeDtypeStruct((o.shape[0] // t, o.shape[1] * t), o.dtype),
        ),
        in_specs=vmem_specs(10),
        out_specs=tuple(vmem_specs(3)),
        scratch_shapes=[
            pltpu.VMEM(kv.shape, jnp.bfloat16),
            pltpu.VMEM(kv.shape, jnp.bfloat16),
            pltpu.VMEM((stacked, HEAD_DIM), jnp.float32),
            pltpu.SemaphoreType.DMA((n,)),
            pltpu.SemaphoreType.DMA((n,)),
            pltpu.SemaphoreType.DMA((t,)),
            pltpu.SemaphoreType.DMA((t,)),
        ],
        compiler_params=pltpu.CompilerParams(collective_id=1, has_side_effects=True),
    )(q, g, o, kv, rpos, rlab, cpos, clab, m, l)


def on_device(query_rows, key_rows, value_rows, out_grad, segment_ids, span_order):
    ctx_size = lax.axis_size("ctx")
    ctx_index = lax.axis_index("ctx")
    local_rows = query_rows.shape[0]
    heads_here = query_rows.shape[1] // HEAD_DIM
    total_rows = local_rows * ctx_size
    tp_size = lax.axis_size("tp")
    kv_all, grad_rows, rpos, rlab, cpos_row, clab_row, cpos, clab = ctx_gather(
        key_rows, value_rows, out_grad, span_order, segment_ids, ctx_size, tp_size)
    attn_local, row_max, total = attention_fwd(
        query_rows, kv_all.reshape(total_rows, kv_all.shape[2]), rpos, rlab, cpos_row, clab_row)
    query_grad, reduced, attn_spread = bwd_scatter(
        query_rows, grad_rows, attn_local, kv_all, rpos, rlab, cpos, clab, row_max, total,
        ctx_size, tp_size)
    key_grad = reduced[:, :HEAD_DIM].astype(jnp.bfloat16)
    value_grad = reduced[:, HEAD_DIM:].astype(jnp.bfloat16)
    return (attn_spread, query_grad, key_grad, value_grad)


def solution(mesh):
    placed = (P("ctx", "tp"), P("ctx", "tp"), P("ctx", "tp"), P(("ctx", "tp"), None), P(), P())
    return jax.shard_map(
        on_device,
        mesh=mesh,
        in_specs=placed,
        out_specs=(P(("ctx", "tp"), None), P("ctx", "tp"), P("ctx", "tp"), P("ctx", "tp")),
        check_vma=False,
    )
```

```python
import functools
import math

import jax
import jax.numpy as jnp
from jax import lax
from jax.experimental import pallas as pl
from jax.experimental.pallas import tpu as pltpu
from jax.sharding import PartitionSpec as P

HEAD_DIM = 128
SPAN = 64
MESH = pl.DeviceIdType.MESH


CTX_SHAPE = (4, 4, 2)


def ctx_peer(me, i, n, sign):
    if n != math.prod(CTX_SHAPE):
        return lax.rem(me + sign * i + n, n)
    sx, sy, sz = CTX_SHAPE
    dz = lax.rem(i, sz)
    dx = lax.rem(i // sz, sx)
    dy = i // (sz * sx)
    x = me // (sy * sz)
    y = lax.rem(me // sz, sy)
    z = lax.rem(me, sz)
    x = lax.rem(x + sign * dx + sx, sx)
    y = lax.rem(y + sign * dy + sy, sy)
    z = lax.rem(z + sign * dz + sz, sz)
    return (x * sy + y) * sz + z


def greet_all(n, me, t=1, mt=None):
    barrier = pltpu.get_barrier_semaphore()

    def greet(i, c):
        peer = lax.rem(me + i, n)
        pl.semaphore_signal(barrier, inc=1, device_id={"ctx": peer}, device_id_type=MESH)
        return c

    def greet_tp(i, c):
        peer = lax.rem(mt + i, t)
        pl.semaphore_signal(barrier, inc=1, device_id={"tp": peer}, device_id_type=MESH)
        return c

    lax.fori_loop(1, n, greet, 0)
    if t > 1:
        lax.fori_loop(1, t, greet_tp, 0)
    pl.semaphore_wait(barrier, n - 1 + t - 1)


def tp_exchange(t, mt, src_of, dst_of, send_sem, recv_sem):
    def copy_to(peer):
        return pltpu.make_async_remote_copy(
            src_of(peer), dst_of(mt), send_sem.at[peer], recv_sem.at[mt],
            device_id={"tp": peer}, device_id_type=MESH)

    def copy_from(src):
        return pltpu.make_async_remote_copy(
            src_of(mt), dst_of(src), send_sem.at[src], recv_sem.at[src],
            device_id={"tp": src}, device_id_type=MESH)

    def start():
        def send(i, c):
            copy_to(lax.rem(mt + i, t)).start()
            return c

        lax.fori_loop(1, t, send, 0)

    def finish():
        def wait(i, c):
            copy_to(lax.rem(mt + i, t)).wait_send()
            copy_from(lax.rem(mt + t - i, t)).wait_recv()
            return c

        lax.fori_loop(1, t, wait, 0)

    return start, finish


def mask_vectors(me, heads, so_ref, seg_ref, rpos_ref, rlab_ref, cpos_ref, clab_ref, cgrid_ref, lgrid_ref):
    seg = seg_ref[...]
    prompt_end = jnp.sum(jnp.sum((seg == 0).astype(jnp.int32), axis=1, keepdims=True), axis=0, keepdims=True)
    chosen_end = jnp.sum(jnp.sum((seg <= 1).astype(jnp.int32), axis=1, keepdims=True), axis=0, keepdims=True)

    def label_of(pos):
        return (pos >= prompt_end).astype(jnp.int32) + (pos >= chosen_end).astype(jnp.int32)

    def position_of(rows):
        block = lax.shift_right_logical(rows, 6)
        start = jnp.zeros(rows.shape, jnp.int32)
        for b in range(so_ref.shape[0]):
            start = jnp.where(block == b, so_ref[b], start)
        return start * SPAN + jnp.bitwise_and(rows, SPAN - 1)

    lanes = lax.broadcasted_iota(jnp.int32, cpos_ref.shape, 1)
    cpos = position_of(lanes)
    cpos_ref[...] = cpos
    clab_ref[...] = label_of(cpos)
    grid = (lax.broadcasted_iota(jnp.int32, cgrid_ref.shape, 0) * cgrid_ref.shape[1]
            + lax.broadcasted_iota(jnp.int32, cgrid_ref.shape, 1))
    gpos = position_of(grid)
    cgrid_ref[...] = gpos
    lgrid_ref[...] = label_of(gpos)
    local = rpos_ref.shape[0] // heads
    within = jnp.bitwise_and(lax.broadcasted_iota(jnp.int32, rpos_ref.shape, 0), local - 1)
    first = so_ref[me * (local // SPAN)]
    second = so_ref[me * (local // SPAN) + 1]
    start = jnp.where(within < SPAN, first, second)
    rpos = start * SPAN + jnp.bitwise_and(within, SPAN - 1)
    rpos_ref[...] = rpos
    rlab_ref[...] = label_of(rpos)


def gather_kernel(n, t, k_ref, v_ref, og_ref, so_ref, seg_ref, out_ref, grad_ref,
                  rpos_ref, rlab_ref, cpos_ref, clab_ref, cgrid_ref, lgrid_ref,
                  send_sem, recv_sem, vsend_sem, vrecv_sem, gsend_sem, grecv_sem):
    me = lax.axis_index("ctx")
    mt = lax.axis_index("tp")
    greet_all(n, me, t, mt)
    rows = og_ref.shape[0]
    cols = grad_ref.shape[1]

    def grad_src(p):
        return og_ref.at[:, pl.ds(pl.multiple_of(p * cols, cols), cols)]

    def grad_dst(p):
        return grad_ref.at[pl.ds(pl.multiple_of(p * rows, rows), rows), :]

    grad_start, grad_finish = tp_exchange(t, mt, grad_src, grad_dst, gsend_sem, grecv_sem)
    grad_start()

    width = k_ref.shape[1]

    def copies(dst, peer, slot):
        return (
            pltpu.make_async_remote_copy(
                k_ref, out_ref.at[dst, :, :width], send_sem.at[slot], recv_sem.at[dst],
                device_id={"ctx": peer}, device_id_type=MESH),
            pltpu.make_async_remote_copy(
                v_ref, out_ref.at[dst, :, width:], vsend_sem.at[slot], vrecv_sem.at[dst],
                device_id={"ctx": peer}, device_id_type=MESH),
        )

    def send(i, c):
        peer = ctx_peer(me, i, n, 1)
        for copy in copies(me, peer, peer):
            copy.start()
        return c

    lax.fori_loop(1, n, send, 0)
    out_ref[me, :, :width] = k_ref[...]
    out_ref[me, :, width:] = v_ref[...]
    mask_vectors(me, grad_ref.shape[1] // HEAD_DIM, so_ref, seg_ref,
                 rpos_ref, rlab_ref, cpos_ref, clab_ref, cgrid_ref, lgrid_ref)
    grad_ref[pl.ds(pl.multiple_of(mt * rows, rows), rows), :] = og_ref[
        :, pl.ds(pl.multiple_of(mt * cols, cols), cols)]

    def wait(i, c):
        peer = ctx_peer(me, i, n, 1)
        for copy in copies(me, peer, peer):
            copy.wait_send()
        src = ctx_peer(me, i, n, -1)
        for copy in copies(src, src, src):
            copy.wait_recv()
        return c

    lax.fori_loop(1, n, wait, 0)
    grad_finish()


def ctx_gather(key_rows, value_rows, out_grad, span_order, segment_ids, n, t):
    rows = key_rows.shape[0]
    width = key_rows.shape[1] + value_rows.shape[1]
    grad_shape = (out_grad.shape[0] * t, out_grad.shape[1] // t)
    stacked = rows * (grad_shape[1] // HEAD_DIM)
    seg = segment_ids.reshape(n, segment_ids.shape[0] // n)
    column = jax.ShapeDtypeStruct((1, n * rows), jnp.int32)
    row = jax.ShapeDtypeStruct((stacked, 1), jnp.int32)
    grid = jax.ShapeDtypeStruct((n, rows), jnp.int32)
    return pl.pallas_call(
        functools.partial(gather_kernel, n, t),
        out_shape=(
            jax.ShapeDtypeStruct((n, rows, width), key_rows.dtype),
            jax.ShapeDtypeStruct(grad_shape, out_grad.dtype),
            row, row, column, column, grid, grid,
        ),
        in_specs=[pl.BlockSpec(memory_space=pltpu.VMEM)] * 3
        + [pl.BlockSpec(memory_space=pltpu.SMEM), pl.BlockSpec(memory_space=pltpu.VMEM)],
        out_specs=(pl.BlockSpec(memory_space=pltpu.VMEM),) * 8,
        scratch_shapes=[pltpu.SemaphoreType.DMA((n,))] * 4 + [pltpu.SemaphoreType.DMA((t,))] * 2,
        compiler_params=pltpu.CompilerParams(collective_id=0, has_side_effects=True),
    )(key_rows, value_rows, out_grad, span_order, seg)


KEY_BLOCK = 1024
FWD_GROUP = 8
NT_DIMS = (((1,), (1,)), ((), ()))
TN_DIMS = (((0,), (0,)), ((), ()))


def stack_heads(ref):
    heads = ref.shape[1] // HEAD_DIM
    return jnp.concatenate([ref[:, h * HEAD_DIM:(h + 1) * HEAD_DIM] for h in range(heads)], axis=0)


def unstack_heads(ref, value):
    rows = ref.shape[0]
    for h in range(ref.shape[1] // HEAD_DIM):
        ref[:, h * HEAD_DIM:(h + 1) * HEAD_DIM] = value[h * rows:(h + 1) * rows]


def key_block(kv_ref, cpos_ref, clab_ref, rpos, rlab, kb):
    size = min(KEY_BLOCK, kv_ref.shape[0])
    start = pl.multiple_of(kb * size, size)
    keys = kv_ref[pl.ds(start, size), :HEAD_DIM]
    values = kv_ref[pl.ds(start, size), HEAD_DIM:]
    cpos = cpos_ref[:, pl.ds(start, size)]
    clab = clab_ref[:, pl.ds(start, size)]
    visible = (cpos <= rpos) & ((clab == 0) | (clab == rlab))
    return start, keys, values, visible


def fwd_kernel(q_ref, kv_ref, rpos_ref, rlab_ref, cpos_ref, clab_ref, o_ref, m_ref, l_ref, acc_sc):
    scale = 1.0 / math.sqrt(HEAD_DIM)
    queries = stack_heads(q_ref)
    rpos = rpos_ref[...]
    rlab = rlab_ref[...]
    m_ref[...] = jnp.full(m_ref.shape, -jnp.inf, jnp.float32)
    l_ref[...] = jnp.zeros(l_ref.shape, jnp.float32)
    acc_sc[...] = jnp.zeros(acc_sc.shape, jnp.float32)

    def body(kb, c):
        _, keys, values, visible = key_block(kv_ref, cpos_ref, clab_ref, rpos, rlab, kb)
        scores = lax.dot_general(queries, keys, NT_DIMS, preferred_element_type=jnp.float32) * scale
        scores = jnp.where(visible, scores, -jnp.inf)
        running = m_ref[...]
        new_max = jnp.maximum(running, jnp.max(scores, axis=-1, keepdims=True))
        shift = jnp.where(new_max == -jnp.inf, 0.0, new_max)
        factor = jnp.exp(running - shift)
        weights = jnp.exp(scores - shift)
        l_ref[...] = l_ref[...] * factor + jnp.sum(weights, axis=-1, keepdims=True)
        acc_sc[...] = acc_sc[...] * factor + jnp.dot(
            weights.astype(jnp.bfloat16), values, preferred_element_type=jnp.float32)
        m_ref[...] = new_max
        return c

    lax.fori_loop(0, kv_ref.shape[0] // min(KEY_BLOCK, kv_ref.shape[0]), body, 0)
    unstack_heads(o_ref, (acc_sc[...] / l_ref[...]).astype(o_ref.dtype))


def vmem_specs(n):
    return [pl.BlockSpec(memory_space=pltpu.VMEM)] * n


def attention_fwd(q, kv, rpos, rlab, cpos, clab):
    stacked = rpos.shape[0]
    return pl.pallas_call(
        fwd_kernel,
        out_shape=(
            jax.ShapeDtypeStruct(q.shape, jnp.bfloat16),
            jax.ShapeDtypeStruct((stacked, 1), jnp.float32),
            jax.ShapeDtypeStruct((stacked, 1), jnp.float32),
        ),
        in_specs=vmem_specs(6),
        out_specs=tuple(vmem_specs(3)),
        scratch_shapes=[pltpu.VMEM((stacked, HEAD_DIM), jnp.float32)],
    )(q, kv, rpos, rlab, cpos, clab)


def column_visible(cpos_ref, clab_ref, block, rpos, rlab):
    cpos = cpos_ref[pl.ds(block, 1), :]
    clab = clab_ref[pl.ds(block, 1), :]
    return (cpos <= rpos) & ((clab == 0) | (clab == rlab))


def fwd_groups(n, queries, kv_ref, cpos_ref, clab_ref, rpos, rlab, m_ref, l_ref, acc_sc, o_ref):
    scale = 1.0 / math.sqrt(HEAD_DIM)
    group = math.gcd(n, FWD_GROUP)
    m_ref[...] = jnp.full(m_ref.shape, -jnp.inf, jnp.float32)
    l_ref[...] = jnp.zeros(l_ref.shape, jnp.float32)
    acc_sc[...] = jnp.zeros(acc_sc.shape, jnp.float32)

    def body(j, c):
        first = j * group
        block = jnp.concatenate([kv_ref[first + b] for b in range(group)], axis=0)
        cpos = jnp.concatenate([cpos_ref[pl.ds(first + b, 1), :] for b in range(group)], axis=1)
        clab = jnp.concatenate([clab_ref[pl.ds(first + b, 1), :] for b in range(group)], axis=1)
        visible = (cpos <= rpos) & ((clab == 0) | (clab == rlab))
        keys = block[:, :HEAD_DIM]
        values = block[:, HEAD_DIM:]
        scores = lax.dot_general(queries, keys, NT_DIMS, preferred_element_type=jnp.float32) * scale
        scores = jnp.where(visible, scores, -jnp.inf)
        running = m_ref[...]
        new_max = jnp.maximum(running, jnp.max(scores, axis=-1, keepdims=True))
        shift = jnp.where(new_max == -jnp.inf, 0.0, new_max)
        factor = jnp.exp(running - shift)
        weights = jnp.exp(scores - shift)
        l_ref[...] = l_ref[...] * factor + jnp.sum(weights, axis=-1, keepdims=True)
        acc_sc[...] = acc_sc[...] * factor + jnp.dot(
            weights.astype(jnp.bfloat16), values, preferred_element_type=jnp.float32)
        m_ref[...] = new_max
        return c

    lax.fori_loop(0, n // group, body, 0)
    unstack_heads(o_ref, (acc_sc[...] / l_ref[...]).astype(o_ref.dtype))


def bwd_scatter_kernel(n, t, q_ref, g_ref, kv_ref, rpos_ref, rlab_ref, cpos_ref, clab_ref,
                       dq_ref, red_ref, spread_ref, o_ref, m_ref, l_ref, terms_sc, held, dq_sc,
                       send_sem, recv_sem, osend_sem, orecv_sem):
    me = lax.axis_index("ctx")
    mt = lax.axis_index("tp")
    greet_all(n, me, t, mt)
    fwd_groups(n, stack_heads(q_ref), kv_ref, cpos_ref, clab_ref, rpos_ref[...], rlab_ref[...],
               m_ref, l_ref, dq_sc, o_ref)
    rows = spread_ref.shape[0]
    cols = o_ref.shape[1]

    def out_src(p):
        return o_ref.at[pl.ds(pl.multiple_of(p * rows, rows), rows), :]

    def out_dst(p):
        return spread_ref.at[:, pl.ds(pl.multiple_of(p * cols, cols), cols)]

    out_start, out_finish = tp_exchange(t, mt, out_src, out_dst, osend_sem, orecv_sem)
    out_start()
    spread_ref[:, pl.ds(pl.multiple_of(mt * cols, cols), cols)] = o_ref[
        pl.ds(pl.multiple_of(mt * rows, rows), rows), :]
    scale = 1.0 / math.sqrt(HEAD_DIM)
    queries = stack_heads(q_ref)
    grads = stack_heads(g_ref)
    outs = stack_heads(o_ref)
    delta = jnp.sum(grads.astype(jnp.float32) * outs.astype(jnp.float32), axis=-1, keepdims=True)
    rpos = rpos_ref[...]
    rlab = rlab_ref[...]
    row_max = m_ref[...]
    inv_total = 1.0 / l_ref[...]
    dq_sc[...] = jnp.zeros(dq_sc.shape, jnp.float32)

    def copy_to(peer):
        return pltpu.make_async_remote_copy(
            terms_sc.at[peer], held.at[me], send_sem.at[peer], recv_sem.at[me],
            device_id={"ctx": peer}, device_id_type=MESH)

    def copy_from(src):
        return pltpu.make_async_remote_copy(
            terms_sc.at[src], held.at[src], send_sem.at[src], recv_sem.at[src],
            device_id={"ctx": src}, device_id_type=MESH)

    def block_terms(p):
        block = kv_ref[p]
        keys = block[:, :HEAD_DIM]
        values = block[:, HEAD_DIM:]
        visible = column_visible(cpos_ref, clab_ref, p, rpos, rlab)
        scores = lax.dot_general(queries, keys, NT_DIMS, preferred_element_type=jnp.float32) * scale
        probs = jnp.where(visible, jnp.exp(scores - row_max), 0.0) * inv_total
        dprob = lax.dot_general(grads, values, NT_DIMS, preferred_element_type=jnp.float32)
        dscore_b = (probs * (dprob - delta)).astype(jnp.bfloat16)
        probs_b = probs.astype(jnp.bfloat16)
        dq_sc[...] += jnp.dot(dscore_b, keys, preferred_element_type=jnp.float32)
        key_term = lax.dot_general(dscore_b, queries, TN_DIMS, preferred_element_type=jnp.float32) * scale
        value_term = lax.dot_general(probs_b, grads, TN_DIMS, preferred_element_type=jnp.float32)
        return jnp.concatenate([key_term, value_term], axis=1)

    red_ref[...] = block_terms(me)

    def step(i, c):
        peer = ctx_peer(me, i, n, 1)
        terms_sc[peer] = block_terms(peer).astype(terms_sc.dtype)

        @pl.when(i >= 2)
        def _():
            copy_to(ctx_peer(me, i - 1, n, 1)).start()

        return c

    lax.fori_loop(1, n, step, 0)
    copy_to(ctx_peer(me, n - 1, n, 1)).start()
    unstack_heads(dq_ref, (dq_sc[...] * scale).astype(dq_ref.dtype))

    def arrive(i, c):
        src = ctx_peer(me, i, n, -1)
        copy_from(src).wait_recv()
        red_ref[...] += held[src].astype(jnp.float32)
        return c

    lax.fori_loop(1, n, arrive, 0)

    def drain(i, c):
        copy_to(ctx_peer(me, i, n, 1)).wait_send()
        return c

    lax.fori_loop(1, n, drain, 0)
    out_finish()


def bwd_scatter(q, g, kv, rpos, rlab, cpos, clab, n, t):
    _, rows, width = kv.shape
    stacked = rpos.shape[0]
    return pl.pallas_call(
        functools.partial(bwd_scatter_kernel, n, t),
        out_shape=(
            jax.ShapeDtypeStruct(q.shape, jnp.bfloat16),
            jax.ShapeDtypeStruct((rows, width), jnp.float32),
            jax.ShapeDtypeStruct((q.shape[0] // t, q.shape[1] * t), jnp.bfloat16),
        ),
        in_specs=vmem_specs(7),
        out_specs=tuple(vmem_specs(3)),
        scratch_shapes=[
            pltpu.VMEM(q.shape, jnp.bfloat16),
            pltpu.VMEM((stacked, 1), jnp.float32),
            pltpu.VMEM((stacked, 1), jnp.float32),
            pltpu.VMEM(kv.shape, jnp.bfloat16),
            pltpu.VMEM(kv.shape, jnp.bfloat16),
            pltpu.VMEM((stacked, HEAD_DIM), jnp.float32),
            pltpu.SemaphoreType.DMA((n,)),
            pltpu.SemaphoreType.DMA((n,)),
            pltpu.SemaphoreType.DMA((t,)),
            pltpu.SemaphoreType.DMA((t,)),
        ],
        compiler_params=pltpu.CompilerParams(collective_id=1, has_side_effects=True),
    )(q, g, kv, rpos, rlab, cpos, clab)


def on_device(query_rows, key_rows, value_rows, out_grad, segment_ids, span_order):
    ctx_size = lax.axis_size("ctx")
    ctx_index = lax.axis_index("ctx")
    local_rows = query_rows.shape[0]
    heads_here = query_rows.shape[1] // HEAD_DIM
    total_rows = local_rows * ctx_size
    tp_size = lax.axis_size("tp")
    kv_all, grad_rows, rpos, rlab, cpos_row, clab_row, cpos, clab = ctx_gather(
        key_rows, value_rows, out_grad, span_order, segment_ids, ctx_size, tp_size)
    query_grad, reduced, attn_spread = bwd_scatter(
        query_rows, grad_rows, kv_all, rpos, rlab, cpos, clab, ctx_size, tp_size)
    key_grad = reduced[:, :HEAD_DIM].astype(jnp.bfloat16)
    value_grad = reduced[:, HEAD_DIM:].astype(jnp.bfloat16)
    return (attn_spread, query_grad, key_grad, value_grad)


def solution(mesh):
    placed = (P("ctx", "tp"), P("ctx", "tp"), P("ctx", "tp"), P(("ctx", "tp"), None), P(), P())
    return jax.shard_map(
        on_device,
        mesh=mesh,
        in_specs=placed,
        out_specs=(P(("ctx", "tp"), None), P("ctx", "tp"), P("ctx", "tp"), P("ctx", "tp")),
        check_vma=False,
    )
```

```python
import functools
import math

import jax
import jax.numpy as jnp
from jax import lax
from jax.experimental import pallas as pl
from jax.experimental.pallas import tpu as pltpu
from jax.sharding import PartitionSpec as P

HEAD_DIM = 128
SPAN = 64
MESH = pl.DeviceIdType.MESH


CTX_SHAPE = (4, 4, 2)


def ctx_peer(me, i, n, sign):
    if n != math.prod(CTX_SHAPE):
        return lax.rem(me + sign * i + n, n)
    sx, sy, sz = CTX_SHAPE
    dz = lax.rem(i, sz)
    dx = lax.rem(i // sz, sx)
    dy = i // (sz * sx)
    x = me // (sy * sz)
    y = lax.rem(me // sz, sy)
    z = lax.rem(me, sz)
    x = lax.rem(x + sign * dx + sx, sx)
    y = lax.rem(y + sign * dy + sy, sy)
    z = lax.rem(z + sign * dz + sz, sz)
    return (x * sy + y) * sz + z


def greet_all(n, me, t=1, mt=None):
    barrier = pltpu.get_barrier_semaphore()

    def greet(i, c):
        peer = lax.rem(me + i, n)
        pl.semaphore_signal(barrier, inc=1, device_id={"ctx": peer}, device_id_type=MESH)
        return c

    def greet_tp(i, c):
        peer = lax.rem(mt + i, t)
        pl.semaphore_signal(barrier, inc=1, device_id={"tp": peer}, device_id_type=MESH)
        return c

    lax.fori_loop(1, n, greet, 0)
    if t > 1:
        lax.fori_loop(1, t, greet_tp, 0)
    pl.semaphore_wait(barrier, n - 1 + t - 1)


def tp_exchange(t, mt, src_of, dst_of, send_sem, recv_sem):
    def copy_to(peer):
        return pltpu.make_async_remote_copy(
            src_of(peer), dst_of(mt), send_sem.at[peer], recv_sem.at[mt],
            device_id={"tp": peer}, device_id_type=MESH)

    def copy_from(src):
        return pltpu.make_async_remote_copy(
            src_of(mt), dst_of(src), send_sem.at[src], recv_sem.at[src],
            device_id={"tp": src}, device_id_type=MESH)

    def start():
        def send(i, c):
            copy_to(lax.rem(mt + i, t)).start()
            return c

        lax.fori_loop(1, t, send, 0)

    def finish():
        def wait(i, c):
            copy_to(lax.rem(mt + i, t)).wait_send()
            copy_from(lax.rem(mt + t - i, t)).wait_recv()
            return c

        lax.fori_loop(1, t, wait, 0)

    return start, finish


def mask_vectors(me, heads, so_ref, seg_ref, rpos_ref, rlab_ref, cpos_ref, clab_ref, cgrid_ref, lgrid_ref):
    seg = seg_ref[...]
    prompt_end = jnp.sum(jnp.sum((seg == 0).astype(jnp.int32), axis=1, keepdims=True), axis=0, keepdims=True)
    chosen_end = jnp.sum(jnp.sum((seg <= 1).astype(jnp.int32), axis=1, keepdims=True), axis=0, keepdims=True)

    def label_of(pos):
        return (pos >= prompt_end).astype(jnp.int32) + (pos >= chosen_end).astype(jnp.int32)

    def position_of(rows):
        block = lax.shift_right_logical(rows, 6)
        start = jnp.zeros(rows.shape, jnp.int32)
        for b in range(so_ref.shape[0]):
            start = jnp.where(block == b, so_ref[b], start)
        return start * SPAN + jnp.bitwise_and(rows, SPAN - 1)

    lanes = lax.broadcasted_iota(jnp.int32, cpos_ref.shape, 1)
    cpos = position_of(lanes)
    cpos_ref[...] = cpos
    clab_ref[...] = label_of(cpos)
    grid = (lax.broadcasted_iota(jnp.int32, cgrid_ref.shape, 0) * cgrid_ref.shape[1]
            + lax.broadcasted_iota(jnp.int32, cgrid_ref.shape, 1))
    gpos = position_of(grid)
    cgrid_ref[...] = gpos
    lgrid_ref[...] = label_of(gpos)
    local = rpos_ref.shape[0] // heads
    within = jnp.bitwise_and(lax.broadcasted_iota(jnp.int32, rpos_ref.shape, 0), local - 1)
    first = so_ref[me * (local // SPAN)]
    second = so_ref[me * (local // SPAN) + 1]
    start = jnp.where(within < SPAN, first, second)
    rpos = start * SPAN + jnp.bitwise_and(within, SPAN - 1)
    rpos_ref[...] = rpos
    rlab_ref[...] = label_of(rpos)


def gather_kernel(n, t, k_ref, v_ref, og_ref, so_ref, seg_ref, out_ref, grad_ref,
                  rpos_ref, rlab_ref, cpos_ref, clab_ref, cgrid_ref, lgrid_ref,
                  send_sem, recv_sem, vsend_sem, vrecv_sem, gsend_sem, grecv_sem):
    me = lax.axis_index("ctx")
    mt = lax.axis_index("tp")
    greet_all(n, me, t, mt)
    rows = og_ref.shape[0]
    cols = grad_ref.shape[1]

    def grad_src(p):
        return og_ref.at[:, pl.ds(pl.multiple_of(p * cols, cols), cols)]

    def grad_dst(p):
        return grad_ref.at[pl.ds(pl.multiple_of(p * rows, rows), rows), :]

    grad_start, grad_finish = tp_exchange(t, mt, grad_src, grad_dst, gsend_sem, grecv_sem)
    grad_start()

    width = k_ref.shape[1]

    def copies(dst, peer, slot):
        return (
            pltpu.make_async_remote_copy(
                k_ref, out_ref.at[dst, :, :width], send_sem.at[slot], recv_sem.at[dst],
                device_id={"ctx": peer}, device_id_type=MESH),
            pltpu.make_async_remote_copy(
                v_ref, out_ref.at[dst, :, width:], vsend_sem.at[slot], vrecv_sem.at[dst],
                device_id={"ctx": peer}, device_id_type=MESH),
        )

    def send(i, c):
        peer = ctx_peer(me, i, n, 1)
        for copy in copies(me, peer, peer):
            copy.start()
        return c

    lax.fori_loop(1, n, send, 0)
    out_ref[me, :, :width] = k_ref[...]
    out_ref[me, :, width:] = v_ref[...]
    mask_vectors(me, grad_ref.shape[1] // HEAD_DIM, so_ref, seg_ref,
                 rpos_ref, rlab_ref, cpos_ref, clab_ref, cgrid_ref, lgrid_ref)
    grad_ref[pl.ds(pl.multiple_of(mt * rows, rows), rows), :] = og_ref[
        :, pl.ds(pl.multiple_of(mt * cols, cols), cols)]

    def wait(i, c):
        peer = ctx_peer(me, i, n, 1)
        for copy in copies(me, peer, peer):
            copy.wait_send()
        src = ctx_peer(me, i, n, -1)
        for copy in copies(src, src, src):
            copy.wait_recv()
        return c

    lax.fori_loop(1, n, wait, 0)
    grad_finish()


def ctx_gather(key_rows, value_rows, out_grad, span_order, segment_ids, n, t):
    rows = key_rows.shape[0]
    width = key_rows.shape[1] + value_rows.shape[1]
    grad_shape = (out_grad.shape[0] * t, out_grad.shape[1] // t)
    stacked = rows * (grad_shape[1] // HEAD_DIM)
    seg = segment_ids.reshape(n, segment_ids.shape[0] // n)
    column = jax.ShapeDtypeStruct((1, n * rows), jnp.int32)
    row = jax.ShapeDtypeStruct((stacked, 1), jnp.int32)
    grid = jax.ShapeDtypeStruct((n, rows), jnp.int32)
    return pl.pallas_call(
        functools.partial(gather_kernel, n, t),
        out_shape=(
            jax.ShapeDtypeStruct((n, rows, width), key_rows.dtype),
            jax.ShapeDtypeStruct(grad_shape, out_grad.dtype),
            row, row, column, column, grid, grid,
        ),
        in_specs=[pl.BlockSpec(memory_space=pltpu.VMEM)] * 3
        + [pl.BlockSpec(memory_space=pltpu.SMEM), pl.BlockSpec(memory_space=pltpu.VMEM)],
        out_specs=(pl.BlockSpec(memory_space=pltpu.VMEM),) * 8,
        scratch_shapes=[pltpu.SemaphoreType.DMA((n,))] * 4 + [pltpu.SemaphoreType.DMA((t,))] * 2,
        compiler_params=pltpu.CompilerParams(collective_id=0, has_side_effects=True),
    )(key_rows, value_rows, out_grad, span_order, seg)


KEY_BLOCK = 1024
FWD_GROUP = 8
NT_DIMS = (((1,), (1,)), ((), ()))
TN_DIMS = (((0,), (0,)), ((), ()))


def stack_heads(ref):
    heads = ref.shape[1] // HEAD_DIM
    return jnp.concatenate([ref[:, h * HEAD_DIM:(h + 1) * HEAD_DIM] for h in range(heads)], axis=0)


def unstack_heads(ref, value):
    rows = ref.shape[0]
    for h in range(ref.shape[1] // HEAD_DIM):
        ref[:, h * HEAD_DIM:(h + 1) * HEAD_DIM] = value[h * rows:(h + 1) * rows]


def key_block(kv_ref, cpos_ref, clab_ref, rpos, rlab, kb):
    size = min(KEY_BLOCK, kv_ref.shape[0])
    start = pl.multiple_of(kb * size, size)
    keys = kv_ref[pl.ds(start, size), :HEAD_DIM]
    values = kv_ref[pl.ds(start, size), HEAD_DIM:]
    cpos = cpos_ref[:, pl.ds(start, size)]
    clab = clab_ref[:, pl.ds(start, size)]
    visible = (cpos <= rpos) & ((clab == 0) | (clab == rlab))
    return start, keys, values, visible


def fwd_kernel(q_ref, kv_ref, rpos_ref, rlab_ref, cpos_ref, clab_ref, o_ref, m_ref, l_ref, acc_sc):
    scale = 1.0 / math.sqrt(HEAD_DIM)
    queries = stack_heads(q_ref)
    rpos = rpos_ref[...]
    rlab = rlab_ref[...]
    m_ref[...] = jnp.full(m_ref.shape, -jnp.inf, jnp.float32)
    l_ref[...] = jnp.zeros(l_ref.shape, jnp.float32)
    acc_sc[...] = jnp.zeros(acc_sc.shape, jnp.float32)

    def body(kb, c):
        _, keys, values, visible = key_block(kv_ref, cpos_ref, clab_ref, rpos, rlab, kb)
        scores = lax.dot_general(queries, keys, NT_DIMS, preferred_element_type=jnp.float32) * scale
        scores = jnp.where(visible, scores, -jnp.inf)
        running = m_ref[...]
        new_max = jnp.maximum(running, jnp.max(scores, axis=-1, keepdims=True))
        shift = jnp.where(new_max == -jnp.inf, 0.0, new_max)
        factor = jnp.exp(running - shift)
        weights = jnp.exp(scores - shift)
        l_ref[...] = l_ref[...] * factor + jnp.sum(weights, axis=-1, keepdims=True)
        acc_sc[...] = acc_sc[...] * factor + jnp.dot(
            weights.astype(jnp.bfloat16), values, preferred_element_type=jnp.float32)
        m_ref[...] = new_max
        return c

    lax.fori_loop(0, kv_ref.shape[0] // min(KEY_BLOCK, kv_ref.shape[0]), body, 0)
    unstack_heads(o_ref, (acc_sc[...] / l_ref[...]).astype(o_ref.dtype))


def vmem_specs(n):
    return [pl.BlockSpec(memory_space=pltpu.VMEM)] * n


def attention_fwd(q, kv, rpos, rlab, cpos, clab):
    stacked = rpos.shape[0]
    return pl.pallas_call(
        fwd_kernel,
        out_shape=(
            jax.ShapeDtypeStruct(q.shape, jnp.bfloat16),
            jax.ShapeDtypeStruct((stacked, 1), jnp.float32),
            jax.ShapeDtypeStruct((stacked, 1), jnp.float32),
        ),
        in_specs=vmem_specs(6),
        out_specs=tuple(vmem_specs(3)),
        scratch_shapes=[pltpu.VMEM((stacked, HEAD_DIM), jnp.float32)],
    )(q, kv, rpos, rlab, cpos, clab)


def column_visible(cpos_ref, clab_ref, block, rpos, rlab):
    cpos = cpos_ref[pl.ds(block, 1), :]
    clab = clab_ref[pl.ds(block, 1), :]
    return (cpos <= rpos) & ((clab == 0) | (clab == rlab))


def fwd_groups(n, queries, kv_ref, cpos_ref, clab_ref, rpos, rlab, m_ref, l_ref, acc_sc, o_ref):
    scale = 1.0 / math.sqrt(HEAD_DIM)
    group = math.gcd(n, FWD_GROUP)
    m_ref[...] = jnp.full(m_ref.shape, -jnp.inf, jnp.float32)
    l_ref[...] = jnp.zeros(l_ref.shape, jnp.float32)
    acc_sc[...] = jnp.zeros(acc_sc.shape, jnp.float32)

    def body(j, c):
        first = j * group
        block = jnp.concatenate([kv_ref[first + b] for b in range(group)], axis=0)
        cpos = jnp.concatenate([cpos_ref[pl.ds(first + b, 1), :] for b in range(group)], axis=1)
        clab = jnp.concatenate([clab_ref[pl.ds(first + b, 1), :] for b in range(group)], axis=1)
        visible = (cpos <= rpos) & ((clab == 0) | (clab == rlab))
        keys = block[:, :HEAD_DIM]
        values = block[:, HEAD_DIM:]
        scores = lax.dot_general(queries, keys, NT_DIMS, preferred_element_type=jnp.float32) * scale
        scores = jnp.where(visible, scores, -jnp.inf)
        running = m_ref[...]
        new_max = jnp.maximum(running, jnp.max(scores, axis=-1, keepdims=True))
        shift = jnp.where(new_max == -jnp.inf, 0.0, new_max)
        factor = jnp.exp(running - shift)
        weights = jnp.exp(scores - shift)
        l_ref[...] = l_ref[...] * factor + jnp.sum(weights, axis=-1, keepdims=True)
        acc_sc[...] = acc_sc[...] * factor + jnp.dot(
            weights.astype(jnp.bfloat16), values, preferred_element_type=jnp.float32)
        m_ref[...] = new_max
        return c

    lax.fori_loop(0, n // group, body, 0)
    unstack_heads(o_ref, (acc_sc[...] / l_ref[...]).astype(o_ref.dtype))


def bwd_scatter_kernel(n, t, q_ref, g_ref, kv_ref, rpos_ref, rlab_ref, cpos_ref, clab_ref,
                       dq_ref, kg_ref, vg_ref, spread_ref, o_ref, m_ref, l_ref, red_ref, terms_sc, held, dq_sc,
                       send_sem, recv_sem, osend_sem, orecv_sem):
    me = lax.axis_index("ctx")
    mt = lax.axis_index("tp")
    greet_all(n, me, t, mt)
    fwd_groups(n, stack_heads(q_ref), kv_ref, cpos_ref, clab_ref, rpos_ref[...], rlab_ref[...],
               m_ref, l_ref, dq_sc, o_ref)
    rows = spread_ref.shape[0]
    cols = o_ref.shape[1]

    def out_src(p):
        return o_ref.at[pl.ds(pl.multiple_of(p * rows, rows), rows), :]

    def out_dst(p):
        return spread_ref.at[:, pl.ds(pl.multiple_of(p * cols, cols), cols)]

    out_start, out_finish = tp_exchange(t, mt, out_src, out_dst, osend_sem, orecv_sem)
    out_start()
    spread_ref[:, pl.ds(pl.multiple_of(mt * cols, cols), cols)] = o_ref[
        pl.ds(pl.multiple_of(mt * rows, rows), rows), :]
    scale = 1.0 / math.sqrt(HEAD_DIM)
    queries = stack_heads(q_ref)
    grads = stack_heads(g_ref)
    outs = stack_heads(o_ref)
    delta = jnp.sum(grads.astype(jnp.float32) * outs.astype(jnp.float32), axis=-1, keepdims=True)
    rpos = rpos_ref[...]
    rlab = rlab_ref[...]
    row_max = m_ref[...]
    inv_total = 1.0 / l_ref[...]
    dq_sc[...] = jnp.zeros(dq_sc.shape, jnp.float32)

    def copy_to(peer):
        return pltpu.make_async_remote_copy(
            terms_sc.at[peer], held.at[me], send_sem.at[peer], recv_sem.at[me],
            device_id={"ctx": peer}, device_id_type=MESH)

    def copy_from(src):
        return pltpu.make_async_remote_copy(
            terms_sc.at[src], held.at[src], send_sem.at[src], recv_sem.at[src],
            device_id={"ctx": src}, device_id_type=MESH)

    def block_terms(p):
        block = kv_ref[p]
        keys = block[:, :HEAD_DIM]
        values = block[:, HEAD_DIM:]
        visible = column_visible(cpos_ref, clab_ref, p, rpos, rlab)
        scores = lax.dot_general(queries, keys, NT_DIMS, preferred_element_type=jnp.float32) * scale
        probs = jnp.where(visible, jnp.exp(scores - row_max), 0.0) * inv_total
        dprob = lax.dot_general(grads, values, NT_DIMS, preferred_element_type=jnp.float32)
        dscore_b = (probs * (dprob - delta)).astype(jnp.bfloat16)
        probs_b = probs.astype(jnp.bfloat16)
        dq_sc[...] += jnp.dot(dscore_b, keys, preferred_element_type=jnp.float32)
        key_term = lax.dot_general(dscore_b, queries, TN_DIMS, preferred_element_type=jnp.float32) * scale
        value_term = lax.dot_general(probs_b, grads, TN_DIMS, preferred_element_type=jnp.float32)
        return jnp.concatenate([key_term, value_term], axis=1)

    red_ref[...] = block_terms(me)

    def step(i, c):
        peer = ctx_peer(me, i, n, 1)
        terms_sc[peer] = block_terms(peer).astype(terms_sc.dtype)

        @pl.when(i >= 2)
        def _():
            copy_to(ctx_peer(me, i - 1, n, 1)).start()

        return c

    lax.fori_loop(1, n, step, 0)
    copy_to(ctx_peer(me, n - 1, n, 1)).start()
    unstack_heads(dq_ref, (dq_sc[...] * scale).astype(dq_ref.dtype))

    def arrive(i, c):
        src = ctx_peer(me, i, n, -1)
        copy_from(src).wait_recv()
        red_ref[...] += held[src].astype(jnp.float32)
        return c

    lax.fori_loop(1, n, arrive, 0)
    kg_ref[...] = red_ref[:, :HEAD_DIM].astype(kg_ref.dtype)
    vg_ref[...] = red_ref[:, HEAD_DIM:].astype(vg_ref.dtype)

    def drain(i, c):
        copy_to(ctx_peer(me, i, n, 1)).wait_send()
        return c

    lax.fori_loop(1, n, drain, 0)
    out_finish()


def bwd_scatter(q, g, kv, rpos, rlab, cpos, clab, n, t):
    _, rows, width = kv.shape
    stacked = rpos.shape[0]
    return pl.pallas_call(
        functools.partial(bwd_scatter_kernel, n, t),
        out_shape=(
            jax.ShapeDtypeStruct(q.shape, jnp.bfloat16),
            jax.ShapeDtypeStruct((rows, HEAD_DIM), jnp.bfloat16),
            jax.ShapeDtypeStruct((rows, width - HEAD_DIM), jnp.bfloat16),
            jax.ShapeDtypeStruct((q.shape[0] // t, q.shape[1] * t), jnp.bfloat16),
        ),
        in_specs=vmem_specs(7),
        out_specs=tuple(vmem_specs(4)),
        scratch_shapes=[
            pltpu.VMEM(q.shape, jnp.bfloat16),
            pltpu.VMEM((stacked, 1), jnp.float32),
            pltpu.VMEM((stacked, 1), jnp.float32),
            pltpu.VMEM((rows, width), jnp.float32),
            pltpu.VMEM(kv.shape, jnp.bfloat16),
            pltpu.VMEM(kv.shape, jnp.bfloat16),
            pltpu.VMEM((stacked, HEAD_DIM), jnp.float32),
            pltpu.SemaphoreType.DMA((n,)),
            pltpu.SemaphoreType.DMA((n,)),
            pltpu.SemaphoreType.DMA((t,)),
            pltpu.SemaphoreType.DMA((t,)),
        ],
        compiler_params=pltpu.CompilerParams(collective_id=1, has_side_effects=True),
    )(q, g, kv, rpos, rlab, cpos, clab)


def on_device(query_rows, key_rows, value_rows, out_grad, segment_ids, span_order):
    ctx_size = lax.axis_size("ctx")
    ctx_index = lax.axis_index("ctx")
    local_rows = query_rows.shape[0]
    heads_here = query_rows.shape[1] // HEAD_DIM
    total_rows = local_rows * ctx_size
    tp_size = lax.axis_size("tp")
    kv_all, grad_rows, rpos, rlab, cpos_row, clab_row, cpos, clab = ctx_gather(
        key_rows, value_rows, out_grad, span_order, segment_ids, ctx_size, tp_size)
    query_grad, key_grad, value_grad, attn_spread = bwd_scatter(
        query_rows, grad_rows, kv_all, rpos, rlab, cpos, clab, ctx_size, tp_size)
    return (attn_spread, query_grad, key_grad, value_grad)


def solution(mesh):
    placed = (P("ctx", "tp"), P("ctx", "tp"), P("ctx", "tp"), P(("ctx", "tp"), None), P(), P())
    return jax.shard_map(
        on_device,
        mesh=mesh,
        in_specs=placed,
        out_specs=(P(("ctx", "tp"), None), P("ctx", "tp"), P("ctx", "tp"), P("ctx", "tp")),
        check_vma=False,
    )
```

```python
import functools
import math

import jax
import jax.numpy as jnp
from jax import lax
from jax.experimental import pallas as pl
from jax.experimental.pallas import tpu as pltpu
from jax.sharding import PartitionSpec as P

HEAD_DIM = 128
SPAN = 64
MESH = pl.DeviceIdType.MESH


CTX_SHAPE = (4, 4, 2)


def ctx_peer(me, i, n, sign):
    if n != math.prod(CTX_SHAPE):
        return lax.rem(me + sign * i + n, n)
    sx, sy, sz = CTX_SHAPE
    dz = lax.rem(i, sz)
    dx = lax.rem(i // sz, sx)
    dy = i // (sz * sx)
    x = me // (sy * sz)
    y = lax.rem(me // sz, sy)
    z = lax.rem(me, sz)
    x = lax.rem(x + sign * dx + sx, sx)
    y = lax.rem(y + sign * dy + sy, sy)
    z = lax.rem(z + sign * dz + sz, sz)
    return (x * sy + y) * sz + z


def greet_all(n, me, t=1, mt=None):
    barrier = pltpu.get_barrier_semaphore()

    def greet(i, c):
        peer = lax.rem(me + i, n)
        pl.semaphore_signal(barrier, inc=1, device_id={"ctx": peer}, device_id_type=MESH)
        return c

    def greet_tp(i, c):
        peer = lax.rem(mt + i, t)
        pl.semaphore_signal(barrier, inc=1, device_id={"tp": peer}, device_id_type=MESH)
        return c

    lax.fori_loop(1, n, greet, 0)
    if t > 1:
        lax.fori_loop(1, t, greet_tp, 0)
    pl.semaphore_wait(barrier, n - 1 + t - 1)


def tp_exchange(t, mt, src_of, dst_of, send_sem, recv_sem):
    def copy_to(peer):
        return pltpu.make_async_remote_copy(
            src_of(peer), dst_of(mt), send_sem.at[peer], recv_sem.at[mt],
            device_id={"tp": peer}, device_id_type=MESH)

    def copy_from(src):
        return pltpu.make_async_remote_copy(
            src_of(mt), dst_of(src), send_sem.at[src], recv_sem.at[src],
            device_id={"tp": src}, device_id_type=MESH)

    def start():
        def send(i, c):
            copy_to(lax.rem(mt + i, t)).start()
            return c

        lax.fori_loop(1, t, send, 0)

    def finish():
        def wait(i, c):
            copy_to(lax.rem(mt + i, t)).wait_send()
            copy_from(lax.rem(mt + t - i, t)).wait_recv()
            return c

        lax.fori_loop(1, t, wait, 0)

    return start, finish


def mask_vectors(me, heads, so_ref, seg_ref, rpos_ref, rlab_ref, cpos_ref, clab_ref, cgrid_ref, lgrid_ref):
    seg = seg_ref[...]
    prompt_end = jnp.sum(jnp.sum((seg == 0).astype(jnp.int32), axis=1, keepdims=True), axis=0, keepdims=True)
    chosen_end = jnp.sum(jnp.sum((seg <= 1).astype(jnp.int32), axis=1, keepdims=True), axis=0, keepdims=True)

    def label_of(pos):
        return (pos >= prompt_end).astype(jnp.int32) + (pos >= chosen_end).astype(jnp.int32)

    def position_of(rows):
        block = lax.shift_right_logical(rows, 6)
        start = jnp.zeros(rows.shape, jnp.int32)
        for b in range(so_ref.shape[0]):
            start = jnp.where(block == b, so_ref[b], start)
        return start * SPAN + jnp.bitwise_and(rows, SPAN - 1)

    lanes = lax.broadcasted_iota(jnp.int32, cpos_ref.shape, 1)
    cpos = position_of(lanes)
    cpos_ref[...] = cpos
    clab_ref[...] = label_of(cpos)
    grid = (lax.broadcasted_iota(jnp.int32, cgrid_ref.shape, 0) * cgrid_ref.shape[1]
            + lax.broadcasted_iota(jnp.int32, cgrid_ref.shape, 1))
    gpos = position_of(grid)
    cgrid_ref[...] = gpos
    lgrid_ref[...] = label_of(gpos)
    local = rpos_ref.shape[0] // heads
    within = jnp.bitwise_and(lax.broadcasted_iota(jnp.int32, rpos_ref.shape, 0), local - 1)
    first = so_ref[me * (local // SPAN)]
    second = so_ref[me * (local // SPAN) + 1]
    start = jnp.where(within < SPAN, first, second)
    rpos = start * SPAN + jnp.bitwise_and(within, SPAN - 1)
    rpos_ref[...] = rpos
    rlab_ref[...] = label_of(rpos)


def gather_kernel(n, t, k_ref, v_ref, og_ref, so_ref, seg_ref, out_ref, grad_ref,
                  rpos_ref, rlab_ref, cpos_ref, clab_ref, cgrid_ref, lgrid_ref,
                  send_sem, recv_sem, vsend_sem, vrecv_sem, gsend_sem, grecv_sem):
    me = lax.axis_index("ctx")
    mt = lax.axis_index("tp")
    greet_all(n, me, t, mt)
    rows = og_ref.shape[0]
    cols = grad_ref.shape[1]

    def grad_src(p):
        return og_ref.at[:, pl.ds(pl.multiple_of(p * cols, cols), cols)]

    def grad_dst(p):
        return grad_ref.at[pl.ds(pl.multiple_of(p * rows, rows), rows), :]

    grad_start, grad_finish = tp_exchange(t, mt, grad_src, grad_dst, gsend_sem, grecv_sem)
    grad_start()

    width = k_ref.shape[1]

    def copies(dst, peer, slot):
        return (
            pltpu.make_async_remote_copy(
                k_ref, out_ref.at[dst, :, :width], send_sem.at[slot], recv_sem.at[dst],
                device_id={"ctx": peer}, device_id_type=MESH),
            pltpu.make_async_remote_copy(
                v_ref, out_ref.at[dst, :, width:], vsend_sem.at[slot], vrecv_sem.at[dst],
                device_id={"ctx": peer}, device_id_type=MESH),
        )

    def send(i, c):
        peer = ctx_peer(me, i, n, 1)
        for copy in copies(me, peer, peer):
            copy.start()
        return c

    lax.fori_loop(1, n, send, 0)
    out_ref[me, :, :width] = k_ref[...]
    out_ref[me, :, width:] = v_ref[...]
    mask_vectors(me, grad_ref.shape[1] // HEAD_DIM, so_ref, seg_ref,
                 rpos_ref, rlab_ref, cpos_ref, clab_ref, cgrid_ref, lgrid_ref)
    grad_ref[pl.ds(pl.multiple_of(mt * rows, rows), rows), :] = og_ref[
        :, pl.ds(pl.multiple_of(mt * cols, cols), cols)]

    def wait(i, c):
        peer = ctx_peer(me, i, n, 1)
        for copy in copies(me, peer, peer):
            copy.wait_send()
        src = ctx_peer(me, i, n, -1)
        for copy in copies(src, src, src):
            copy.wait_recv()
        return c

    lax.fori_loop(1, n, wait, 0)
    grad_finish()


def ctx_gather(key_rows, value_rows, out_grad, span_order, segment_ids, n, t):
    rows = key_rows.shape[0]
    width = key_rows.shape[1] + value_rows.shape[1]
    grad_shape = (out_grad.shape[0] * t, out_grad.shape[1] // t)
    stacked = rows * (grad_shape[1] // HEAD_DIM)
    seg = segment_ids.reshape(n, segment_ids.shape[0] // n)
    column = jax.ShapeDtypeStruct((1, n * rows), jnp.int32)
    row = jax.ShapeDtypeStruct((stacked, 1), jnp.int32)
    grid = jax.ShapeDtypeStruct((n, rows), jnp.int32)
    return pl.pallas_call(
        functools.partial(gather_kernel, n, t),
        out_shape=(
            jax.ShapeDtypeStruct((n, rows, width), key_rows.dtype),
            jax.ShapeDtypeStruct(grad_shape, out_grad.dtype),
            row, row, column, column, grid, grid,
        ),
        in_specs=[pl.BlockSpec(memory_space=pltpu.VMEM)] * 3
        + [pl.BlockSpec(memory_space=pltpu.SMEM), pl.BlockSpec(memory_space=pltpu.VMEM)],
        out_specs=(pl.BlockSpec(memory_space=pltpu.VMEM),) * 8,
        scratch_shapes=[pltpu.SemaphoreType.DMA((n,))] * 4 + [pltpu.SemaphoreType.DMA((t,))] * 2,
        compiler_params=pltpu.CompilerParams(collective_id=0, has_side_effects=True),
    )(key_rows, value_rows, out_grad, span_order, seg)


KEY_BLOCK = 1024
FWD_GROUP = 8
NT_DIMS = (((1,), (1,)), ((), ()))
TN_DIMS = (((0,), (0,)), ((), ()))


def stack_heads(ref):
    heads = ref.shape[1] // HEAD_DIM
    return jnp.concatenate([ref[:, h * HEAD_DIM:(h + 1) * HEAD_DIM] for h in range(heads)], axis=0)


def unstack_heads(ref, value):
    rows = ref.shape[0]
    for h in range(ref.shape[1] // HEAD_DIM):
        ref[:, h * HEAD_DIM:(h + 1) * HEAD_DIM] = value[h * rows:(h + 1) * rows]


def key_block(kv_ref, cpos_ref, clab_ref, rpos, rlab, kb):
    size = min(KEY_BLOCK, kv_ref.shape[0])
    start = pl.multiple_of(kb * size, size)
    keys = kv_ref[pl.ds(start, size), :HEAD_DIM]
    values = kv_ref[pl.ds(start, size), HEAD_DIM:]
    cpos = cpos_ref[:, pl.ds(start, size)]
    clab = clab_ref[:, pl.ds(start, size)]
    visible = (cpos <= rpos) & ((clab == 0) | (clab == rlab))
    return start, keys, values, visible


def fwd_kernel(q_ref, kv_ref, rpos_ref, rlab_ref, cpos_ref, clab_ref, o_ref, m_ref, l_ref, acc_sc):
    scale = 1.0 / math.sqrt(HEAD_DIM)
    queries = stack_heads(q_ref)
    rpos = rpos_ref[...]
    rlab = rlab_ref[...]
    m_ref[...] = jnp.full(m_ref.shape, -jnp.inf, jnp.float32)
    l_ref[...] = jnp.zeros(l_ref.shape, jnp.float32)
    acc_sc[...] = jnp.zeros(acc_sc.shape, jnp.float32)

    def body(kb, c):
        _, keys, values, visible = key_block(kv_ref, cpos_ref, clab_ref, rpos, rlab, kb)
        scores = lax.dot_general(queries, keys, NT_DIMS, preferred_element_type=jnp.float32) * scale
        scores = jnp.where(visible, scores, -jnp.inf)
        running = m_ref[...]
        new_max = jnp.maximum(running, jnp.max(scores, axis=-1, keepdims=True))
        shift = jnp.where(new_max == -jnp.inf, 0.0, new_max)
        factor = jnp.exp(running - shift)
        weights = jnp.exp(scores - shift)
        l_ref[...] = l_ref[...] * factor + jnp.sum(weights, axis=-1, keepdims=True)
        acc_sc[...] = acc_sc[...] * factor + jnp.dot(
            weights.astype(jnp.bfloat16), values, preferred_element_type=jnp.float32)
        m_ref[...] = new_max
        return c

    lax.fori_loop(0, kv_ref.shape[0] // min(KEY_BLOCK, kv_ref.shape[0]), body, 0)
    unstack_heads(o_ref, (acc_sc[...] / l_ref[...]).astype(o_ref.dtype))


def vmem_specs(n):
    return [pl.BlockSpec(memory_space=pltpu.VMEM)] * n


def attention_fwd(q, kv, rpos, rlab, cpos, clab):
    stacked = rpos.shape[0]
    return pl.pallas_call(
        fwd_kernel,
        out_shape=(
            jax.ShapeDtypeStruct(q.shape, jnp.bfloat16),
            jax.ShapeDtypeStruct((stacked, 1), jnp.float32),
            jax.ShapeDtypeStruct((stacked, 1), jnp.float32),
        ),
        in_specs=vmem_specs(6),
        out_specs=tuple(vmem_specs(3)),
        scratch_shapes=[pltpu.VMEM((stacked, HEAD_DIM), jnp.float32)],
    )(q, kv, rpos, rlab, cpos, clab)


def column_visible(cpos_ref, clab_ref, block, rpos, rlab):
    cpos = cpos_ref[pl.ds(block, 1), :]
    clab = clab_ref[pl.ds(block, 1), :]
    return (cpos <= rpos) & ((clab == 0) | (clab == rlab))


def fwd_groups(n, queries, kv_ref, cpos_ref, clab_ref, rpos, rlab, m_ref, l_ref, acc_sc, o_ref):
    scale = 1.0 / math.sqrt(HEAD_DIM)
    group = math.gcd(n, FWD_GROUP)
    m_ref[...] = jnp.full(m_ref.shape, -jnp.inf, jnp.float32)
    l_ref[...] = jnp.zeros(l_ref.shape, jnp.float32)
    acc_sc[...] = jnp.zeros(acc_sc.shape, jnp.float32)

    def body(j, c):
        first = j * group
        block = jnp.concatenate([kv_ref[first + b] for b in range(group)], axis=0)
        cpos = jnp.concatenate([cpos_ref[pl.ds(first + b, 1), :] for b in range(group)], axis=1)
        clab = jnp.concatenate([clab_ref[pl.ds(first + b, 1), :] for b in range(group)], axis=1)
        visible = (cpos <= rpos) & ((clab == 0) | (clab == rlab))
        keys = block[:, :HEAD_DIM]
        values = block[:, HEAD_DIM:]
        scores = lax.dot_general(queries, keys, NT_DIMS, preferred_element_type=jnp.float32) * scale
        scores = jnp.where(visible, scores, -jnp.inf)
        running = m_ref[...]
        new_max = jnp.maximum(running, jnp.max(scores, axis=-1, keepdims=True))
        shift = jnp.where(new_max == -jnp.inf, 0.0, new_max)
        factor = jnp.exp(running - shift)
        weights = jnp.exp(scores - shift)
        l_ref[...] = l_ref[...] * factor + jnp.sum(weights, axis=-1, keepdims=True)
        acc_sc[...] = acc_sc[...] * factor + jnp.dot(
            weights.astype(jnp.bfloat16), values, preferred_element_type=jnp.float32)
        m_ref[...] = new_max
        return c

    lax.fori_loop(0, n // group, body, 0)
    unstack_heads(o_ref, (acc_sc[...] / l_ref[...]).astype(o_ref.dtype))


def bwd_scatter_kernel(n, t, q_ref, g_ref, kv_ref, rpos_ref, rlab_ref, cpos_ref, clab_ref,
                       dq_ref, red_ref, spread_ref, o_ref, m_ref, l_ref, terms_sc, held, dq_sc,
                       send_sem, recv_sem, osend_sem, orecv_sem):
    me = lax.axis_index("ctx")
    mt = lax.axis_index("tp")
    greet_all(n, me, t, mt)
    fwd_groups(n, stack_heads(q_ref), kv_ref, cpos_ref, clab_ref, rpos_ref[...], rlab_ref[...],
               m_ref, l_ref, dq_sc, o_ref)
    rows = spread_ref.shape[0]
    cols = o_ref.shape[1]

    def out_src(p):
        return o_ref.at[pl.ds(pl.multiple_of(p * rows, rows), rows), :]

    def out_dst(p):
        return spread_ref.at[:, pl.ds(pl.multiple_of(p * cols, cols), cols)]

    out_start, out_finish = tp_exchange(t, mt, out_src, out_dst, osend_sem, orecv_sem)
    out_start()
    spread_ref[:, pl.ds(pl.multiple_of(mt * cols, cols), cols)] = o_ref[
        pl.ds(pl.multiple_of(mt * rows, rows), rows), :]
    scale = 1.0 / math.sqrt(HEAD_DIM)
    queries = stack_heads(q_ref)
    grads = stack_heads(g_ref)
    outs = stack_heads(o_ref)
    delta = jnp.sum(grads.astype(jnp.float32) * outs.astype(jnp.float32), axis=-1, keepdims=True)
    rpos = rpos_ref[...]
    rlab = rlab_ref[...]
    row_max = m_ref[...]
    inv_total = 1.0 / l_ref[...]
    dq_sc[...] = jnp.zeros(dq_sc.shape, jnp.float32)

    def copy_to(peer):
        return pltpu.make_async_remote_copy(
            terms_sc.at[peer], held.at[me], send_sem.at[peer], recv_sem.at[me],
            device_id={"ctx": peer}, device_id_type=MESH)

    def copy_from(src):
        return pltpu.make_async_remote_copy(
            terms_sc.at[src], held.at[src], send_sem.at[src], recv_sem.at[src],
            device_id={"ctx": src}, device_id_type=MESH)

    def block_terms(p):
        block = kv_ref[p]
        keys = block[:, :HEAD_DIM]
        values = block[:, HEAD_DIM:]
        visible = column_visible(cpos_ref, clab_ref, p, rpos, rlab)
        scores = lax.dot_general(queries, keys, NT_DIMS, preferred_element_type=jnp.float32) * scale
        probs = jnp.where(visible, jnp.exp(scores - row_max), 0.0) * inv_total
        dprob = lax.dot_general(grads, values, NT_DIMS, preferred_element_type=jnp.float32)
        dscore_b = (probs * (dprob - delta)).astype(jnp.bfloat16)
        probs_b = probs.astype(jnp.bfloat16)
        dq_sc[...] += jnp.dot(dscore_b, keys, preferred_element_type=jnp.float32)
        key_term = lax.dot_general(dscore_b, queries, TN_DIMS, preferred_element_type=jnp.float32) * scale
        value_term = lax.dot_general(probs_b, grads, TN_DIMS, preferred_element_type=jnp.float32)
        return jnp.concatenate([key_term, value_term], axis=1)

    red_ref[...] = block_terms(me)

    def step(i, c):
        peer = ctx_peer(me, i, n, 1)
        terms_sc[peer] = block_terms(peer).astype(terms_sc.dtype)

        @pl.when(i >= 2)
        def _():
            copy_to(ctx_peer(me, i - 1, n, 1)).start()

        return c

    lax.fori_loop(1, n, step, 0)
    copy_to(ctx_peer(me, n - 1, n, 1)).start()
    dq_ref[...] = dq_sc[...] * scale

    def arrive(i, c):
        src = ctx_peer(me, i, n, -1)
        copy_from(src).wait_recv()
        red_ref[...] += held[src].astype(jnp.float32)
        return c

    lax.fori_loop(1, n, arrive, 0)

    def drain(i, c):
        copy_to(ctx_peer(me, i, n, 1)).wait_send()
        return c

    lax.fori_loop(1, n, drain, 0)
    out_finish()


def bwd_scatter(q, g, kv, rpos, rlab, cpos, clab, n, t):
    _, rows, width = kv.shape
    stacked = rpos.shape[0]
    return pl.pallas_call(
        functools.partial(bwd_scatter_kernel, n, t),
        out_shape=(
            jax.ShapeDtypeStruct((stacked, HEAD_DIM), jnp.float32),
            jax.ShapeDtypeStruct((rows, width), jnp.float32),
            jax.ShapeDtypeStruct((q.shape[0] // t, q.shape[1] * t), jnp.bfloat16),
        ),
        in_specs=vmem_specs(7),
        out_specs=tuple(vmem_specs(3)),
        scratch_shapes=[
            pltpu.VMEM(q.shape, jnp.bfloat16),
            pltpu.VMEM((stacked, 1), jnp.float32),
            pltpu.VMEM((stacked, 1), jnp.float32),
            pltpu.VMEM(kv.shape, jnp.bfloat16),
            pltpu.VMEM(kv.shape, jnp.bfloat16),
            pltpu.VMEM((stacked, HEAD_DIM), jnp.float32),
            pltpu.SemaphoreType.DMA((n,)),
            pltpu.SemaphoreType.DMA((n,)),
            pltpu.SemaphoreType.DMA((t,)),
            pltpu.SemaphoreType.DMA((t,)),
        ],
        compiler_params=pltpu.CompilerParams(collective_id=1, has_side_effects=True),
    )(q, g, kv, rpos, rlab, cpos, clab)


def on_device(query_rows, key_rows, value_rows, out_grad, segment_ids, span_order):
    ctx_size = lax.axis_size("ctx")
    ctx_index = lax.axis_index("ctx")
    local_rows = query_rows.shape[0]
    heads_here = query_rows.shape[1] // HEAD_DIM
    total_rows = local_rows * ctx_size
    tp_size = lax.axis_size("tp")
    kv_all, grad_rows, rpos, rlab, cpos_row, clab_row, cpos, clab = ctx_gather(
        key_rows, value_rows, out_grad, span_order, segment_ids, ctx_size, tp_size)
    stacked_grad, reduced, attn_spread = bwd_scatter(
        query_rows, grad_rows, kv_all, rpos, rlab, cpos, clab, ctx_size, tp_size)
    key_grad = reduced[:, :HEAD_DIM].astype(jnp.bfloat16)
    value_grad = reduced[:, HEAD_DIM:].astype(jnp.bfloat16)
    query_grad = jnp.transpose(
        stacked_grad.astype(jnp.bfloat16).reshape(heads_here, local_rows, HEAD_DIM), (1, 0, 2)
    ).reshape(local_rows, heads_here * HEAD_DIM)
    return (attn_spread, query_grad, key_grad, value_grad)


def solution(mesh):
    placed = (P("ctx", "tp"), P("ctx", "tp"), P("ctx", "tp"), P(("ctx", "tp"), None), P(), P())
    return jax.shard_map(
        on_device,
        mesh=mesh,
        in_specs=placed,
        out_specs=(P(("ctx", "tp"), None), P("ctx", "tp"), P("ctx", "tp"), P("ctx", "tp")),
        check_vma=False,
    )
```

```python
import functools
import math

import jax
import jax.numpy as jnp
from jax import lax
from jax.experimental import pallas as pl
from jax.experimental.pallas import tpu as pltpu
from jax.sharding import PartitionSpec as P

HEAD_DIM = 128
SPAN = 64
MESH = pl.DeviceIdType.MESH


CTX_SHAPE = (4, 4, 2)


def ctx_peer(me, i, n, sign):
    if n != math.prod(CTX_SHAPE):
        return lax.rem(me + sign * i + n, n)
    sx, sy, sz = CTX_SHAPE
    dz = lax.rem(i, sz)
    dx = lax.rem(i // sz, sx)
    dy = i // (sz * sx)
    x = me // (sy * sz)
    y = lax.rem(me // sz, sy)
    z = lax.rem(me, sz)
    x = lax.rem(x + sign * dx + sx, sx)
    y = lax.rem(y + sign * dy + sy, sy)
    z = lax.rem(z + sign * dz + sz, sz)
    return (x * sy + y) * sz + z


def greet_all(n, me, t=1, mt=None):
    barrier = pltpu.get_barrier_semaphore()

    def greet(i, c):
        peer = lax.rem(me + i, n)
        pl.semaphore_signal(barrier, inc=1, device_id={"ctx": peer}, device_id_type=MESH)
        return c

    def greet_tp(i, c):
        peer = lax.rem(mt + i, t)
        pl.semaphore_signal(barrier, inc=1, device_id={"tp": peer}, device_id_type=MESH)
        return c

    lax.fori_loop(1, n, greet, 0)
    if t > 1:
        lax.fori_loop(1, t, greet_tp, 0)
    pl.semaphore_wait(barrier, n - 1 + t - 1)


def tp_exchange(t, mt, src_of, dst_of, send_sem, recv_sem):
    def copy_to(peer):
        return pltpu.make_async_remote_copy(
            src_of(peer), dst_of(mt), send_sem.at[peer], recv_sem.at[mt],
            device_id={"tp": peer}, device_id_type=MESH)

    def copy_from(src):
        return pltpu.make_async_remote_copy(
            src_of(mt), dst_of(src), send_sem.at[src], recv_sem.at[src],
            device_id={"tp": src}, device_id_type=MESH)

    def start():
        def send(i, c):
            copy_to(lax.rem(mt + i, t)).start()
            return c

        lax.fori_loop(1, t, send, 0)

    def finish():
        def wait(i, c):
            copy_to(lax.rem(mt + i, t)).wait_send()
            copy_from(lax.rem(mt + t - i, t)).wait_recv()
            return c

        lax.fori_loop(1, t, wait, 0)

    return start, finish


def mask_vectors(me, heads, so_ref, seg_ref, rpos_ref, rlab_ref, cpos_ref, clab_ref, cgrid_ref, lgrid_ref):
    seg = seg_ref[...]
    prompt_end = jnp.sum(jnp.sum((seg == 0).astype(jnp.int32), axis=1, keepdims=True), axis=0, keepdims=True)
    chosen_end = jnp.sum(jnp.sum((seg <= 1).astype(jnp.int32), axis=1, keepdims=True), axis=0, keepdims=True)

    def label_of(pos):
        return (pos >= prompt_end).astype(jnp.int32) + (pos >= chosen_end).astype(jnp.int32)

    def position_of(rows):
        block = lax.shift_right_logical(rows, 6)
        start = jnp.zeros(rows.shape, jnp.int32)
        for b in range(so_ref.shape[0]):
            start = jnp.where(block == b, so_ref[b], start)
        return start * SPAN + jnp.bitwise_and(rows, SPAN - 1)

    lanes = lax.broadcasted_iota(jnp.int32, cpos_ref.shape, 1)
    cpos = position_of(lanes)
    cpos_ref[...] = cpos
    clab_ref[...] = label_of(cpos)
    grid = (lax.broadcasted_iota(jnp.int32, cgrid_ref.shape, 0) * cgrid_ref.shape[1]
            + lax.broadcasted_iota(jnp.int32, cgrid_ref.shape, 1))
    gpos = position_of(grid)
    cgrid_ref[...] = gpos
    lgrid_ref[...] = label_of(gpos)
    local = rpos_ref.shape[0] // heads
    within = jnp.bitwise_and(lax.broadcasted_iota(jnp.int32, rpos_ref.shape, 0), local - 1)
    first = so_ref[me * (local // SPAN)]
    second = so_ref[me * (local // SPAN) + 1]
    start = jnp.where(within < SPAN, first, second)
    rpos = start * SPAN + jnp.bitwise_and(within, SPAN - 1)
    rpos_ref[...] = rpos
    rlab_ref[...] = label_of(rpos)


def gather_kernel(n, t, k_ref, v_ref, og_ref, so_ref, seg_ref, out_ref, grad_ref,
                  rpos_ref, rlab_ref, cpos_ref, clab_ref, cgrid_ref, lgrid_ref,
                  send_sem, recv_sem, vsend_sem, vrecv_sem, gsend_sem, grecv_sem):
    me = lax.axis_index("ctx")
    mt = lax.axis_index("tp")
    greet_all(n, me, t, mt)
    rows = og_ref.shape[0]
    cols = grad_ref.shape[1]

    def grad_src(p):
        return og_ref.at[:, pl.ds(pl.multiple_of(p * cols, cols), cols)]

    def grad_dst(p):
        return grad_ref.at[pl.ds(pl.multiple_of(p * rows, rows), rows), :]

    grad_start, grad_finish = tp_exchange(t, mt, grad_src, grad_dst, gsend_sem, grecv_sem)
    grad_start()

    width = k_ref.shape[1]

    def copies(dst, peer, slot):
        return (
            pltpu.make_async_remote_copy(
                k_ref, out_ref.at[dst, :, :width], send_sem.at[slot], recv_sem.at[dst],
                device_id={"ctx": peer}, device_id_type=MESH),
            pltpu.make_async_remote_copy(
                v_ref, out_ref.at[dst, :, width:], vsend_sem.at[slot], vrecv_sem.at[dst],
                device_id={"ctx": peer}, device_id_type=MESH),
        )

    def send(i, c):
        peer = ctx_peer(me, i, n, 1)
        for copy in copies(me, peer, peer):
            copy.start()
        return c

    lax.fori_loop(1, n, send, 0)
    out_ref[me, :, :width] = k_ref[...]
    out_ref[me, :, width:] = v_ref[...]
    mask_vectors(me, grad_ref.shape[1] // HEAD_DIM, so_ref, seg_ref,
                 rpos_ref, rlab_ref, cpos_ref, clab_ref, cgrid_ref, lgrid_ref)
    grad_ref[pl.ds(pl.multiple_of(mt * rows, rows), rows), :] = og_ref[
        :, pl.ds(pl.multiple_of(mt * cols, cols), cols)]

    def wait(i, c):
        peer = ctx_peer(me, i, n, 1)
        for copy in copies(me, peer, peer):
            copy.wait_send()
        src = ctx_peer(me, i, n, -1)
        for copy in copies(src, src, src):
            copy.wait_recv()
        return c

    lax.fori_loop(1, n, wait, 0)
    grad_finish()


def ctx_gather(key_rows, value_rows, out_grad, span_order, segment_ids, n, t):
    rows = key_rows.shape[0]
    width = key_rows.shape[1] + value_rows.shape[1]
    grad_shape = (out_grad.shape[0] * t, out_grad.shape[1] // t)
    stacked = rows * (grad_shape[1] // HEAD_DIM)
    seg = segment_ids.reshape(n, segment_ids.shape[0] // n)
    column = jax.ShapeDtypeStruct((1, n * rows), jnp.int32)
    row = jax.ShapeDtypeStruct((stacked, 1), jnp.int32)
    grid = jax.ShapeDtypeStruct((n, rows), jnp.int32)
    return pl.pallas_call(
        functools.partial(gather_kernel, n, t),
        out_shape=(
            jax.ShapeDtypeStruct((n, rows, width), key_rows.dtype),
            jax.ShapeDtypeStruct(grad_shape, out_grad.dtype),
            row, row, column, column, grid, grid,
        ),
        in_specs=[pl.BlockSpec(memory_space=pltpu.VMEM)] * 3
        + [pl.BlockSpec(memory_space=pltpu.SMEM), pl.BlockSpec(memory_space=pltpu.VMEM)],
        out_specs=(pl.BlockSpec(memory_space=pltpu.VMEM),) * 8,
        scratch_shapes=[pltpu.SemaphoreType.DMA((n,))] * 4 + [pltpu.SemaphoreType.DMA((t,))] * 2,
        compiler_params=pltpu.CompilerParams(collective_id=0, has_side_effects=True),
    )(key_rows, value_rows, out_grad, span_order, seg)


KEY_BLOCK = 1024
FWD_GROUP = 16
NT_DIMS = (((1,), (1,)), ((), ()))
TN_DIMS = (((0,), (0,)), ((), ()))


def stack_heads(ref):
    heads = ref.shape[1] // HEAD_DIM
    return jnp.concatenate([ref[:, h * HEAD_DIM:(h + 1) * HEAD_DIM] for h in range(heads)], axis=0)


def unstack_heads(ref, value):
    rows = ref.shape[0]
    for h in range(ref.shape[1] // HEAD_DIM):
        ref[:, h * HEAD_DIM:(h + 1) * HEAD_DIM] = value[h * rows:(h + 1) * rows]


def key_block(kv_ref, cpos_ref, clab_ref, rpos, rlab, kb):
    size = min(KEY_BLOCK, kv_ref.shape[0])
    start = pl.multiple_of(kb * size, size)
    keys = kv_ref[pl.ds(start, size), :HEAD_DIM]
    values = kv_ref[pl.ds(start, size), HEAD_DIM:]
    cpos = cpos_ref[:, pl.ds(start, size)]
    clab = clab_ref[:, pl.ds(start, size)]
    visible = (cpos <= rpos) & ((clab == 0) | (clab == rlab))
    return start, keys, values, visible


def fwd_kernel(q_ref, kv_ref, rpos_ref, rlab_ref, cpos_ref, clab_ref, o_ref, m_ref, l_ref, acc_sc):
    scale = 1.0 / math.sqrt(HEAD_DIM)
    queries = stack_heads(q_ref)
    rpos = rpos_ref[...]
    rlab = rlab_ref[...]
    m_ref[...] = jnp.full(m_ref.shape, -jnp.inf, jnp.float32)
    l_ref[...] = jnp.zeros(l_ref.shape, jnp.float32)
    acc_sc[...] = jnp.zeros(acc_sc.shape, jnp.float32)

    def body(kb, c):
        _, keys, values, visible = key_block(kv_ref, cpos_ref, clab_ref, rpos, rlab, kb)
        scores = lax.dot_general(queries, keys, NT_DIMS, preferred_element_type=jnp.float32) * scale
        scores = jnp.where(visible, scores, -jnp.inf)
        running = m_ref[...]
        new_max = jnp.maximum(running, jnp.max(scores, axis=-1, keepdims=True))
        shift = jnp.where(new_max == -jnp.inf, 0.0, new_max)
        factor = jnp.exp(running - shift)
        weights = jnp.exp(scores - shift)
        l_ref[...] = l_ref[...] * factor + jnp.sum(weights, axis=-1, keepdims=True)
        acc_sc[...] = acc_sc[...] * factor + jnp.dot(
            weights.astype(jnp.bfloat16), values, preferred_element_type=jnp.float32)
        m_ref[...] = new_max
        return c

    lax.fori_loop(0, kv_ref.shape[0] // min(KEY_BLOCK, kv_ref.shape[0]), body, 0)
    unstack_heads(o_ref, (acc_sc[...] / l_ref[...]).astype(o_ref.dtype))


def vmem_specs(n):
    return [pl.BlockSpec(memory_space=pltpu.VMEM)] * n


def attention_fwd(q, kv, rpos, rlab, cpos, clab):
    stacked = rpos.shape[0]
    return pl.pallas_call(
        fwd_kernel,
        out_shape=(
            jax.ShapeDtypeStruct(q.shape, jnp.bfloat16),
            jax.ShapeDtypeStruct((stacked, 1), jnp.float32),
            jax.ShapeDtypeStruct((stacked, 1), jnp.float32),
        ),
        in_specs=vmem_specs(6),
        out_specs=tuple(vmem_specs(3)),
        scratch_shapes=[pltpu.VMEM((stacked, HEAD_DIM), jnp.float32)],
    )(q, kv, rpos, rlab, cpos, clab)


def column_visible(cpos_ref, clab_ref, block, rpos, rlab):
    cpos = cpos_ref[pl.ds(block, 1), :]
    clab = clab_ref[pl.ds(block, 1), :]
    return (cpos <= rpos) & ((clab == 0) | (clab == rlab))


def fwd_groups(n, queries, kv_ref, cpos_ref, clab_ref, rpos, rlab, m_ref, l_ref, acc_sc, o_ref):
    scale = 1.0 / math.sqrt(HEAD_DIM)
    group = math.gcd(n, FWD_GROUP)
    m_ref[...] = jnp.full(m_ref.shape, -jnp.inf, jnp.float32)
    l_ref[...] = jnp.zeros(l_ref.shape, jnp.float32)
    acc_sc[...] = jnp.zeros(acc_sc.shape, jnp.float32)

    def body(j, c):
        first = j * group
        block = jnp.concatenate([kv_ref[first + b] for b in range(group)], axis=0)
        cpos = jnp.concatenate([cpos_ref[pl.ds(first + b, 1), :] for b in range(group)], axis=1)
        clab = jnp.concatenate([clab_ref[pl.ds(first + b, 1), :] for b in range(group)], axis=1)
        visible = (cpos <= rpos) & ((clab == 0) | (clab == rlab))
        keys = block[:, :HEAD_DIM]
        values = block[:, HEAD_DIM:]
        scores = lax.dot_general(queries, keys, NT_DIMS, preferred_element_type=jnp.float32) * scale
        scores = jnp.where(visible, scores, -jnp.inf)
        running = m_ref[...]
        new_max = jnp.maximum(running, jnp.max(scores, axis=-1, keepdims=True))
        shift = jnp.where(new_max == -jnp.inf, 0.0, new_max)
        factor = jnp.exp(running - shift)
        weights = jnp.exp(scores - shift)
        l_ref[...] = l_ref[...] * factor + jnp.sum(weights, axis=-1, keepdims=True)
        acc_sc[...] = acc_sc[...] * factor + jnp.dot(
            weights.astype(jnp.bfloat16), values, preferred_element_type=jnp.float32)
        m_ref[...] = new_max
        return c

    lax.fori_loop(0, n // group, body, 0)
    unstack_heads(o_ref, (acc_sc[...] / l_ref[...]).astype(o_ref.dtype))


def bwd_scatter_kernel(n, t, q_ref, g_ref, kv_ref, rpos_ref, rlab_ref, cpos_ref, clab_ref,
                       dq_ref, red_ref, spread_ref, o_ref, m_ref, l_ref, terms_sc, held, dq_sc,
                       send_sem, recv_sem, osend_sem, orecv_sem):
    me = lax.axis_index("ctx")
    mt = lax.axis_index("tp")
    greet_all(n, me, t, mt)
    fwd_groups(n, stack_heads(q_ref), kv_ref, cpos_ref, clab_ref, rpos_ref[...], rlab_ref[...],
               m_ref, l_ref, dq_sc, o_ref)
    rows = spread_ref.shape[0]
    cols = o_ref.shape[1]

    def out_src(p):
        return o_ref.at[pl.ds(pl.multiple_of(p * rows, rows), rows), :]

    def out_dst(p):
        return spread_ref.at[:, pl.ds(pl.multiple_of(p * cols, cols), cols)]

    out_start, out_finish = tp_exchange(t, mt, out_src, out_dst, osend_sem, orecv_sem)
    out_start()
    spread_ref[:, pl.ds(pl.multiple_of(mt * cols, cols), cols)] = o_ref[
        pl.ds(pl.multiple_of(mt * rows, rows), rows), :]
    scale = 1.0 / math.sqrt(HEAD_DIM)
    queries = stack_heads(q_ref)
    grads = stack_heads(g_ref)
    outs = stack_heads(o_ref)
    delta = jnp.sum(grads.astype(jnp.float32) * outs.astype(jnp.float32), axis=-1, keepdims=True)
    rpos = rpos_ref[...]
    rlab = rlab_ref[...]
    row_max = m_ref[...]
    inv_total = 1.0 / l_ref[...]
    dq_sc[...] = jnp.zeros(dq_sc.shape, jnp.float32)

    def copy_to(peer):
        return pltpu.make_async_remote_copy(
            terms_sc.at[peer], held.at[me], send_sem.at[peer], recv_sem.at[me],
            device_id={"ctx": peer}, device_id_type=MESH)

    def copy_from(src):
        return pltpu.make_async_remote_copy(
            terms_sc.at[src], held.at[src], send_sem.at[src], recv_sem.at[src],
            device_id={"ctx": src}, device_id_type=MESH)

    def block_terms(p):
        block = kv_ref[p]
        keys = block[:, :HEAD_DIM]
        values = block[:, HEAD_DIM:]
        visible = column_visible(cpos_ref, clab_ref, p, rpos, rlab)
        scores = lax.dot_general(queries, keys, NT_DIMS, preferred_element_type=jnp.float32) * scale
        probs = jnp.where(visible, jnp.exp(scores - row_max), 0.0) * inv_total
        dprob = lax.dot_general(grads, values, NT_DIMS, preferred_element_type=jnp.float32)
        dscore_b = (probs * (dprob - delta)).astype(jnp.bfloat16)
        probs_b = probs.astype(jnp.bfloat16)
        dq_sc[...] += jnp.dot(dscore_b, keys, preferred_element_type=jnp.float32)
        key_term = lax.dot_general(dscore_b, queries, TN_DIMS, preferred_element_type=jnp.float32) * scale
        value_term = lax.dot_general(probs_b, grads, TN_DIMS, preferred_element_type=jnp.float32)
        return jnp.concatenate([key_term, value_term], axis=1)

    red_ref[...] = block_terms(me)

    def step(i, c):
        peer = ctx_peer(me, i, n, 1)
        terms_sc[peer] = block_terms(peer).astype(terms_sc.dtype)

        @pl.when(i >= 2)
        def _():
            copy_to(ctx_peer(me, i - 1, n, 1)).start()

        return c

    lax.fori_loop(1, n, step, 0)
    copy_to(ctx_peer(me, n - 1, n, 1)).start()
    unstack_heads(dq_ref, (dq_sc[...] * scale).astype(dq_ref.dtype))

    def arrive(i, c):
        src = ctx_peer(me, i, n, -1)
        copy_from(src).wait_recv()
        red_ref[...] += held[src].astype(jnp.float32)
        return c

    lax.fori_loop(1, n, arrive, 0)

    def drain(i, c):
        copy_to(ctx_peer(me, i, n, 1)).wait_send()
        return c

    lax.fori_loop(1, n, drain, 0)
    out_finish()


def bwd_scatter(q, g, kv, rpos, rlab, cpos, clab, n, t):
    _, rows, width = kv.shape
    stacked = rpos.shape[0]
    return pl.pallas_call(
        functools.partial(bwd_scatter_kernel, n, t),
        out_shape=(
            jax.ShapeDtypeStruct(q.shape, jnp.bfloat16),
            jax.ShapeDtypeStruct((rows, width), jnp.float32),
            jax.ShapeDtypeStruct((q.shape[0] // t, q.shape[1] * t), jnp.bfloat16),
        ),
        in_specs=vmem_specs(7),
        out_specs=tuple(vmem_specs(3)),
        scratch_shapes=[
            pltpu.VMEM(q.shape, jnp.bfloat16),
            pltpu.VMEM((stacked, 1), jnp.float32),
            pltpu.VMEM((stacked, 1), jnp.float32),
            pltpu.VMEM(kv.shape, jnp.bfloat16),
            pltpu.VMEM(kv.shape, jnp.bfloat16),
            pltpu.VMEM((stacked, HEAD_DIM), jnp.float32),
            pltpu.SemaphoreType.DMA((n,)),
            pltpu.SemaphoreType.DMA((n,)),
            pltpu.SemaphoreType.DMA((t,)),
            pltpu.SemaphoreType.DMA((t,)),
        ],
        compiler_params=pltpu.CompilerParams(collective_id=1, has_side_effects=True),
    )(q, g, kv, rpos, rlab, cpos, clab)


def on_device(query_rows, key_rows, value_rows, out_grad, segment_ids, span_order):
    ctx_size = lax.axis_size("ctx")
    ctx_index = lax.axis_index("ctx")
    local_rows = query_rows.shape[0]
    heads_here = query_rows.shape[1] // HEAD_DIM
    total_rows = local_rows * ctx_size
    tp_size = lax.axis_size("tp")
    kv_all, grad_rows, rpos, rlab, cpos_row, clab_row, cpos, clab = ctx_gather(
        key_rows, value_rows, out_grad, span_order, segment_ids, ctx_size, tp_size)
    query_grad, reduced, attn_spread = bwd_scatter(
        query_rows, grad_rows, kv_all, rpos, rlab, cpos, clab, ctx_size, tp_size)
    key_grad = reduced[:, :HEAD_DIM].astype(jnp.bfloat16)
    value_grad = reduced[:, HEAD_DIM:].astype(jnp.bfloat16)
    return (attn_spread, query_grad, key_grad, value_grad)


def solution(mesh):
    placed = (P("ctx", "tp"), P("ctx", "tp"), P("ctx", "tp"), P(("ctx", "tp"), None), P(), P())
    return jax.shard_map(
        on_device,
        mesh=mesh,
        in_specs=placed,
        out_specs=(P(("ctx", "tp"), None), P("ctx", "tp"), P("ctx", "tp"), P("ctx", "tp")),
        check_vma=False,
    )
```
